32 devices in a mesh: sample: 4 (over y, x), space: 8 (over z, core).
Axes of the slice: x: 2, y: 2, z: 4, core: 2. Of those that a mesh axis runs over, the one named last changes fastest.
Arguments:
- volume: bfloat16 [4, 16, 16, 4096], P('sample', 'space'), may hold values from -6 to 6
- weight_three: bfloat16 [3, 3, 3, 32, 64], replicated, may hold values from -0.21875 to 0.21875
- bias_three: float32 [64], replicated, may hold values from -3 to 3
- weight_four: bfloat16 [3, 3, 3, 64, 128], replicated, may hold values from -0.15625 to 0.15625
- bias_four: float32 [128], replicated, may hold values from -3 to 3
- cotangent: bfloat16 [4, 16, 4096], P('sample', 'space'), may hold values from -48 to 48
Outputs:
- grad_volume: bfloat16 [4, 16, 16, 4096], P('sample', 'space')
- grad_weight_three: float32 [3, 3, 3, 32, 64], replicated
- grad_bias_three: float32 [64], replicated
- grad_weight_four: float32 [3, 3, 3, 64, 128], replicated
- grad_bias_four: float32 [128], replicated
The draws below stay inside these ranges and needn't reach their ends.
All inputs are finite; a program needn't handle non-finite values.
Results may differ from the reference program's by a relative error of at most 0.0065.
Values may be sent and summed in bfloat16 or wider, within the bound.
A program may use at most 64 MiB of HBM per device.

```python
import jax
import jax.numpy as jnp
from jax import lax

C0 = 32
C1 = 64
C2 = 128
HGT = 16
WID = 128
SAMPLES = 4
NZ = 16


def shard_levels(own_key, dims, split, low, largest):
    loudness = 1.0
    for dim, blocks in split:
        heights = jax.random.uniform(jax.random.fold_in(jax.random.fold_in(own_key, 6), dim), (blocks,), jnp.float32, low / len(split), largest / len(split))
        loudness = loudness * jnp.repeat(jnp.exp(heights), dims[dim] // blocks).reshape((-1,) + (1,) * (len(dims) - 1 - dim))
    return loudness


def centred(rng, dims, scale, bound, split=(), kind=jnp.bfloat16):
    loudness = shard_levels(rng, dims, split, -0.22, 0.18) if split else 1.0
    entries = jax.random.normal(rng, dims, jnp.float32) * scale * loudness
    return jnp.minimum(jnp.maximum(entries, -bound), bound).astype(kind)


def setup_inputs(seed: int = 0) -> dict:
    key_of = jax.random.split(jax.random.key(seed), 7)
    return {
        "volume": centred(key_of[0], (SAMPLES, NZ, HGT, WID * C0), 1.0, 6.0, ((0, 4), (1, 8))),
        "weight_three": centred(key_of[1], (3, 3, 3, C0, C1), (27 * C0) ** -0.5, 0.21875),
        "bias_three": centred(key_of[2], (C1,), 0.5, 3.0, (), jnp.float32),
        "weight_four": centred(key_of[3], (3, 3, 3, C1, C2), (27 * C1) ** -0.5, 0.15625),
        "bias_four": centred(key_of[4], (C2,), 0.5, 3.0, (), jnp.float32),
        "cotangent": centred(key_of[5], (SAMPLES, (NZ // 4) * (HGT // 4), (WID // 4) * C2), 8.0, 48.0, ((0, 4), (1, 8))),
    }


def conv_apply(source, kernel, pads):
    return lax.conv_general_dilated(source[None], kernel, (1, 1, 1), pads, dimension_numbers=('NDHWC', 'DHWIO', 'NDHWC'), preferred_element_type=jnp.float32)[0]

def weight_grad(padded, upstream):
    result = lax.conv_general_dilated(padded[None], upstream[None], (1, 1, 1), 'VALID', dimension_numbers=('CDHWN', 'IDHWO', 'NDHWC'), preferred_element_type=jnp.float32)
    return jnp.transpose(result, (1, 2, 3, 0, 4))

def flipped(kernel):
    return jnp.transpose(jnp.flip(kernel, (0, 1, 2)), (0, 1, 2, 4, 3))

def swish_slope(value):
    sig = jax.nn.sigmoid(value)
    return sig * (1.0 + value * (1.0 - sig))

def average_pool(field):
    depth, height, width, chans = field.shape
    blocks = field.reshape(depth // 2, 2, height // 2, 2, width // 2, 2, chans)
    return lax.optimization_barrier(jnp.mean(blocks, axis=(1, 3, 5)))

def spread_up(field, axes_list):
    for axis_pos in axes_list:
        field = jnp.repeat(field, 2, axis=axis_pos)
    return field * 0.125

def reference(volume, weight_three, bias_three, weight_four, bias_four, cotangent):
    same = [(1, 1), (1, 1), (1, 1)]
    cube_pad = ((1, 1), (1, 1), (1, 1), (0, 0))
    wsum_three = jnp.zeros(weight_three.shape, jnp.float32)
    bsum_three = jnp.zeros(bias_three.shape, jnp.float32)
    wsum_four = jnp.zeros(weight_four.shape, jnp.float32)
    bsum_four = jnp.zeros(bias_four.shape, jnp.float32)
    grad_rows = []
    for sample_index in range(SAMPLES):
        field = volume[sample_index].reshape(NZ, HGT, WID, C0)
        pre_three = conv_apply(field, weight_three, same) + bias_three
        pooled = average_pool(jax.nn.silu(pre_three)).astype(jnp.bfloat16)
        pre_four = conv_apply(pooled, weight_four, same) + bias_four
        upper = cotangent[sample_index].reshape(NZ // 4, HGT // 4, WID // 4, C2).astype(jnp.float32)
        grad_four = (spread_up(upper, (0, 1, 2)) * swish_slope(pre_four)).astype(jnp.bfloat16)
        wsum_four = wsum_four + weight_grad(jnp.pad(pooled, cube_pad), grad_four)
        bsum_four = bsum_four + lax.optimization_barrier(jnp.sum(grad_four.astype(jnp.float32), axis=(0, 1, 2)))
        back_pooled = conv_apply(grad_four, flipped(weight_four), same)
        grad_three = (spread_up(back_pooled, (0, 1, 2)) * swish_slope(pre_three)).astype(jnp.bfloat16)
        wsum_three = wsum_three + weight_grad(jnp.pad(field, cube_pad), grad_three)
        bsum_three = bsum_three + lax.optimization_barrier(jnp.sum(grad_three.astype(jnp.float32), axis=(0, 1, 2)))
        grad_field = conv_apply(grad_three, flipped(weight_three), same).astype(jnp.bfloat16)
        grad_rows.append(grad_field.reshape(NZ, HGT, WID * C0))
    return (jnp.stack(grad_rows), wsum_three, bsum_three, wsum_four, bsum_four)
```

```python
import functools

import jax
import jax.numpy as jnp
from jax import lax
from jax.experimental import pallas as pl
from jax.experimental.pallas import tpu as pltpu
from jax.sharding import PartitionSpec as P

F32 = jnp.float32
BF16 = jnp.bfloat16
MESH = pl.DeviceIdType.MESH
LANES = 128


def slot_of(cell, cells, chans, main, low_side):
    if cell < 0:
        return main + low_side
    if cell == cells:
        return main
    return cell * chans


def place_forward(wide, fwd, low_in):
    cin, cout = wide.shape[1], wide.shape[2]
    fwd[...] = jnp.zeros(fwd.shape, fwd.dtype)
    for tap in range(9):
        for dx in range(3):
            for c in range(LANES // cin):
                row = tap * 2 * LANES + slot_of(c + dx - 1, LANES // cin, cin, LANES, low_in)
                fwd[row : row + cin, c * cout : (c + 1) * cout] = wide[tap * 3 + dx]


def place_back(wide, back, low_out):
    cin, cout = wide.shape[1], wide.shape[2]
    back[...] = jnp.zeros(back.shape, back.dtype)
    for tap in range(9):
        for dx in range(3):
            for c in range(LANES // cin):
                col = tap * (back.shape[1] // 9)
                col += slot_of(c - dx + 1, LANES // cin, cout, 2 * LANES, low_out)
                back[c * cin : (c + 1) * cin, col : col + cout] = wide[(8 - tap) * 3 + dx]


def spread(raw, dst):
    for g in range(dst.shape[1]):
        dst[:, g, :] = raw[:, g * LANES : (g + 1) * LANES].astype(F32)


def neighbours(low, high, groups):
    rows = low.shape[0]
    place = lax.broadcasted_iota(jnp.int32, low.shape, 0) % groups
    right = jnp.where(place == groups - 1, 0.0, pltpu.roll(low, rows - 1, 0))
    left = jnp.where(place == 0, 0.0, pltpu.roll(high, 1, 0))
    return right, left


def widen(plane, first, last):
    h, g, lanes = plane.shape
    flat = plane.astype(F32).reshape(h * g, lanes)
    right, left = neighbours(flat[:, :LANES], flat[:, lanes - LANES :], g)
    if first == LANES:
        side = jnp.concatenate([right, left], axis=1)
    else:
        lane = lax.broadcasted_iota(jnp.int32, right.shape, 1)
        side = jnp.where(lane < first, right, jnp.where(lane >= last, left, 0.0))
    return jnp.concatenate([plane.astype(BF16), side.astype(BF16).reshape(h, g, -1)], axis=2)


def fill(ext, plane, e, first, last):
    height = ext.shape[1] - 2
    edge = jnp.zeros(ext.shape[2:], ext.dtype)
    ext[e, 0] = edge
    ext[e, height + 1] = edge
    ext[e, 1 : height + 1] = widen(plane, first, last)


def window(ext, d, h0, rows, steps=(0, 1, 2)):
    parts = [
        ext[d + dz, pl.ds(h0 + dy, rows)].reshape(-1, ext.shape[3])
        for dz in steps
        for dy in range(3)
    ]
    return jnp.concatenate(parts, axis=1)


def of_steps(steps, unit):
    return pl.ds(steps[0] * 3 * unit, len(steps) * 3 * unit)


def split_steps(d, depth):
    own = [dz for dz in range(3) if 1 <= d + dz <= depth]
    return own, [dz for dz in range(3) if dz not in own]


def nt(a, b):
    return lax.dot_general(a, b, (((1,), (1,)), ((), ())), preferred_element_type=F32)


def slope(v):
    s = jax.nn.sigmoid(v)
    return s * (1.0 + v * (1.0 - s))


def first_own(vol, w, pre, ext):
    depth, height, g, _ = vol.shape
    for d in range(depth):
        fill(ext, vol[d], d + 1, 32, 96)
    step = 8

    @pl.loop(0, height // step)
    def _(block):
        h0 = block * step
        for d in range(depth):
            own, _ = split_steps(d, depth)
            left = window(ext, d, h0, step, own)
            value = jnp.dot(left, w[of_steps(own, ext.shape[3])], preferred_element_type=F32)
            pre[d, pl.ds(h0, step)] = value.reshape(step, g, -1)


def first_kernel(low, high, w, bias, pre, pooled, ext):
    depth, height, g, _ = pre.shape
    fill(ext, low[0], 0, 32, 96)
    fill(ext, high[0], depth + 1, 32, 96)
    step = 8

    @pl.loop(0, height // step)
    def _(block):
        h0 = block * step
        total = 0.0
        for d in range(depth):
            value = pre[d, pl.ds(h0, step)].reshape(step * g, -1) + bias[...]
            _, rest = split_steps(d, depth)
            for dz in rest:
                left = window(ext, d, h0, step, [dz])
                value = value + jnp.dot(
                    left, w[of_steps([dz], ext.shape[3])], preferred_element_type=F32
                )
            pre[d, pl.ds(h0, step)] = value.reshape(step, g, -1)
            total = total + value * jax.nn.sigmoid(value)
        total = jnp.sum(total.reshape(step // 2, 2, g, -1), axis=1).reshape(step // 2 * g, -1)
        a, b = total[:, :LANES], total[:, LANES:]
        lane = lax.broadcasted_iota(jnp.int32, a.shape, 1)
        half = LANES // 2
        mean = jnp.where(lane < half, a + pltpu.roll(a, half, 1), b + pltpu.roll(b, half, 1))
        pooled[pl.ds(block * (step // 2), step // 2)] = (
            (mean * 0.125).astype(BF16).reshape(step // 2, g, LANES)
        )


def second_kernel(pooled, low, high, w, bias, cot, grad, bsum, ext):
    height, g, _ = pooled.shape
    fill(ext, low[...], 0, 64, 64)
    fill(ext, high[...], 2, 64, 64)
    pre = jnp.dot(window(ext, 0, 0, height), w[...], preferred_element_type=F32) + bias[...]
    up = cot[...]
    up = jnp.broadcast_to(up[:, None], (height // 2, 2, g, LANES)).reshape(height * g, LANES)
    up = jnp.concatenate([up, up], axis=1) * 0.125
    value = (up * slope(pre)).astype(BF16)
    grad[...] = value.reshape(grad.shape)
    total = jnp.sum(value.astype(F32), axis=0, keepdims=True)
    bsum[0:1] = total[:, :LANES] + total[:, LANES:]


def tn(a, b):
    return lax.dot_general(a, b, (((0,), (0,)), ((), ())), preferred_element_type=F32)


def keep(buf, piece, rows):
    _, samples, chips, per, _ = buf.shape
    for k in range(rows.shape[0] // 16):
        first = (piece + k) * 16
        chunk, row = first // per, first % per
        core, rest = divmod(chunk, samples * chips)
        buf[core, rest // chips, rest % chips, row : row + 16] = rows[k * 16 : k * 16 + 16]


def kept(buf, piece):
    _, samples, chips, per, _ = buf.shape
    chunk, row = piece * 16 // per, piece * 16 % per
    core, rest = divmod(chunk, samples * chips)
    return buf[core, rest // chips, rest % chips, row : row + 16]


def wgrad_four(ext, grad, buf):
    height = grad.shape[0]
    up = grad[...].reshape(-1, 2 * LANES)
    for tap in range(9):
        part = tn(ext[tap // 3, tap % 3 : tap % 3 + height].reshape(-1, 2 * LANES), up)
        for dx in range(3):
            total = 0.0
            for c in range(2):
                row = slot_of(c + dx - 1, 2, 64, LANES, 64)
                total = total + part[row : row + 64, c * LANES : (c + 1) * LANES]
            keep(buf, (tap * 3 + dx) * 4, total.astype(BF16))


def wgrad_three(ext, grad, buf):
    depth, height = grad.shape[:2]
    for tap in range(9):
        part = 0.0
        for d in range(depth):
            part = part + tn(
                ext[tap // 3 + d, tap % 3 : tap % 3 + height].reshape(-1, 2 * LANES),
                grad[d].reshape(-1, 2 * LANES),
            )
        for dx in range(3):
            even, odd = 0.0, 0.0
            for c in range(4):
                row = slot_of(c + dx - 1, 4, 32, LANES, 96)
                piece = part[row : row + 32, c // 2 * LANES : (c // 2 + 1) * LANES]
                if c % 2:
                    odd = odd + piece
                else:
                    even = even + piece
            total = even + pltpu.roll(odd, 64, 1)
            lane = lax.broadcasted_iota(jnp.int32, (16, LANES), 1)
            packed = jnp.where(lane < 64, total[:16], pltpu.roll(total[16:], 64, 1))
            keep(buf, tap * 3 + dx, packed.astype(BF16))


def third_own(grad, w, part, ext):
    height = grad.shape[0]
    fill(ext, grad[...], 1, LANES, LANES)
    part[...] = nt(window(ext, 0, 0, height, [1]), w[:, of_steps([1], ext.shape[3])])


def third_kernel(low, high, w, part, pre, out, bsum, ext):
    height, g, _ = low.shape
    fill(ext, low[...], 0, LANES, LANES)
    fill(ext, high[...], 2, LANES, LANES)
    back = part[...]
    for dz in (0, 2):
        back = back + nt(window(ext, 0, 0, height, [dz]), w[:, of_steps([dz], ext.shape[3])])
    back = back * 0.125
    turned = pltpu.roll(back, 64, 1)
    lane = lax.broadcasted_iota(jnp.int32, back.shape, 1)
    up = jnp.concatenate(
        [jnp.where(lane < 64, back, turned), jnp.where(lane < 64, turned, back)], axis=1
    ).reshape(height, g, 2 * LANES)
    total = 0.0
    for d in range(pre.shape[0]):
        for h in range(height):
            value = (up[h][None] * slope(pre[d, 2 * h : 2 * h + 2])).astype(BF16)
            out[d, 2 * h : 2 * h + 2] = value
            total = total + jnp.sum(value.astype(F32), axis=0)
    total = jnp.sum(total, axis=0, keepdims=True)
    total = total[:, :LANES] + total[:, LANES:]
    bsum[1:2] = total + pltpu.roll(total, 64, 1)


def fourth_fill(grad, low, high, ext):
    depth = grad.shape[0]
    fill(ext, low[0], 0, 64, 64)
    for d in range(depth):
        fill(ext, grad[d], d + 1, 64, 64)
    fill(ext, high[0], depth + 1, 64, 64)


def fourth_part(w, out, ext, block):
    depth, height, g, _ = out.shape
    step = height // 2
    h0 = block * step
    for d in range(depth):
        value = nt(window(ext, d, h0, step), w[...])
        out[d, pl.ds(h0, step)] = value.reshape(step, g, LANES)


class Reduce:
    def __init__(self, net, buf, out, got_a, acc, got_b, mid, got_c):
        self.net = net
        self.buf, self.out = buf, out
        self.got_a, self.acc, self.got_b, self.mid, self.got_c = got_a, acc, got_b, mid, got_c

    def pair(self):
        n = self.net
        self.copies = [n.move(self.buf.at[1 - n.core], self.got_a, n.other)]

    def end(self):
        for copy in self.copies:
            copy.wait()

    def samples(self):
        n = self.net
        self.end()
        self.acc[...] = (self.buf[n.core].astype(F32) + self.got_a[...].astype(F32)).astype(BF16)
        self.copies = [
            n.move(self.acc.at[to[0]], self.got_b.at[j], to) for j, to in enumerate(n.peers)
        ]

    def chips(self):
        n = self.net
        total = self.acc[n.s].astype(F32)
        for j, copy in enumerate(self.copies):
            copy.wait()
            total = total + self.got_b[j].astype(F32)
        self.mid[...] = total.astype(BF16)
        self.copies = [
            n.move(self.mid.at[chip], self.got_c.at[j], to)
            for j, (chip, to) in enumerate(n.line)
        ]

    def back_chips(self):
        n = self.net
        total = self.mid[n.chip].astype(F32)
        for j, copy in enumerate(self.copies):
            copy.wait()
            total = total + self.got_c[j].astype(F32)
        here = self.out.at[n.core, n.s, n.chip]
        here[...] = total.astype(BF16)
        self.copies = [n.move(here, here, to) for _, to in n.line]
        self.wide = [[n.move(here, here, to)] for to in n.peers]

    def back_samples(self):
        n = self.net
        chips = len(n.line) + 1
        for j, copy in enumerate(self.copies):
            copy.wait()
            source = lax.rem(n.chip + chips - 1 - j, chips)
            here = self.out.at[n.core, n.s, source]
            for k, to in enumerate(n.peers):
                self.wide[k].append(n.move(here, here, to))

    def back_pair(self):
        n = self.net
        here = self.out.at[n.core, n.s]
        self.copies = [n.move(here, here, n.other)]
        samples = len(n.peers) + 1
        for k, group in enumerate(self.wide):
            for copy in group:
                copy.wait()
            here = self.out.at[n.core, lax.rem(n.s + samples - 1 - k, samples)]
            self.copies.append(n.move(here, here, n.other))


class Gather:
    def __init__(self, net, buf, out, got_a, field):
        self.net = net
        self.buf, self.out, self.got_a, self.field = buf, out, got_a, field

    def scatter(self):
        n = self.net
        self.copies = [
            n.move(self.buf.at[core, s], self.got_a.at[j], to)
            for j, (core, s, to) in enumerate(n.plane)
        ]

    def along(self):
        n = self.net
        total = self.buf[n.core, n.s].astype(F32)
        for j, copy in enumerate(self.copies):
            copy.wait()
            total = total + self.got_a[j].astype(F32)
        here = self.field.at[n.chip]
        here[...] = total.astype(BF16)
        self.copies = [n.move(here, here, to) for _, to in n.line]

    def back(self):
        n = self.net
        for copy in self.copies:
            copy.wait()
        here = self.out.at[n.core, n.s]
        here[...] = jnp.sum(self.field[...].astype(F32), axis=0).astype(BF16)
        self.copies = [n.move(here, here, to) for _, _, to in n.plane]

    def end(self):
        for copy in self.copies:
            copy.wait()


class Net:
    def __init__(self, samples, space, send, recv):
        self.count = 0
        self.send, self.recv = send, recv
        self.space = space
        self.s = lax.axis_index("sample")
        self.p = lax.axis_index("space")
        self.core = lax.rem(self.p, 2)
        self.chip = lax.div(self.p, 2)
        self.other = (self.s, self.chip * 2 + 1 - self.core)
        self.peers = [(lax.rem(self.s + j, samples), self.p) for j in range(1, samples)]
        self.plane = []
        for j in range(samples - 1, -1, -1):
            for k in (1, 0):
                if j or k:
                    s, core = lax.rem(self.s + j, samples), lax.rem(self.core + k, 2)
                    self.plane.append((core, s, (s, self.chip * 2 + core)))
        self.line = []
        for j in range(1, space // 2):
            to = lax.rem(self.chip + j, space // 2)
            self.line.append((to, (self.s, to * 2 + self.core)))
        self.has_low = self.p > 0
        self.has_high = self.p < space - 1
        self.above = (self.s, lax.rem(self.p + 1, space))
        self.below = (self.s, lax.rem(self.p + space - 1, space))

    def greet(self):
        barrier = pltpu.get_barrier_semaphore()

        def signal(to):
            pl.semaphore_signal(barrier, inc=1, device_id=to, device_id_type=MESH)

        for to in [self.above, self.below]:
            signal(to)
        for _, _, to in self.plane:
            signal(to)
        for _, to in self.line:
            signal(to)

    def met(self):
        barrier = pltpu.get_barrier_semaphore()
        pl.semaphore_wait(barrier, 2 + len(self.plane) + len(self.line))

    def make(self, src, dst, to):
        copy = pltpu.make_async_remote_copy(
            src_ref=src,
            dst_ref=dst,
            send_sem=self.send.at[self.count],
            recv_sem=self.recv.at[self.count],
            device_id=to,
            device_id_type=MESH,
        )
        self.count += 1
        return copy

    def move(self, src, dst, to):
        copy = self.make(src, dst, to)
        copy.start()
        return copy

    def halo(self, first, last, low, high):
        up = self.make(last, low, self.above)
        down = self.make(first, high, self.below)

        @pl.when(self.has_high)
        def _():
            up.start()

        @pl.when(self.has_low)
        def _():
            down.start()

        @pl.when(self.p == 0)
        def _():
            low[...] = jnp.zeros(low.shape, low.dtype)

        @pl.when(self.p == self.space - 1)
        def _():
            high[...] = jnp.zeros(high.shape, high.dtype)

        def finish():
            @pl.when(self.has_high)
            def _():
                up.wait_send()
                down.wait_recv()

            @pl.when(self.has_low)
            def _():
                down.wait_send()
                up.wait_recv()

        return finish


def copies_of(samples, space):
    chips = space // 2
    four = 1 + (samples - 1) + 2 * (chips - 1) + chips * (samples - 1) + samples
    flat, line = 2 * samples - 1, chips - 1
    return 2 * 4 + 1 + four + 2 * flat + line + flat + line


def share(net, rows, gots):
    def group(src, got, mine, targets):
        copies = [net.move(src, got.at[mine], to) for to in targets]
        got[mine] = src[...]
        return copies

    samples = gots[0].shape[0] // 2
    mine = net.core * samples + net.s
    copies = group(rows.at[0], gots[0], mine, [to for _, _, to in net.plane])
    yield
    for copy in copies:
        copy.wait()
    rows[1] = jnp.sum(gots[0][...], axis=0)
    copies = group(rows.at[1], gots[1], net.chip, [to for _, to in net.line])
    yield
    for copy in copies:
        copy.wait()
    rows[2] = jnp.sum(gots[1][...], axis=0)
    yield


def mono_kernel(samples, space, *refs):
    vol_hbm, tile_hbm, w3_hbm, w4_hbm, b3_hbm, b4_hbm = refs[:6]
    out, out4, out3, bsum = refs[6:10]
    refs = list(refs[10:])
    w3, w4, fwd3, fwd4, back3, back4 = refs[:6]
    pre, pooled, ext3, grad4, ext4, grad3, wide4, wide3 = refs[6:14]
    halos = refs[14:22]
    other_tile, rows = refs[22:24]
    gots = refs[24:26]
    part4 = refs[26:32]
    part3 = refs[32:35]
    cells, low_cells, high_cells, plane, bias3, bias4 = refs[35:41]
    send, recv, vol, tile, b3, b4, part, here = refs[41:]
    loads = [
        pltpu.make_async_copy(w3_hbm, w3, here.at[0]),
        pltpu.make_async_copy(vol_hbm, vol, here.at[2]),
        pltpu.make_async_copy(b3_hbm, b3, here.at[4]),
        pltpu.make_async_copy(b4_hbm, b4, here.at[5]),
        pltpu.make_async_copy(w4_hbm, w4, here.at[1]),
        pltpu.make_async_copy(tile_hbm, tile, here.at[3]),
    ]
    for load in loads:
        load.start()
    net = Net(samples, space, send, recv)
    net.greet()
    depth = vol.shape[0]
    four = Reduce(net, part4[0], out4, *part4[1:])
    three = Gather(net, part3[0], out3, *part3[1:])
    net.met()
    done = net.halo(vol_hbm.at[0], vol_hbm.at[depth - 1], halos[0], halos[1])
    tile_copy = net.move(tile_hbm, other_tile, net.other)
    loads[0].wait()
    place_forward(w3, fwd3, 96)
    loads[2].wait()
    loads[3].wait()
    for bias, narrow in ((bias3, b3), (bias4, b4)):
        width = narrow.shape[1]
        for c in range(bias.shape[1] // width):
            bias[:, c * width : (c + 1) * width] = narrow[...]
    loads[1].wait()
    for d in range(depth):
        spread(vol.at[d], cells.at[d])
    first_own(cells, fwd3, pre, ext3)
    done()
    spread(halos[0], low_cells.at[0])
    spread(halos[1], high_cells.at[0])
    first_kernel(low_cells, high_cells, fwd3, bias3, pre, pooled, ext3)
    done = net.halo(pooled, pooled, halos[2], halos[3])
    fill(ext4, pooled[...], 1, 64, 64)
    loads[4].wait()
    place_forward(w4, fwd4, 64)
    place_back(w4, back4, 128)
    place_back(w3, back3, 64)
    loads[5].wait()
    tile_copy.wait()
    odd = net.core == 1
    mine, theirs = tile[...].astype(F32), other_tile[...].astype(F32)
    spread(jnp.where(odd, theirs, mine), plane.at[: tile.shape[0]])
    spread(jnp.where(odd, mine, theirs), plane.at[tile.shape[0] :])
    rows[...] = jnp.zeros(rows.shape, F32)
    four.buf[...] = jnp.zeros(four.buf.shape, BF16)
    three.buf[...] = jnp.zeros(three.buf.shape, BF16)
    done()
    second_kernel(pooled, halos[2], halos[3], fwd4, bias4, plane, grad4, rows.at[0], ext4)
    done = net.halo(grad4, grad4, halos[4], halos[5])
    wgrad_four(ext4, grad4, four.buf)
    four.pair()
    third_own(grad4, back4, part, wide4)
    four.samples()
    done()
    third_kernel(halos[4], halos[5], back4, part, pre, grad3, rows.at[0], wide4)
    done = net.halo(grad3.at[0], grad3.at[depth - 1], halos[6].at[0], halos[7].at[0])
    bias_steps = share(net, rows, gots)
    next(bias_steps)
    wgrad_three(ext3, grad3, three.buf)
    three.scatter()
    four.chips()
    next(bias_steps)
    done()
    fourth_fill(grad3, halos[6], halos[7], wide3)
    fourth_part(back3, cells, wide3, 0)
    three.along()
    four.back_chips()
    next(bias_steps)
    fourth_part(back3, cells, wide3, 1)
    for d in range(depth):
        for g in range(cells.shape[2]):
            out[d, :, g * LANES : (g + 1) * LANES] = cells[d, :, g, :].astype(BF16)
    bsum[...] = rows[2]
    four.back_samples()
    three.back()
    four.back_pair()
    four.end()
    three.end()


def finish_kernel(grad, out4, out3, bsum, volume, wsum3, wsum4, bsum3, bsum4):
    volume[...] = grad[...]
    for t in range(27):
        for k in range(4):
            wsum4[t, k * 16 : k * 16 + 16] = kept(out4, t * 4 + k).astype(F32)
        value = kept(out3, t).astype(F32)
        wsum3[t, :16] = value[:, :64]
        wsum3[t, 16:] = pltpu.roll(value, 64, 1)[:, :64]
    bsum4[...] = bsum[0:1]
    bsum3[...] = bsum[1:2, : bsum3.shape[1]]


def per_of(samples, chips, rows):
    per = 16
    while per * 2 * samples * chips < rows:
        per *= 2
    return per


def parts(samples, chips, rows):
    per = per_of(samples, chips, rows)
    return [
        pltpu.VMEM((2, samples, chips, per, LANES), BF16),
        pltpu.VMEM((samples, chips, per, LANES), BF16),
        pltpu.VMEM((samples, chips, per, LANES), BF16),
        pltpu.VMEM((max(samples - 1, 1), chips, per, LANES), BF16),
        pltpu.VMEM((chips, per, LANES), BF16),
        pltpu.VMEM((max(chips - 1, 1), per, LANES), BF16),
    ]


def pieces(samples, chips, rows):
    per = per_of(samples, 1, rows)
    return [
        pltpu.VMEM((2, samples, 1, per, LANES), BF16),
        pltpu.VMEM((2 * samples - 1, 1, per, LANES), BF16),
        pltpu.VMEM((chips, 1, per, LANES), BF16),
    ]


def local(volume, weight_three, bias_three, weight_four, bias_four, cotangent):
    cin, mid = weight_three.shape[3:]
    cout = weight_four.shape[4]
    depth, height = volume.shape[1:3]
    groups = volume.shape[3] // LANES
    samples, space = lax.axis_size("sample"), lax.axis_size("space")
    tile = cotangent[0]
    w3 = weight_three.reshape(27, cin, mid)
    w4 = weight_four.reshape(27, mid, cout)
    wide = 2 * LANES
    half = height // 2
    shape = jax.ShapeDtypeStruct
    vm = pltpu.VMEM
    copies = copies_of(samples, space)
    vmem = pl.BlockSpec(memory_space=pltpu.VMEM)
    far = pl.BlockSpec(memory_space=pltpu.HBM)
    packed = [
        shape((2, samples, chips, per_of(samples, chips, n), LANES), BF16)
        for chips, n in ((space // 2, 27 * mid), (1, 27 * cin // 2))
    ]
    raw = shape(volume.shape[1:], BF16)
    results = pl.pallas_call(
        functools.partial(mono_kernel, samples, space),
        out_shape=[raw, *packed, shape((8, LANES), F32)],
        in_specs=[far] * 6,
        out_specs=[vmem] * 4,
        scratch_shapes=[
            vm(w3.shape, BF16),
            vm(w4.shape, BF16),
            vm((9 * wide, wide), BF16),
            vm((9 * wide, wide), BF16),
            vm((LANES, 9 * 3 * LANES), BF16),
            vm((LANES, 9 * 4 * LANES), BF16),
            vm((depth, height, groups, wide), F32),
            vm((half, groups, LANES), BF16),
            vm((depth + 2, height + 2, groups, wide), BF16),
            vm((half, groups, wide), BF16),
            vm((3, half + 2, groups, wide), BF16),
            vm((depth, height, groups, wide), BF16),
            vm((3, half + 2, groups, 4 * LANES), BF16),
            vm((depth + 2, height + 2, groups, 3 * LANES), BF16),
            *[vm(volume.shape[2:], BF16)] * 2,
            *[vm((half, groups, LANES), BF16)] * 2,
            *[vm((half, groups, wide), BF16)] * 2,
            *[vm((1, height, groups, wide), BF16)] * 2,
            vm(tile.shape, BF16),
            vm((3, 8, LANES), F32),
            vm((2 * samples, 8, LANES), F32),
            vm((space // 2, 8, LANES), F32),
            *parts(samples, space // 2, 27 * mid),
            *pieces(samples, space // 2, 27 * cin // 2),
            vm((depth, height, groups, LANES), F32),
            *[vm((1, height, groups, LANES), F32)] * 2,
            vm((2 * tile.shape[0], groups, LANES), F32),
            vm((1, wide), F32),
            vm((1, wide), F32),
            pltpu.SemaphoreType.DMA((copies,)),
            pltpu.SemaphoreType.DMA((copies,)),
            vm(volume.shape[1:], BF16),
            vm(tile.shape, BF16),
            vm((1, mid), F32),
            vm((1, cout), F32),
            vm((half * groups, LANES), F32),
            pltpu.SemaphoreType.DMA((6,)),
        ],
        compiler_params=pltpu.CompilerParams(
            collective_id=0, has_side_effects=True, vmem_limit_bytes=36 * 2**20
        ),
    )(
        *[
            pltpu.with_memory_space_constraint(a, pltpu.HBM)
            for a in (volume[0], tile, w3, w4, bias_three[None], bias_four[None])
        ]
    )
    grad_field, wsum_three, wsum_four, bsum_three, bsum_four = pl.pallas_call(
        finish_kernel,
        out_shape=[
            raw,
            shape((27, cin, mid), F32),
            shape((27, mid, cout), F32),
            shape((1, mid), F32),
            shape((1, cout), F32),
        ],
        in_specs=[vmem] * 4,
        out_specs=[vmem] * 5,
        compiler_params=pltpu.CompilerParams(vmem_limit_bytes=16 * 2**20),
    )(*results)
    return (
        grad_field.reshape(volume.shape),
        wsum_three.reshape(weight_three.shape),
        bsum_three[0],
        wsum_four.reshape(weight_four.shape),
        bsum_four[0],
    )


def solution(mesh):
    placed = (P("sample", "space", None, None), P(), P(), P(), P(), P("sample", "space", None))
    return jax.shard_map(
        local,
        mesh=mesh,
        in_specs=placed,
        out_specs=(P("sample", "space", None, None), P(), P(), P(), P()),
        check_vma=False,
    )
```

```python
import functools

import jax
import jax.numpy as jnp
from jax import lax
from jax.experimental import pallas as pl
from jax.experimental.pallas import tpu as pltpu
from jax.sharding import PartitionSpec as P

F32 = jnp.float32
BF16 = jnp.bfloat16
MESH = pl.DeviceIdType.MESH
LANES = 128
HALVES = (range(0, 5), range(5, 9))


def slot_of(cell, cells, chans, main, low_side):
    if cell < 0:
        return main + low_side
    if cell == cells:
        return main
    return cell * chans


def place_forward(wide, fwd, low_in):
    cin, cout = wide.shape[1], wide.shape[2]
    fwd[...] = jnp.zeros(fwd.shape, fwd.dtype)
    for tap in range(9):
        for dx in range(3):
            for c in range(LANES // cin):
                row = tap * 2 * LANES + slot_of(c + dx - 1, LANES // cin, cin, LANES, low_in)
                fwd[row : row + cin, c * cout : (c + 1) * cout] = wide[tap * 3 + dx]


def place_back(wide, back, low_out):
    cin, cout = wide.shape[1], wide.shape[2]
    back[...] = jnp.zeros(back.shape, back.dtype)
    for tap in range(9):
        for dx in range(3):
            for c in range(LANES // cin):
                col = tap * (back.shape[1] // 9)
                col += slot_of(c - dx + 1, LANES // cin, cout, 2 * LANES, low_out)
                back[c * cin : (c + 1) * cin, col : col + cout] = wide[(8 - tap) * 3 + dx]


def spread(raw, dst):
    for g in range(dst.shape[1]):
        dst[:, g, :] = raw[:, g * LANES : (g + 1) * LANES].astype(F32)


def neighbours(low, high, groups):
    rows = low.shape[0]
    place = lax.broadcasted_iota(jnp.int32, low.shape, 0) % groups
    right = jnp.where(place == groups - 1, 0.0, pltpu.roll(low, rows - 1, 0))
    left = jnp.where(place == 0, 0.0, pltpu.roll(high, 1, 0))
    return right, left


def widen(plane, first, last):
    h, g, lanes = plane.shape
    flat = plane.astype(F32).reshape(h * g, lanes)
    right, left = neighbours(flat[:, :LANES], flat[:, lanes - LANES :], g)
    if first == LANES:
        side = jnp.concatenate([right, left], axis=1)
    else:
        lane = lax.broadcasted_iota(jnp.int32, right.shape, 1)
        side = jnp.where(lane < first, right, jnp.where(lane >= last, left, 0.0))
    return jnp.concatenate([plane.astype(BF16), side.astype(BF16).reshape(h, g, -1)], axis=2)


def fill(ext, plane, e, first, last):
    height = ext.shape[1] - 2
    edge = jnp.zeros(ext.shape[2:], ext.dtype)
    ext[e, 0] = edge
    ext[e, height + 1] = edge
    ext[e, 1 : height + 1] = widen(plane, first, last)


def window(ext, d, h0, rows, steps=(0, 1, 2)):
    parts = [
        ext[d + dz, pl.ds(h0 + dy, rows)].reshape(-1, ext.shape[3])
        for dz in steps
        for dy in range(3)
    ]
    return jnp.concatenate(parts, axis=1)


def of_steps(steps, unit):
    return pl.ds(steps[0] * 3 * unit, len(steps) * 3 * unit)


def split_steps(d, depth):
    own = [dz for dz in range(3) if 1 <= d + dz <= depth]
    return own, [dz for dz in range(3) if dz not in own]


def nt(a, b):
    return lax.dot_general(a, b, (((1,), (1,)), ((), ())), preferred_element_type=F32)


def slope(v):
    s = jax.nn.sigmoid(v)
    return s * (1.0 + v * (1.0 - s))


def first_own(vol, w, pre, ext):
    depth, height, g, _ = vol.shape
    for d in range(depth):
        fill(ext, vol[d], d + 1, 32, 96)
    step = 8

    @pl.loop(0, height // step)
    def _(block):
        h0 = block * step
        for d in range(depth):
            own, _ = split_steps(d, depth)
            left = window(ext, d, h0, step, own)
            value = jnp.dot(left, w[of_steps(own, ext.shape[3])], preferred_element_type=F32)
            pre[d, pl.ds(h0, step)] = value.reshape(step, g, -1)


def first_kernel(low, high, w, bias, pre, pooled, ext):
    depth, height, g, _ = pre.shape
    fill(ext, low[0], 0, 32, 96)
    fill(ext, high[0], depth + 1, 32, 96)
    step = 8

    @pl.loop(0, height // step)
    def _(block):
        h0 = block * step
        total = 0.0
        for d in range(depth):
            value = pre[d, pl.ds(h0, step)].reshape(step * g, -1) + bias[...]
            _, rest = split_steps(d, depth)
            for dz in rest:
                left = window(ext, d, h0, step, [dz])
                value = value + jnp.dot(
                    left, w[of_steps([dz], ext.shape[3])], preferred_element_type=F32
                )
            pre[d, pl.ds(h0, step)] = value.reshape(step, g, -1)
            total = total + value * jax.nn.sigmoid(value)
        total = jnp.sum(total.reshape(step // 2, 2, g, -1), axis=1).reshape(step // 2 * g, -1)
        a, b = total[:, :LANES], total[:, LANES:]
        lane = lax.broadcasted_iota(jnp.int32, a.shape, 1)
        half = LANES // 2
        mean = jnp.where(lane < half, a + pltpu.roll(a, half, 1), b + pltpu.roll(b, half, 1))
        pooled[pl.ds(block * (step // 2), step // 2)] = (
            (mean * 0.125).astype(BF16).reshape(step // 2, g, LANES)
        )


def slopes(pre):
    @pl.loop(0, pre.shape[1] // 2)
    def _(block):
        for d in range(pre.shape[0]):
            here = pl.ds(block * 2, 2)
            pre[d, here] = slope(pre[d, here])


def second_own(w, bias, part, ext):
    height = ext.shape[1] - 2
    own = w[of_steps([1], ext.shape[3])]
    part[...] = jnp.dot(window(ext, 0, 0, height, [1]), own, preferred_element_type=F32) + bias[...]


def second_kernel(low, high, w, part, cot, grad, bsum, ext):
    height, g, _ = low.shape
    fill(ext, low[...], 0, 64, 64)
    fill(ext, high[...], 2, 64, 64)
    pre = part[...]
    for dz in (0, 2):
        rest = w[of_steps([dz], ext.shape[3])]
        pre = pre + jnp.dot(window(ext, 0, 0, height, [dz]), rest, preferred_element_type=F32)
    up = cot[...]
    up = jnp.broadcast_to(up[:, None], (height // 2, 2, g, LANES)).reshape(height * g, LANES)
    up = jnp.concatenate([up, up], axis=1) * 0.125
    value = (up * slope(pre)).astype(BF16)
    grad[...] = value.reshape(grad.shape)
    total = jnp.sum(value.astype(F32), axis=0, keepdims=True)
    bsum[0:1] = total[:, :LANES] + total[:, LANES:]


def tn(a, b):
    return lax.dot_general(a, b, (((0,), (0,)), ((), ())), preferred_element_type=F32)


def keep(buf, piece, rows):
    _, samples, chips, per, _ = buf.shape
    for k in range(rows.shape[0] // 16):
        first = (piece + k) * 16
        chunk, row = first // per, first % per
        core, rest = divmod(chunk, samples * chips)
        buf[core, rest // chips, rest % chips, row : row + 16] = rows[k * 16 : k * 16 + 16]


def kept(buf, piece):
    _, samples, chips, per, _ = buf.shape
    chunk, row = piece * 16 // per, piece * 16 % per
    core, rest = divmod(chunk, samples * chips)
    return buf[core, rest // chips, rest % chips, row : row + 16]


def wgrad_four(ext, grad, buf, taps):
    height = grad.shape[0]
    up = grad[...].reshape(-1, 2 * LANES)
    for place, tap in enumerate(taps):
        part = tn(ext[tap // 3, tap % 3 : tap % 3 + height].reshape(-1, 2 * LANES), up)
        for dx in range(3):
            total = 0.0
            for c in range(2):
                row = slot_of(c + dx - 1, 2, 64, LANES, 64)
                total = total + part[row : row + 64, c * LANES : (c + 1) * LANES]
            keep(buf, (place * 3 + dx) * 4, total.astype(BF16))


def wgrad_three(ext, grad, buf, taps):
    depth, height = grad.shape[:2]
    for tap in taps:
        part = 0.0
        for d in range(depth):
            part = part + tn(
                ext[tap // 3 + d, tap % 3 : tap % 3 + height].reshape(-1, 2 * LANES),
                grad[d].reshape(-1, 2 * LANES),
            )
        for dx in range(3):
            even, odd = 0.0, 0.0
            for c in range(4):
                row = slot_of(c + dx - 1, 4, 32, LANES, 96)
                piece = part[row : row + 32, c // 2 * LANES : (c // 2 + 1) * LANES]
                if c % 2:
                    odd = odd + piece
                else:
                    even = even + piece
            total = even + pltpu.roll(odd, 64, 1)
            lane = lax.broadcasted_iota(jnp.int32, (16, LANES), 1)
            packed = jnp.where(lane < 64, total[:16], pltpu.roll(total[16:], 64, 1))
            keep(buf, tap * 3 + dx, packed.astype(BF16))


def third_own(grad, w, part, ext):
    height = grad.shape[0]
    fill(ext, grad[...], 1, LANES, LANES)
    part[...] = nt(window(ext, 0, 0, height, [1]), w[:, of_steps([1], ext.shape[3])])


def third_kernel(low, high, w, part, pre, out, bsum, ext):
    height, g, _ = low.shape
    fill(ext, low[...], 0, LANES, LANES)
    fill(ext, high[...], 2, LANES, LANES)
    back = part[...]
    for dz in (0, 2):
        back = back + nt(window(ext, 0, 0, height, [dz]), w[:, of_steps([dz], ext.shape[3])])
    back = back * 0.125
    turned = pltpu.roll(back, 64, 1)
    lane = lax.broadcasted_iota(jnp.int32, back.shape, 1)
    up = jnp.concatenate(
        [jnp.where(lane < 64, back, turned), jnp.where(lane < 64, turned, back)], axis=1
    ).reshape(height, g, 2 * LANES)
    total = 0.0
    for d in range(pre.shape[0]):
        for h in range(height):
            value = (up[h][None] * pre[d, 2 * h : 2 * h + 2]).astype(BF16)
            out[d, 2 * h : 2 * h + 2] = value
            total = total + jnp.sum(value.astype(F32), axis=0)
    total = jnp.sum(total, axis=0, keepdims=True)
    total = total[:, :LANES] + total[:, LANES:]
    bsum[1:2] = total + pltpu.roll(total, 64, 1)


def fourth_fill(grad, low, high, ext):
    depth = grad.shape[0]
    fill(ext, low[0], 0, 64, 64)
    for d in range(depth):
        fill(ext, grad[d], d + 1, 64, 64)
    fill(ext, high[0], depth + 1, 64, 64)


def fourth_part(w, out, ext, block):
    depth, height, g, _ = out.shape
    step = height // 2
    h0 = block * step
    for d in range(depth):
        value = nt(window(ext, d, h0, step), w[...])
        out[d, pl.ds(h0, step)] = value.reshape(step, g, LANES)


class Reduce:
    def __init__(self, net, buf, out, got_a, acc, got_b, mid, got_c):
        self.net = net
        self.buf, self.out = buf, out
        self.got_a, self.acc, self.got_b, self.mid, self.got_c = got_a, acc, got_b, mid, got_c

    def pair(self):
        n = self.net
        self.copies = [n.move(self.buf.at[1 - n.core], self.got_a, n.other)]

    def end(self):
        for copy in self.copies:
            copy.wait()

    def samples(self):
        n = self.net
        self.end()
        self.acc[...] = (self.buf[n.core].astype(F32) + self.got_a[...].astype(F32)).astype(BF16)
        self.copies = [
            n.move(self.acc.at[to[0]], self.got_b.at[j], to) for j, to in enumerate(n.peers)
        ]

    def chips(self):
        n = self.net
        total = self.acc[n.s].astype(F32)
        for j, copy in enumerate(self.copies):
            copy.wait()
            total = total + self.got_b[j].astype(F32)
        self.mid[...] = total.astype(BF16)
        self.copies = [
            n.move(self.mid.at[chip], self.got_c.at[j], to)
            for j, (chip, to) in enumerate(n.line)
        ]

    def back_chips(self):
        n = self.net
        total = self.mid[n.chip].astype(F32)
        for j, copy in enumerate(self.copies):
            copy.wait()
            total = total + self.got_c[j].astype(F32)
        here = self.out.at[n.core, n.s, n.chip]
        here[...] = total.astype(BF16)
        self.copies = [n.move(here, here, to) for _, to in n.line]
        self.wide = [[n.move(here, here, to)] for to in n.peers]

    def back_samples(self):
        n = self.net
        chips = len(n.line) + 1
        for j, copy in enumerate(self.copies):
            copy.wait()
            source = lax.rem(n.chip + chips - 1 - j, chips)
            here = self.out.at[n.core, n.s, source]
            for k, to in enumerate(n.peers):
                self.wide[k].append(n.move(here, here, to))

    def back_pair(self):
        n = self.net
        here = self.out.at[n.core, n.s]
        self.copies = [n.move(here, here, n.other)]
        samples = len(n.peers) + 1
        for k, group in enumerate(self.wide):
            for copy in group:
                copy.wait()
            here = self.out.at[n.core, lax.rem(n.s + samples - 1 - k, samples)]
            self.copies.append(n.move(here, here, n.other))


class Gather:
    def __init__(self, net, buf, out, got_a, field):
        self.net = net
        self.buf, self.out, self.got_a, self.field = buf, out, got_a, field

    def scatter(self):
        n = self.net
        self.copies = [
            n.move(self.buf.at[core, s], self.got_a.at[j], to)
            for j, (core, s, to) in enumerate(n.plane)
        ]

    def along(self):
        n = self.net
        total = self.buf[n.core, n.s].astype(F32)
        for j, copy in enumerate(self.copies):
            copy.wait()
            total = total + self.got_a[j].astype(F32)
        here = self.field.at[n.chip]
        here[...] = total.astype(BF16)
        self.copies = [n.move(here, here, to) for _, to in n.line]

    def back(self):
        n = self.net
        for copy in self.copies:
            copy.wait()
        here = self.out.at[n.core, n.s]
        here[...] = jnp.sum(self.field[...].astype(F32), axis=0).astype(BF16)
        self.copies = [n.move(here, here, to) for _, _, to in n.plane]

    def end(self):
        for copy in self.copies:
            copy.wait()


class Net:
    def __init__(self, samples, space, send, recv):
        self.count = 0
        self.send, self.recv = send, recv
        self.space = space
        self.s = lax.axis_index("sample")
        self.p = lax.axis_index("space")
        self.core = lax.rem(self.p, 2)
        self.chip = lax.div(self.p, 2)
        self.other = (self.s, self.chip * 2 + 1 - self.core)
        self.peers = [(lax.rem(self.s + j, samples), self.p) for j in range(1, samples)]
        self.plane = []
        for j in range(samples - 1, -1, -1):
            for k in (1, 0):
                if j or k:
                    s, core = lax.rem(self.s + j, samples), lax.rem(self.core + k, 2)
                    self.plane.append((core, s, (s, self.chip * 2 + core)))
        self.line = []
        for j in range(1, space // 2):
            to = lax.rem(self.chip + j, space // 2)
            self.line.append((to, (self.s, to * 2 + self.core)))
        self.has_low = self.p > 0
        self.has_high = self.p < space - 1
        self.above = (self.s, lax.rem(self.p + 1, space))
        self.below = (self.s, lax.rem(self.p + space - 1, space))

    def greet(self):
        barrier = pltpu.get_barrier_semaphore()

        def signal(to):
            pl.semaphore_signal(barrier, inc=1, device_id=to, device_id_type=MESH)

        for to in [self.above, self.below]:
            signal(to)
        for _, _, to in self.plane:
            signal(to)
        for _, to in self.line:
            signal(to)

    def met(self):
        barrier = pltpu.get_barrier_semaphore()
        pl.semaphore_wait(barrier, 2 + len(self.plane) + len(self.line))

    def make(self, src, dst, to):
        copy = pltpu.make_async_remote_copy(
            src_ref=src,
            dst_ref=dst,
            send_sem=self.send.at[self.count],
            recv_sem=self.recv.at[self.count],
            device_id=to,
            device_id_type=MESH,
        )
        self.count += 1
        return copy

    def move(self, src, dst, to):
        copy = self.make(src, dst, to)
        copy.start()
        return copy

    def halo(self, first, last, low, high):
        up = self.make(last, low, self.above)
        down = self.make(first, high, self.below)

        @pl.when(self.has_high)
        def _():
            up.start()

        @pl.when(self.has_low)
        def _():
            down.start()

        @pl.when(self.p == 0)
        def _():
            low[...] = jnp.zeros(low.shape, low.dtype)

        @pl.when(self.p == self.space - 1)
        def _():
            high[...] = jnp.zeros(high.shape, high.dtype)

        def finish():
            @pl.when(self.has_high)
            def _():
                up.wait_send()
                down.wait_recv()

            @pl.when(self.has_low)
            def _():
                down.wait_send()
                up.wait_recv()

        return finish


def copies_of(samples, space):
    chips = space // 2
    four = 2 * (1 + (samples - 1) + 2 * (chips - 1) + chips * (samples - 1) + samples)
    flat, line = 2 * samples - 1, chips - 1
    return 2 * 4 + 1 + four + 2 * flat + line + flat + line


def share(net, rows, gots):
    def group(src, got, mine, targets):
        copies = [net.move(src, got.at[mine], to) for to in targets]
        got[mine] = src[...]
        return copies

    samples = gots[0].shape[0] // 2
    mine = net.core * samples + net.s
    copies = group(rows.at[0], gots[0], mine, [to for _, _, to in net.plane])
    yield
    for copy in copies:
        copy.wait()
    rows[1] = jnp.sum(gots[0][...], axis=0)
    copies = group(rows.at[1], gots[1], net.chip, [to for _, to in net.line])
    yield
    for copy in copies:
        copy.wait()
    rows[2] = jnp.sum(gots[1][...], axis=0)
    yield


def mono_kernel(samples, space, *refs):
    vol_hbm, tile_hbm, w3_hbm, w4_hbm, b3_hbm, b4_hbm = refs[:6]
    out, *outs4, out3, bsum = refs[6:11]
    refs = list(refs[11:])
    w3, w4, fwd3, fwd4, back3, back4 = refs[:6]
    pre, pooled, ext3, grad4, ext4, grad3, wide4, wide3 = refs[6:14]
    halos = refs[14:22]
    other_tile, rows = refs[22:24]
    gots = refs[24:26]
    parts4 = refs[26:32], refs[32:38]
    part3 = refs[38:41]
    cells, low_cells, high_cells, plane, bias3, bias4 = refs[41:47]
    send, recv, vol, tile, b3, b4, part, part_fwd, here = refs[47:]
    loads = [
        pltpu.make_async_copy(w3_hbm, w3, here.at[0]),
        pltpu.make_async_copy(vol_hbm, vol, here.at[2]),
        pltpu.make_async_copy(b3_hbm, b3, here.at[4]),
        pltpu.make_async_copy(b4_hbm, b4, here.at[5]),
        pltpu.make_async_copy(w4_hbm, w4, here.at[1]),
        pltpu.make_async_copy(tile_hbm, tile, here.at[3]),
    ]
    for load in loads:
        load.start()
    net = Net(samples, space, send, recv)
    net.greet()
    depth = vol.shape[0]
    fours = [Reduce(net, p[0], o, *p[1:]) for p, o in zip(parts4, outs4)]
    three = Gather(net, part3[0], out3, *part3[1:])
    net.met()
    done = net.halo(vol_hbm.at[0], vol_hbm.at[depth - 1], halos[0], halos[1])
    tile_copy = net.move(tile_hbm, other_tile, net.other)
    loads[0].wait()
    place_forward(w3, fwd3, 96)
    loads[2].wait()
    loads[3].wait()
    for bias, narrow in ((bias3, b3), (bias4, b4)):
        width = narrow.shape[1]
        for c in range(bias.shape[1] // width):
            bias[:, c * width : (c + 1) * width] = narrow[...]
    loads[1].wait()
    for d in range(depth):
        spread(vol.at[d], cells.at[d])
    first_own(cells, fwd3, pre, ext3)
    done()
    spread(halos[0], low_cells.at[0])
    spread(halos[1], high_cells.at[0])
    first_kernel(low_cells, high_cells, fwd3, bias3, pre, pooled, ext3)
    done = net.halo(pooled, pooled, halos[2], halos[3])
    fill(ext4, pooled[...], 1, 64, 64)
    loads[4].wait()
    place_forward(w4, fwd4, 64)
    second_own(fwd4, bias4, part_fwd, ext4)
    place_back(w4, back4, 128)
    loads[5].wait()
    tile_copy.wait()
    odd = net.core == 1
    mine, theirs = tile[...].astype(F32), other_tile[...].astype(F32)
    spread(jnp.where(odd, theirs, mine), plane.at[: tile.shape[0]])
    spread(jnp.where(odd, mine, theirs), plane.at[tile.shape[0] :])
    rows[...] = jnp.zeros(rows.shape, F32)
    for each in (*fours, three):
        each.buf[...] = jnp.zeros(each.buf.shape, BF16)
    slopes(pre)
    done()
    second_kernel(halos[2], halos[3], fwd4, part_fwd, plane, grad4, rows.at[0], ext4)
    done = net.halo(grad4, grad4, halos[4], halos[5])
    for four, taps in zip(fours, HALVES):
        wgrad_four(ext4, grad4, four.buf, taps)
        four.pair()
    third_own(grad4, back4, part, wide4)
    fours[0].samples()
    place_back(w3, back3, 64)
    fours[1].samples()
    done()
    third_kernel(halos[4], halos[5], back4, part, pre, grad3, rows.at[0], wide4)
    done = net.halo(grad3.at[0], grad3.at[depth - 1], halos[6].at[0], halos[7].at[0])
    bias_steps = share(net, rows, gots)
    next(bias_steps)
    wgrad_three(ext3, grad3, three.buf, range(0, 3))
    fours[0].chips()
    wgrad_three(ext3, grad3, three.buf, range(3, 6))
    fours[1].chips()
    wgrad_three(ext3, grad3, three.buf, range(6, 9))
    three.scatter()
    done()
    fours[0].back_chips()
    fourth_fill(grad3, halos[6], halos[7], wide3)
    fours[1].back_chips()
    next(bias_steps)
    fourth_part(back3, cells, wide3, 0)
    three.along()
    next(bias_steps)
    fourth_part(back3, cells, wide3, 1)
    for d in range(depth):
        for g in range(cells.shape[2]):
            out[d, :, g * LANES : (g + 1) * LANES] = cells[d, :, g, :].astype(BF16)
    bsum[...] = rows[2]
    for four in fours:
        four.back_samples()
    three.back()
    for four in fours:
        four.back_pair()
    for each in (*fours, three):
        each.end()


def finish_kernel(grad, out4a, out4b, out3, bsum, volume, wsum3, wsum4, bsum3, bsum4):
    volume[...] = grad[...]
    for out4, taps in zip((out4a, out4b), HALVES):
        for place, tap in enumerate(taps):
            for dx in range(3):
                for k in range(4):
                    rows = kept(out4, (place * 3 + dx) * 4 + k)
                    wsum4[tap * 3 + dx, k * 16 : k * 16 + 16] = rows.astype(F32)
    for t in range(27):
        value = kept(out3, t).astype(F32)
        wsum3[t, :16] = value[:, :64]
        wsum3[t, 16:] = pltpu.roll(value, 64, 1)[:, :64]
    bsum4[...] = bsum[0:1]
    bsum3[...] = bsum[1:2, : bsum3.shape[1]]


def per_of(samples, chips, rows):
    per = 16
    while per * 2 * samples * chips < rows:
        per *= 2
    return per


def parts(samples, chips, rows):
    per = per_of(samples, chips, rows)
    return [
        pltpu.VMEM((2, samples, chips, per, LANES), BF16),
        pltpu.VMEM((samples, chips, per, LANES), BF16),
        pltpu.VMEM((samples, chips, per, LANES), BF16),
        pltpu.VMEM((max(samples - 1, 1), chips, per, LANES), BF16),
        pltpu.VMEM((chips, per, LANES), BF16),
        pltpu.VMEM((max(chips - 1, 1), per, LANES), BF16),
    ]


def pieces(samples, chips, rows):
    per = per_of(samples, 1, rows)
    return [
        pltpu.VMEM((2, samples, 1, per, LANES), BF16),
        pltpu.VMEM((2 * samples - 1, 1, per, LANES), BF16),
        pltpu.VMEM((chips, 1, per, LANES), BF16),
    ]


def local(volume, weight_three, bias_three, weight_four, bias_four, cotangent):
    cin, mid = weight_three.shape[3:]
    cout = weight_four.shape[4]
    depth, height = volume.shape[1:3]
    groups = volume.shape[3] // LANES
    samples, space = lax.axis_size("sample"), lax.axis_size("space")
    tile = cotangent[0]
    w3 = weight_three.reshape(27, cin, mid)
    w4 = weight_four.reshape(27, mid, cout)
    wide = 2 * LANES
    half = height // 2
    shape = jax.ShapeDtypeStruct
    vm = pltpu.VMEM
    copies = copies_of(samples, space)
    vmem = pl.BlockSpec(memory_space=pltpu.VMEM)
    far = pl.BlockSpec(memory_space=pltpu.HBM)
    counts = [3 * len(taps) * mid for taps in HALVES]
    packed = [
        shape((2, samples, chips, per_of(samples, chips, n), LANES), BF16)
        for chips, n in (*[(space // 2, n) for n in counts], (1, 27 * cin // 2))
    ]
    raw = shape(volume.shape[1:], BF16)
    results = pl.pallas_call(
        functools.partial(mono_kernel, samples, space),
        out_shape=[raw, *packed, shape((8, LANES), F32)],
        in_specs=[far] * 6,
        out_specs=[vmem] * 5,
        scratch_shapes=[
            vm(w3.shape, BF16),
            vm(w4.shape, BF16),
            vm((9 * wide, wide), BF16),
            vm((9 * wide, wide), BF16),
            vm((LANES, 9 * 3 * LANES), BF16),
            vm((LANES, 9 * 4 * LANES), BF16),
            vm((depth, height, groups, wide), F32),
            vm((half, groups, LANES), BF16),
            vm((depth + 2, height + 2, groups, wide), BF16),
            vm((half, groups, wide), BF16),
            vm((3, half + 2, groups, wide), BF16),
            vm((depth, height, groups, wide), BF16),
            vm((3, half + 2, groups, 4 * LANES), BF16),
            vm((depth + 2, height + 2, groups, 3 * LANES), BF16),
            *[vm(volume.shape[2:], BF16)] * 2,
            *[vm((half, groups, LANES), BF16)] * 2,
            *[vm((half, groups, wide), BF16)] * 2,
            *[vm((1, height, groups, wide), BF16)] * 2,
            vm(tile.shape, BF16),
            vm((3, 8, LANES), F32),
            vm((2 * samples, 8, LANES), F32),
            vm((space // 2, 8, LANES), F32),
            *parts(samples, space // 2, counts[0]),
            *parts(samples, space // 2, counts[1]),
            *pieces(samples, space // 2, 27 * cin // 2),
            vm((depth, height, groups, LANES), F32),
            *[vm((1, height, groups, LANES), F32)] * 2,
            vm((2 * tile.shape[0], groups, LANES), F32),
            vm((1, wide), F32),
            vm((1, wide), F32),
            pltpu.SemaphoreType.DMA((copies,)),
            pltpu.SemaphoreType.DMA((copies,)),
            vm(volume.shape[1:], BF16),
            vm(tile.shape, BF16),
            vm((1, mid), F32),
            vm((1, cout), F32),
            vm((half * groups, LANES), F32),
            vm((half * groups, wide), F32),
            pltpu.SemaphoreType.DMA((6,)),
        ],
        compiler_params=pltpu.CompilerParams(
            collective_id=0, has_side_effects=True, vmem_limit_bytes=36 * 2**20
        ),
    )(
        *[
            pltpu.with_memory_space_constraint(a, pltpu.HBM)
            for a in (volume[0], tile, w3, w4, bias_three[None], bias_four[None])
        ]
    )
    grad_field, wsum_three, wsum_four, bsum_three, bsum_four = pl.pallas_call(
        finish_kernel,
        out_shape=[
            raw,
            shape((27, cin, mid), F32),
            shape((27, mid, cout), F32),
            shape((1, mid), F32),
            shape((1, cout), F32),
        ],
        in_specs=[vmem] * 5,
        out_specs=[vmem] * 5,
        compiler_params=pltpu.CompilerParams(vmem_limit_bytes=16 * 2**20),
    )(*results)
    return (
        grad_field.reshape(volume.shape),
        wsum_three.reshape(weight_three.shape),
        bsum_three[0],
        wsum_four.reshape(weight_four.shape),
        bsum_four[0],
    )


def solution(mesh):
    placed = (P("sample", "space", None, None), P(), P(), P(), P(), P("sample", "space", None))
    return jax.shard_map(
        local,
        mesh=mesh,
        in_specs=placed,
        out_specs=(P("sample", "space", None, None), P(), P(), P(), P()),
        check_vma=False,
    )
```

```python
import functools

import jax
import jax.numpy as jnp
from jax import lax
from jax.experimental import pallas as pl
from jax.experimental.pallas import tpu as pltpu
from jax.sharding import PartitionSpec as P

F32 = jnp.float32
BF16 = jnp.bfloat16
MESH = pl.DeviceIdType.MESH
LANES = 128
HALVES = (range(0, 5), range(5, 9))


def slot_of(cell, cells, chans, main, low_side):
    if cell < 0:
        return main + low_side
    if cell == cells:
        return main
    return cell * chans


def place_forward(wide, fwd, low_in):
    cin, cout = wide.shape[1], wide.shape[2]
    fwd[...] = jnp.zeros(fwd.shape, fwd.dtype)
    for tap in range(9):
        for dx in range(3):
            for c in range(LANES // cin):
                row = tap * 2 * LANES + slot_of(c + dx - 1, LANES // cin, cin, LANES, low_in)
                fwd[row : row + cin, c * cout : (c + 1) * cout] = wide[tap * 3 + dx]


def place_back(wide, back, low_out):
    cin, cout = wide.shape[1], wide.shape[2]
    back[...] = jnp.zeros(back.shape, back.dtype)
    for tap in range(9):
        for dx in range(3):
            for c in range(LANES // cin):
                col = tap * (back.shape[1] // 9)
                col += slot_of(c - dx + 1, LANES // cin, cout, 2 * LANES, low_out)
                back[c * cin : (c + 1) * cin, col : col + cout] = wide[(8 - tap) * 3 + dx]


def spread(raw, dst):
    for g in range(dst.shape[1]):
        dst[:, g, :] = raw[:, g * LANES : (g + 1) * LANES].astype(F32)


def neighbours(low, high, groups):
    rows = low.shape[0]
    place = lax.broadcasted_iota(jnp.int32, low.shape, 0) % groups
    right = jnp.where(place == groups - 1, 0.0, pltpu.roll(low, rows - 1, 0))
    left = jnp.where(place == 0, 0.0, pltpu.roll(high, 1, 0))
    return right, left


def widen(plane, first, last):
    h, g, lanes = plane.shape
    flat = plane.astype(F32).reshape(h * g, lanes)
    right, left = neighbours(flat[:, :LANES], flat[:, lanes - LANES :], g)
    if first == LANES:
        side = jnp.concatenate([right, left], axis=1)
    else:
        lane = lax.broadcasted_iota(jnp.int32, right.shape, 1)
        side = jnp.where(lane < first, right, jnp.where(lane >= last, left, 0.0))
    return jnp.concatenate([plane.astype(BF16), side.astype(BF16).reshape(h, g, -1)], axis=2)


def fill(ext, plane, e, first, last):
    height = ext.shape[1] - 2
    edge = jnp.zeros(ext.shape[2:], ext.dtype)
    ext[e, 0] = edge
    ext[e, height + 1] = edge
    ext[e, 1 : height + 1] = widen(plane, first, last)


def window(ext, d, h0, rows, steps=(0, 1, 2)):
    parts = [
        ext[d + dz, pl.ds(h0 + dy, rows)].reshape(-1, ext.shape[3])
        for dz in steps
        for dy in range(3)
    ]
    return jnp.concatenate(parts, axis=1)


def of_steps(steps, unit):
    return pl.ds(steps[0] * 3 * unit, len(steps) * 3 * unit)


def split_steps(d, depth):
    own = [dz for dz in range(3) if 1 <= d + dz <= depth]
    return own, [dz for dz in range(3) if dz not in own]


def nt(a, b):
    return lax.dot_general(a, b, (((1,), (1,)), ((), ())), preferred_element_type=F32)


def slope(v):
    s = jax.nn.sigmoid(v)
    return s * (1.0 + v * (1.0 - s))


def first_own(vol, w, pre, ext):
    depth, height, g, _ = vol.shape
    for d in range(depth):
        fill(ext, vol[d], d + 1, 32, 96)
    step = 8

    @pl.loop(0, height // step)
    def _(block):
        h0 = block * step
        for d in range(depth):
            own, _ = split_steps(d, depth)
            left = window(ext, d, h0, step, own)
            value = jnp.dot(left, w[of_steps(own, ext.shape[3])], preferred_element_type=F32)
            pre[d, pl.ds(h0, step)] = value.reshape(step, g, -1)


def first_kernel(low, high, w, bias, pre, pooled, ext):
    depth, height, g, _ = pre.shape
    fill(ext, low[0], 0, 32, 96)
    fill(ext, high[0], depth + 1, 32, 96)
    step = 8

    @pl.loop(0, height // step)
    def _(block):
        h0 = block * step
        total = 0.0
        for d in range(depth):
            value = pre[d, pl.ds(h0, step)].reshape(step * g, -1) + bias[...]
            _, rest = split_steps(d, depth)
            for dz in rest:
                left = window(ext, d, h0, step, [dz])
                value = value + jnp.dot(
                    left, w[of_steps([dz], ext.shape[3])], preferred_element_type=F32
                )
            pre[d, pl.ds(h0, step)] = value.reshape(step, g, -1)
            total = total + value * jax.nn.sigmoid(value)
        total = jnp.sum(total.reshape(step // 2, 2, g, -1), axis=1).reshape(step // 2 * g, -1)
        a, b = total[:, :LANES], total[:, LANES:]
        lane = lax.broadcasted_iota(jnp.int32, a.shape, 1)
        half = LANES // 2
        mean = jnp.where(lane < half, a + pltpu.roll(a, half, 1), b + pltpu.roll(b, half, 1))
        pooled[pl.ds(block * (step // 2), step // 2)] = (
            (mean * 0.125).astype(BF16).reshape(step // 2, g, LANES)
        )


def slopes(pre):
    @pl.loop(0, pre.shape[1] // 2)
    def _(block):
        for d in range(pre.shape[0]):
            here = pl.ds(block * 2, 2)
            pre[d, here] = slope(pre[d, here])


def second_own(w, bias, part, ext):
    height = ext.shape[1] - 2
    own = w[of_steps([1], ext.shape[3])]
    part[...] = jnp.dot(window(ext, 0, 0, height, [1]), own, preferred_element_type=F32) + bias[...]


def second_kernel(low, high, w, part, cot, grad, bsum, ext):
    height, g, _ = low.shape
    fill(ext, low[...], 0, 64, 64)
    fill(ext, high[...], 2, 64, 64)
    pre = part[...]
    for dz in (0, 2):
        rest = w[of_steps([dz], ext.shape[3])]
        pre = pre + jnp.dot(window(ext, 0, 0, height, [dz]), rest, preferred_element_type=F32)
    up = cot[...]
    up = jnp.broadcast_to(up[:, None], (height // 2, 2, g, LANES)).reshape(height * g, LANES)
    up = jnp.concatenate([up, up], axis=1) * 0.125
    value = (up * slope(pre)).astype(BF16)
    grad[...] = value.reshape(grad.shape)
    total = jnp.sum(value.astype(F32), axis=0, keepdims=True)
    bsum[0:1] = total[:, :LANES] + total[:, LANES:]


def tn(a, b):
    return lax.dot_general(a, b, (((0,), (0,)), ((), ())), preferred_element_type=F32)


def keep(buf, piece, rows):
    _, samples, chips, per, _ = buf.shape
    for k in range(rows.shape[0] // 16):
        first = (piece + k) * 16
        chunk, row = first // per, first % per
        core, rest = divmod(chunk, samples * chips)
        buf[core, rest // chips, rest % chips, row : row + 16] = rows[k * 16 : k * 16 + 16]


def kept(buf, piece):
    _, samples, chips, per, _ = buf.shape
    chunk, row = piece * 16 // per, piece * 16 % per
    core, rest = divmod(chunk, samples * chips)
    return buf[core, rest // chips, rest % chips, row : row + 16]


def wgrad_four(ext, grad, buf, taps):
    height = grad.shape[0]
    up = grad[...].reshape(-1, 2 * LANES)
    for place, tap in enumerate(taps):
        part = tn(ext[tap // 3, tap % 3 : tap % 3 + height].reshape(-1, 2 * LANES), up)
        for dx in range(3):
            total = 0.0
            for c in range(2):
                row = slot_of(c + dx - 1, 2, 64, LANES, 64)
                total = total + part[row : row + 64, c * LANES : (c + 1) * LANES]
            keep(buf, (place * 3 + dx) * 4, total.astype(BF16))


def wgrad_three(ext, grad, buf, taps):
    depth, height = grad.shape[:2]
    for tap in taps:
        part = 0.0
        for d in range(depth):
            part = part + tn(
                ext[tap // 3 + d, tap % 3 : tap % 3 + height].reshape(-1, 2 * LANES),
                grad[d].reshape(-1, 2 * LANES),
            )
        for dx in range(3):
            even, odd = 0.0, 0.0
            for c in range(4):
                row = slot_of(c + dx - 1, 4, 32, LANES, 96)
                piece = part[row : row + 32, c // 2 * LANES : (c // 2 + 1) * LANES]
                if c % 2:
                    odd = odd + piece
                else:
                    even = even + piece
            total = even + pltpu.roll(odd, 64, 1)
            lane = lax.broadcasted_iota(jnp.int32, (16, LANES), 1)
            packed = jnp.where(lane < 64, total[:16], pltpu.roll(total[16:], 64, 1))
            keep(buf, tap * 3 + dx, packed.astype(BF16))


def third_near(grad, w, first, last, ext):
    fill(ext, grad[...], 0, LANES, LANES)
    for dz, side in ((2, first), (0, last)):
        side[...] = third_step(w, dz, ext).astype(BF16).reshape(side.shape)


def third_step(w, dz, ext):
    return nt(window(ext, -dz, 0, ext.shape[1] - 2, [dz]), w[:, of_steps([dz], ext.shape[3])])


def third_kernel(low, high, part, pre, out, bsum):
    height, g, _ = low.shape
    back = part[...]
    for side in (low, high):
        back = back + side[...].astype(F32).reshape(back.shape)
    back = back * 0.125
    turned = pltpu.roll(back, 64, 1)
    lane = lax.broadcasted_iota(jnp.int32, back.shape, 1)
    up = jnp.concatenate(
        [jnp.where(lane < 64, back, turned), jnp.where(lane < 64, turned, back)], axis=1
    ).reshape(height, g, 2 * LANES)
    total = 0.0
    for d in range(pre.shape[0]):
        for h in range(height):
            value = (up[h][None] * pre[d, 2 * h : 2 * h + 2]).astype(BF16)
            out[d, 2 * h : 2 * h + 2] = value
            total = total + jnp.sum(value.astype(F32), axis=0)
    total = jnp.sum(total, axis=0, keepdims=True)
    total = total[:, :LANES] + total[:, LANES:]
    bsum[1:2] = total + pltpu.roll(total, 64, 1)


def fourth_near(grad, w, first, last, ext):
    depth, height = grad.shape[:2]
    for d in range(depth):
        fill(ext, grad[d], d, 64, 64)
    step = height // 2

    @pl.loop(0, 2)
    def _(block):
        h0 = block * step
        for d, dz, side in ((0, 2, first), (depth - 1, 0, last)):
            left = window(ext, d - dz, h0, step, [dz])
            value = nt(left, w[:, of_steps([dz], ext.shape[3])])
            side[0, pl.ds(h0, step)] = value.astype(BF16).reshape(step, -1, LANES)


def fourth_part(w, out, ext, block):
    depth, height, g, _ = out.shape
    step = height // 2
    h0 = block * step
    for d in range(depth):
        own, _ = split_steps(d, depth)
        left = window(ext, d - 1, h0, step, own)
        value = nt(left, w[:, of_steps(own, ext.shape[3])])
        out[d, pl.ds(h0, step)] = value.reshape(step, g, LANES)


class Reduce:
    def __init__(self, net, buf, out, got_a, acc, got_b, mid, got_c):
        self.net = net
        self.buf, self.out = buf, out
        self.got_a, self.acc, self.got_b, self.mid, self.got_c = got_a, acc, got_b, mid, got_c

    def pair(self):
        n = self.net
        self.copy = n.move(self.buf.at[1 - n.core], self.got_a, n.other)

    def samples(self):
        n = self.net
        self.copy.wait()
        self.acc[...] = (self.buf[n.core].astype(F32) + self.got_a[...].astype(F32)).astype(BF16)
        self.sem = n.ticket()
        for j, to in enumerate(n.peers):
            n.move(self.acc.at[to[0]], self.got_b.at[j], to, self.sem)

    def chips(self):
        n = self.net
        n.settle(self.got_b, self.sem)
        total = self.acc[n.s].astype(F32)
        for j in range(len(n.peers)):
            total = total + self.got_b[j].astype(F32)
        self.mid[...] = total.astype(BF16)
        self.sem = n.ticket()
        for j, (chip, to) in enumerate(n.line):
            n.move(self.mid.at[chip], self.got_c.at[j], to, self.sem)

    def back_chips(self):
        n = self.net
        n.settle(self.got_c, self.sem)
        total = self.mid[n.chip].astype(F32)
        for j in range(len(n.line)):
            total = total + self.got_c[j].astype(F32)
        here = self.out.at[n.core, n.s, n.chip]
        here[...] = total.astype(BF16)
        self.sem = n.ticket()
        for _, to in n.line:
            n.move(here, here, to, self.sem)
        self.wide = [n.ticket() for _ in n.peers]
        for k, to in enumerate(n.peers):
            n.move(here, here, to, self.wide[k])

    def back_samples(self):
        n = self.net
        chips = len(n.line) + 1
        n.settle(self.got_c, self.sem)
        for j in range(chips - 1):
            here = self.out.at[n.core, n.s, lax.rem(n.chip + chips - 1 - j, chips)]
            for k, to in enumerate(n.peers):
                n.move(here, here, to, self.wide[k])

    def back_pair(self):
        n = self.net
        samples = len(n.peers) + 1
        self.sem = n.ticket()
        here = self.out.at[n.core, n.s]
        n.move(here, here, n.other, self.sem)
        for k, sem in enumerate(self.wide):
            here = self.out.at[n.core, lax.rem(n.s + samples - 1 - k, samples)]
            n.settle(here, sem)
            n.move(here, here, n.other, self.sem)

    def end(self):
        self.net.settle(self.out.at[1 - self.net.core], self.sem)


class Gather:
    def __init__(self, net, buf, out, got_a, field):
        self.net = net
        self.buf, self.out, self.got_a, self.field = buf, out, got_a, field

    def scatter(self):
        n = self.net
        self.sem = n.ticket()
        for j, (core, s, to) in enumerate(n.plane):
            n.move(self.buf.at[core, s], self.got_a.at[j], to, self.sem)

    def along(self):
        n = self.net
        n.settle(self.got_a, self.sem)
        total = self.buf[n.core, n.s].astype(F32)
        for j in range(len(n.plane)):
            total = total + self.got_a[j].astype(F32)
        here = self.field.at[n.chip]
        here[...] = total.astype(BF16)
        self.sem = n.ticket()
        for _, to in n.line:
            n.move(here, here, to, self.sem)

    def back(self):
        n = self.net
        n.settle(self.field.at[1:], self.sem)
        here = self.out.at[n.core, n.s]
        here[...] = jnp.sum(self.field[...].astype(F32), axis=0).astype(BF16)
        self.sem = n.ticket()
        for _, _, to in n.plane:
            n.move(here, here, to, self.sem)

    def end(self):
        self.net.settle(self.got_a, self.sem)


class Net:
    def __init__(self, samples, space, send, recv):
        self.count = 0
        self.send, self.recv = send, recv
        self.space = space
        self.s = lax.axis_index("sample")
        self.p = lax.axis_index("space")
        self.core = lax.rem(self.p, 2)
        self.chip = lax.div(self.p, 2)
        self.other = (self.s, self.chip * 2 + 1 - self.core)
        self.peers = [(lax.rem(self.s + j, samples), self.p) for j in range(1, samples)]
        self.plane = []
        for j in range(samples - 1, -1, -1):
            for k in (1, 0):
                if j or k:
                    s, core = lax.rem(self.s + j, samples), lax.rem(self.core + k, 2)
                    self.plane.append((core, s, (s, self.chip * 2 + core)))
        self.line = []
        for j in range(1, space // 2):
            to = lax.rem(self.chip + j, space // 2)
            self.line.append((to, (self.s, to * 2 + self.core)))
        self.has_low = self.p > 0
        self.has_high = self.p < space - 1
        self.above = (self.s, lax.rem(self.p + 1, space))
        self.below = (self.s, lax.rem(self.p + space - 1, space))

    def greet(self):
        barrier = pltpu.get_barrier_semaphore()

        def signal(to):
            pl.semaphore_signal(barrier, inc=1, device_id=to, device_id_type=MESH)

        for to in [self.above, self.below]:
            signal(to)
        for _, _, to in self.plane:
            signal(to)
        for _, to in self.line:
            signal(to)

    def met(self):
        barrier = pltpu.get_barrier_semaphore()
        pl.semaphore_wait(barrier, 2 + len(self.plane) + len(self.line))

    def ticket(self):
        self.count += 1
        return self.count - 1

    def make(self, src, dst, to, sem=None):
        sem = self.ticket() if sem is None else sem
        return pltpu.make_async_remote_copy(
            src_ref=src,
            dst_ref=dst,
            send_sem=self.send.at[sem],
            recv_sem=self.recv.at[sem],
            device_id=to,
            device_id_type=MESH,
        )

    def move(self, src, dst, to, sem=None):
        copy = self.make(src, dst, to, sem)
        copy.start()
        return copy

    def settle(self, ref, sem):
        for of in (self.send, self.recv):
            pltpu.make_async_copy(ref, ref, of.at[sem]).wait()

    def halo(self, first, last, low, high):
        up = self.make(last, low, self.above)
        down = self.make(first, high, self.below)

        @pl.when(self.has_high)
        def _():
            up.start()

        @pl.when(self.has_low)
        def _():
            down.start()

        @pl.when(self.p == 0)
        def _():
            low[...] = jnp.zeros(low.shape, low.dtype)

        @pl.when(self.p == self.space - 1)
        def _():
            high[...] = jnp.zeros(high.shape, high.dtype)

        def finish():
            @pl.when(self.has_high)
            def _():
                up.wait_send()
                down.wait_recv()

            @pl.when(self.has_low)
            def _():
                down.wait_send()
                up.wait_recv()

        return finish


def copies_of(samples):
    return 4 * 2 + 1 + 2 * (5 + samples - 1) + 3 + 2


def share(net, rows, gots):
    def group(src, got, mine, targets):
        sem = net.ticket()
        for to in targets:
            net.move(src, got.at[mine], to, sem)
        got[mine] = src[...]
        return sem

    samples = gots[0].shape[0] // 2
    mine = net.core * samples + net.s
    sem = group(rows.at[0], gots[0], mine, [to for _, _, to in net.plane])
    yield
    net.settle(gots[0].at[1:], sem)
    rows[1] = jnp.sum(gots[0][...], axis=0)
    sem = group(rows.at[1], gots[1], net.chip, [to for _, to in net.line])
    yield
    net.settle(gots[1].at[1:], sem)
    rows[2] = jnp.sum(gots[1][...], axis=0)
    yield


def mono_kernel(samples, space, *refs):
    vol_hbm, tile_hbm, w3_hbm, w4_hbm, b3_hbm, b4_hbm = refs[:6]
    out, *outs4, out3, bsum = refs[6:11]
    refs = list(refs[11:])
    w3, w4, fwd3, fwd4, back3, back4 = refs[:6]
    pre, pooled, ext3, grad4, ext4, grad3, wide4, wide3 = refs[6:14]
    halos = refs[14:22]
    near = refs[-4:]
    other_tile, rows = refs[22:24]
    gots = refs[24:26]
    parts4 = refs[26:32], refs[32:38]
    part3 = refs[38:41]
    cells, low_cells, high_cells, plane, bias3, bias4 = refs[41:47]
    send, recv, vol, tile, b3, b4, part, part_fwd, here = refs[47:-4]
    loads = [
        pltpu.make_async_copy(w3_hbm, w3, here.at[0]),
        pltpu.make_async_copy(vol_hbm, vol, here.at[2]),
        pltpu.make_async_copy(b3_hbm, b3, here.at[4]),
        pltpu.make_async_copy(b4_hbm, b4, here.at[5]),
        pltpu.make_async_copy(w4_hbm, w4, here.at[1]),
        pltpu.make_async_copy(tile_hbm, tile, here.at[3]),
    ]
    for load in loads:
        load.start()
    net = Net(samples, space, send, recv)
    net.greet()
    depth = vol.shape[0]
    fours = [Reduce(net, p[0], o, *p[1:]) for p, o in zip(parts4, outs4)]
    three = Gather(net, part3[0], out3, *part3[1:])
    net.met()
    done = net.halo(vol_hbm.at[0], vol_hbm.at[depth - 1], halos[0], halos[1])
    tile_copy = net.move(tile_hbm, other_tile, net.other)
    loads[0].wait()
    place_forward(w3, fwd3, 96)
    loads[2].wait()
    loads[3].wait()
    for bias, narrow in ((bias3, b3), (bias4, b4)):
        width = narrow.shape[1]
        for c in range(bias.shape[1] // width):
            bias[:, c * width : (c + 1) * width] = narrow[...]
    loads[1].wait()
    for d in range(depth):
        spread(vol.at[d], cells.at[d])
    first_own(cells, fwd3, pre, ext3)
    done()
    spread(halos[0], low_cells.at[0])
    spread(halos[1], high_cells.at[0])
    first_kernel(low_cells, high_cells, fwd3, bias3, pre, pooled, ext3)
    done = net.halo(pooled, pooled, halos[2], halos[3])
    fill(ext4, pooled[...], 1, 64, 64)
    loads[4].wait()
    place_forward(w4, fwd4, 64)
    second_own(fwd4, bias4, part_fwd, ext4)
    place_back(w4, back4, 128)
    loads[5].wait()
    tile_copy.wait()
    odd = net.core == 1
    mine, theirs = tile[...].astype(F32), other_tile[...].astype(F32)
    spread(jnp.where(odd, theirs, mine), plane.at[: tile.shape[0]])
    spread(jnp.where(odd, mine, theirs), plane.at[tile.shape[0] :])
    rows[...] = jnp.zeros(rows.shape, F32)
    for each in (*fours, three):
        each.buf[...] = jnp.zeros(each.buf.shape, BF16)
    slopes(pre)
    done()
    second_kernel(halos[2], halos[3], fwd4, part_fwd, plane, grad4, rows.at[0], ext4)
    third_near(grad4, back4, near[0], near[1], wide4)
    done = net.halo(near[0], near[1], halos[4], halos[5])
    for four, taps in zip(fours, HALVES):
        wgrad_four(ext4, grad4, four.buf, taps)
        four.pair()
    part[...] = third_step(back4, 1, wide4)
    fours[0].samples()
    place_back(w3, back3, 64)
    fours[1].samples()
    done()
    third_kernel(halos[4], halos[5], part, pre, grad3, rows.at[0])
    bias_steps = share(net, rows, gots)
    next(bias_steps)
    wgrad_three(ext3, grad3, three.buf, range(0, 3))
    fours[0].chips()
    wgrad_three(ext3, grad3, three.buf, range(3, 6))
    fours[1].chips()
    wgrad_three(ext3, grad3, three.buf, range(6, 9))
    three.scatter()
    fourth_near(grad3, back3, near[2], near[3], wide3)
    fours[0].back_chips()
    done = net.halo(near[2], near[3], halos[6], halos[7])
    fourth_part(back3, cells, wide3, 0)
    fours[1].back_chips()
    next(bias_steps)
    fourth_part(back3, cells, wide3, 1)
    three.along()
    done()
    for d, side in ((0, halos[6]), (depth - 1, halos[7])):
        cells[d] = cells[d] + side[0].astype(F32)
    for d in range(depth):
        for g in range(cells.shape[2]):
            out[d, :, g * LANES : (g + 1) * LANES] = cells[d, :, g, :].astype(BF16)
    fours[0].back_samples()
    fours[1].back_samples()
    three.back()
    next(bias_steps)
    bsum[...] = rows[2]
    fours[0].back_pair()
    fours[1].back_pair()
    for each in (*fours, three):
        each.end()


def finish_kernel(grad, out4a, out4b, out3, bsum, volume, wsum3, wsum4, bsum3, bsum4):
    volume[...] = grad[...]
    for out4, taps in zip((out4a, out4b), HALVES):
        for place, tap in enumerate(taps):
            for dx in range(3):
                for k in range(4):
                    rows = kept(out4, (place * 3 + dx) * 4 + k)
                    wsum4[tap * 3 + dx, k * 16 : k * 16 + 16] = rows.astype(F32)
    for t in range(27):
        value = kept(out3, t).astype(F32)
        wsum3[t, :16] = value[:, :64]
        wsum3[t, 16:] = pltpu.roll(value, 64, 1)[:, :64]
    bsum4[...] = bsum[0:1]
    bsum3[...] = bsum[1:2, : bsum3.shape[1]]


def per_of(samples, chips, rows):
    per = 16
    while per * 2 * samples * chips < rows:
        per *= 2
    return per


def parts(samples, chips, rows):
    per = per_of(samples, chips, rows)
    return [
        pltpu.VMEM((2, samples, chips, per, LANES), BF16),
        pltpu.VMEM((samples, chips, per, LANES), BF16),
        pltpu.VMEM((samples, chips, per, LANES), BF16),
        pltpu.VMEM((max(samples - 1, 1), chips, per, LANES), BF16),
        pltpu.VMEM((chips, per, LANES), BF16),
        pltpu.VMEM((max(chips - 1, 1), per, LANES), BF16),
    ]


def pieces(samples, chips, rows):
    per = per_of(samples, 1, rows)
    return [
        pltpu.VMEM((2, samples, 1, per, LANES), BF16),
        pltpu.VMEM((2 * samples - 1, 1, per, LANES), BF16),
        pltpu.VMEM((chips, 1, per, LANES), BF16),
    ]


def local(volume, weight_three, bias_three, weight_four, bias_four, cotangent):
    cin, mid = weight_three.shape[3:]
    cout = weight_four.shape[4]
    depth, height = volume.shape[1:3]
    groups = volume.shape[3] // LANES
    samples, space = lax.axis_size("sample"), lax.axis_size("space")
    tile = cotangent[0]
    w3 = weight_three.reshape(27, cin, mid)
    w4 = weight_four.reshape(27, mid, cout)
    wide = 2 * LANES
    half = height // 2
    shape = jax.ShapeDtypeStruct
    vm = pltpu.VMEM
    copies = copies_of(samples)
    vmem = pl.BlockSpec(memory_space=pltpu.VMEM)
    far = pl.BlockSpec(memory_space=pltpu.HBM)
    counts = [3 * len(taps) * mid for taps in HALVES]
    packed = [
        shape((2, samples, chips, per_of(samples, chips, n), LANES), BF16)
        for chips, n in (*[(space // 2, n) for n in counts], (1, 27 * cin // 2))
    ]
    raw = shape(volume.shape[1:], BF16)
    results = pl.pallas_call(
        functools.partial(mono_kernel, samples, space),
        out_shape=[raw, *packed, shape((8, LANES), F32)],
        in_specs=[far] * 6,
        out_specs=[vmem] * 5,
        scratch_shapes=[
            vm(w3.shape, BF16),
            vm(w4.shape, BF16),
            vm((9 * wide, wide), BF16),
            vm((9 * wide, wide), BF16),
            vm((LANES, 9 * 3 * LANES), BF16),
            vm((LANES, 9 * 4 * LANES), BF16),
            vm((depth, height, groups, wide), F32),
            vm((half, groups, LANES), BF16),
            vm((depth + 2, height + 2, groups, wide), BF16),
            vm((half, groups, wide), BF16),
            vm((3, half + 2, groups, wide), BF16),
            vm((depth, height, groups, wide), BF16),
            vm((1, half + 2, groups, 4 * LANES), BF16),
            vm((depth, height + 2, groups, 3 * LANES), BF16),
            *[vm(volume.shape[2:], BF16)] * 2,
            *[vm((half, groups, LANES), BF16)] * 2,
            *[vm((half, groups, LANES), BF16)] * 2,
            *[vm((1, height, groups, LANES), BF16)] * 2,
            vm(tile.shape, BF16),
            vm((3, 8, LANES), F32),
            vm((2 * samples, 8, LANES), F32),
            vm((space // 2, 8, LANES), F32),
            *parts(samples, space // 2, counts[0]),
            *parts(samples, space // 2, counts[1]),
            *pieces(samples, space // 2, 27 * cin // 2),
            vm((depth, height, groups, LANES), F32),
            *[vm((1, height, groups, LANES), F32)] * 2,
            vm((2 * tile.shape[0], groups, LANES), F32),
            vm((1, wide), F32),
            vm((1, wide), F32),
            pltpu.SemaphoreType.DMA((copies,)),
            pltpu.SemaphoreType.DMA((copies,)),
            vm(volume.shape[1:], BF16),
            vm(tile.shape, BF16),
            vm((1, mid), F32),
            vm((1, cout), F32),
            vm((half * groups, LANES), F32),
            vm((half * groups, wide), F32),
            pltpu.SemaphoreType.DMA((6,)),
            *[vm((half, groups, LANES), BF16)] * 2,
            *[vm((1, height, groups, LANES), BF16)] * 2,
        ],
        compiler_params=pltpu.CompilerParams(
            collective_id=0, has_side_effects=True, vmem_limit_bytes=36 * 2**20
        ),
    )(
        *[
            pltpu.with_memory_space_constraint(a, pltpu.HBM)
            for a in (volume[0], tile, w3, w4, bias_three[None], bias_four[None])
        ]
    )
    grad_field, wsum_three, wsum_four, bsum_three, bsum_four = pl.pallas_call(
        finish_kernel,
        out_shape=[
            raw,
            shape((27, cin, mid), F32),
            shape((27, mid, cout), F32),
            shape((1, mid), F32),
            shape((1, cout), F32),
        ],
        in_specs=[vmem] * 5,
        out_specs=[vmem] * 5,
        compiler_params=pltpu.CompilerParams(vmem_limit_bytes=16 * 2**20),
    )(*results)
    return (
        grad_field.reshape(volume.shape),
        wsum_three.reshape(weight_three.shape),
        bsum_three[0],
        wsum_four.reshape(weight_four.shape),
        bsum_four[0],
    )


def solution(mesh):
    placed = (P("sample", "space", None, None), P(), P(), P(), P(), P("sample", "space", None))
    return jax.shard_map(
        local,
        mesh=mesh,
        in_specs=placed,
        out_specs=(P("sample", "space", None, None), P(), P(), P(), P()),
        check_vma=False,
    )
```

```python
import functools

import jax
import jax.numpy as jnp
from jax import lax
from jax.experimental import pallas as pl
from jax.experimental.pallas import tpu as pltpu
from jax.sharding import PartitionSpec as P

F32 = jnp.float32
BF16 = jnp.bfloat16
MESH = pl.DeviceIdType.MESH
LANES = 128
HALVES = (range(0, 5), range(5, 9))


def slot_of(cell, cells, chans, main, low_side):
    if cell < 0:
        return main + low_side
    if cell == cells:
        return main
    return cell * chans


def place_forward(wide, fwd, low_in):
    cin, cout = wide.shape[1], wide.shape[2]
    fwd[...] = jnp.zeros(fwd.shape, fwd.dtype)
    for tap in range(9):
        for dx in range(3):
            for c in range(LANES // cin):
                row = tap * 2 * LANES + slot_of(c + dx - 1, LANES // cin, cin, LANES, low_in)
                fwd[row : row + cin, c * cout : (c + 1) * cout] = wide[tap * 3 + dx]


def place_back(wide, back, low_out, blocks=(0, 0, 0)):
    cin, cout = wide.shape[1], wide.shape[2]
    per = 3 if max(blocks) else 9
    unit = back.shape[1] // per
    back[...] = jnp.zeros(back.shape, back.dtype)
    for tap in range(9):
        for dx in range(3):
            for c in range(LANES // cin):
                row = blocks[tap // 3] * LANES + c * cin
                col = tap % per * unit
                col += slot_of(c - dx + 1, LANES // cin, cout, 2 * LANES, low_out)
                back[row : row + cin, col : col + cout] = wide[(8 - tap) * 3 + dx]


def spread(raw, dst):
    for g in range(dst.shape[1]):
        dst[:, g, :] = raw[:, g * LANES : (g + 1) * LANES].astype(F32)


def neighbours(low, high, groups):
    rows = low.shape[0]
    place = lax.broadcasted_iota(jnp.int32, low.shape, 0) % groups
    right = jnp.where(place == groups - 1, 0.0, pltpu.roll(low, rows - 1, 0))
    left = jnp.where(place == 0, 0.0, pltpu.roll(high, 1, 0))
    return right, left


def widen(plane, first, last):
    h, g, lanes = plane.shape
    flat = plane.astype(F32).reshape(h * g, lanes)
    right, left = neighbours(flat[:, :LANES], flat[:, lanes - LANES :], g)
    if first == LANES:
        side = jnp.concatenate([right, left], axis=1)
    else:
        lane = lax.broadcasted_iota(jnp.int32, right.shape, 1)
        side = jnp.where(lane < first, right, jnp.where(lane >= last, left, 0.0))
    return jnp.concatenate([plane.astype(BF16), side.astype(BF16).reshape(h, g, -1)], axis=2)


def fill(ext, plane, e, first, last):
    height = ext.shape[1] - 2
    edge = jnp.zeros(ext.shape[2:], ext.dtype)
    ext[e, 0] = edge
    ext[e, height + 1] = edge
    ext[e, 1 : height + 1] = widen(plane, first, last)


def window(ext, d, h0, rows, steps=(0, 1, 2)):
    parts = [
        ext[d + dz, pl.ds(h0 + dy, rows)].reshape(-1, ext.shape[3])
        for dz in steps
        for dy in range(3)
    ]
    return jnp.concatenate(parts, axis=1)


def of_steps(steps, unit):
    return pl.ds(steps[0] * 3 * unit, len(steps) * 3 * unit)


def split_steps(d, depth):
    own = [dz for dz in range(3) if 1 <= d + dz <= depth]
    return own, [dz for dz in range(3) if dz not in own]


def nt(a, b):
    return lax.dot_general(a, b, (((1,), (1,)), ((), ())), preferred_element_type=F32)


def slope(v):
    s = jax.nn.sigmoid(v)
    return s * (1.0 + v * (1.0 - s))


def first_own(vol, w, pre, ext):
    depth, height, g, _ = vol.shape
    for d in range(depth):
        fill(ext, vol[d], d + 1, 32, 96)
    step = 8

    @pl.loop(0, height // step)
    def _(block):
        h0 = block * step
        for d in range(depth):
            own, _ = split_steps(d, depth)
            left = window(ext, d, h0, step, own)
            value = jnp.dot(left, w[of_steps(own, ext.shape[3])], preferred_element_type=F32)
            pre[d, pl.ds(h0, step)] = value.reshape(step, g, -1)


def first_kernel(low, high, w, bias, pre, pooled, ext):
    depth, height, g, _ = pre.shape
    fill(ext, low[0], 0, 32, 96)
    fill(ext, high[0], depth + 1, 32, 96)
    step = 8

    @pl.loop(0, height // step)
    def _(block):
        h0 = block * step
        total = 0.0
        for d in range(depth):
            value = pre[d, pl.ds(h0, step)].reshape(step * g, -1) + bias[...]
            _, rest = split_steps(d, depth)
            for dz in rest:
                left = window(ext, d, h0, step, [dz])
                value = value + jnp.dot(
                    left, w[of_steps([dz], ext.shape[3])], preferred_element_type=F32
                )
            pre[d, pl.ds(h0, step)] = value.reshape(step, g, -1)
            total = total + value * jax.nn.sigmoid(value)
        total = jnp.sum(total.reshape(step // 2, 2, g, -1), axis=1).reshape(step // 2 * g, -1)
        a, b = total[:, :LANES], total[:, LANES:]
        lane = lax.broadcasted_iota(jnp.int32, a.shape, 1)
        half = LANES // 2
        mean = jnp.where(lane < half, a + pltpu.roll(a, half, 1), b + pltpu.roll(b, half, 1))
        pooled[pl.ds(block * (step // 2), step // 2)] = (
            (mean * 0.125).astype(BF16).reshape(step // 2, g, LANES)
        )


def slopes(pre):
    @pl.loop(0, pre.shape[1] // 2)
    def _(block):
        for d in range(pre.shape[0]):
            here = pl.ds(block * 2, 2)
            pre[d, here] = slope(pre[d, here])


def second_own(w, bias, part, ext):
    height = ext.shape[1] - 2
    own = w[of_steps([1], ext.shape[3])]
    part[...] = jnp.dot(window(ext, 0, 0, height, [1]), own, preferred_element_type=F32) + bias[...]


def second_kernel(low, high, w, part, cot, grad, bsum, ext):
    height, g, _ = low.shape
    fill(ext, low[...], 0, 64, 64)
    fill(ext, high[...], 2, 64, 64)
    pre = part[...]
    for dz in (0, 2):
        rest = w[of_steps([dz], ext.shape[3])]
        pre = pre + jnp.dot(window(ext, 0, 0, height, [dz]), rest, preferred_element_type=F32)
    up = cot[...]
    up = jnp.broadcast_to(up[:, None], (height // 2, 2, g, LANES)).reshape(height * g, LANES)
    up = jnp.concatenate([up, up], axis=1) * 0.125
    value = (up * slope(pre)).astype(BF16)
    grad[...] = value.reshape(grad.shape)
    total = jnp.sum(value.astype(F32), axis=0, keepdims=True)
    bsum[0:1] = total[:, :LANES] + total[:, LANES:]


def tn(a, b):
    return lax.dot_general(a, b, (((0,), (0,)), ((), ())), preferred_element_type=F32)


def keep(buf, piece, rows):
    _, samples, chips, per, _ = buf.shape
    for k in range(rows.shape[0] // 16):
        first = (piece + k) * 16
        chunk, row = first // per, first % per
        core, rest = divmod(chunk, samples * chips)
        buf[core, rest // chips, rest % chips, row : row + 16] = rows[k * 16 : k * 16 + 16]


def kept(buf, piece):
    _, samples, chips, per, _ = buf.shape
    chunk, row = piece * 16 // per, piece * 16 % per
    core, rest = divmod(chunk, samples * chips)
    return buf[core, rest // chips, rest % chips, row : row + 16]


def wgrad_four(ext, grad, buf, taps):
    height = grad.shape[0]
    up = grad[...].reshape(-1, 2 * LANES)
    for place, tap in enumerate(taps):
        part = tn(ext[tap // 3, tap % 3 : tap % 3 + height].reshape(-1, 2 * LANES), up)
        for dx in range(3):
            total = 0.0
            for c in range(2):
                row = slot_of(c + dx - 1, 2, 64, LANES, 64)
                total = total + part[row : row + 64, c * LANES : (c + 1) * LANES]
            keep(buf, (place * 3 + dx) * 4, total.astype(BF16))


def wgrad_three(ext, grad, buf, taps):
    depth, height = grad.shape[:2]
    for tap in taps:
        part = 0.0
        for d in range(depth):
            part = part + tn(
                ext[tap // 3 + d, tap % 3 : tap % 3 + height].reshape(-1, 2 * LANES),
                grad[d].reshape(-1, 2 * LANES),
            )
        for dx in range(3):
            even, odd = 0.0, 0.0
            for c in range(4):
                row = slot_of(c + dx - 1, 4, 32, LANES, 96)
                piece = part[row : row + 32, c // 2 * LANES : (c // 2 + 1) * LANES]
                if c % 2:
                    odd = odd + piece
                else:
                    even = even + piece
            total = even + pltpu.roll(odd, 64, 1)
            lane = lax.broadcasted_iota(jnp.int32, (16, LANES), 1)
            packed = jnp.where(lane < 64, total[:16], pltpu.roll(total[16:], 64, 1))
            keep(buf, tap * 3 + dx, packed.astype(BF16))


def third_near(grad, w, first, last, ext):
    fill(ext, grad[...], 0, LANES, LANES)
    value = nt(third_window(ext), w[: 2 * LANES]).astype(BF16)
    first[...] = value[:, :LANES].reshape(first.shape)
    last[...] = value[:, LANES:].reshape(last.shape)


def third_window(ext):
    return window(ext, 0, 0, ext.shape[1] - 2, [0])


def third_kernel(low, high, part, pre, out, bsum):
    height, g, _ = low.shape
    back = part[...]
    for side in (low, high):
        back = back + side[...].astype(F32).reshape(back.shape)
    back = back * 0.125
    turned = pltpu.roll(back, 64, 1)
    lane = lax.broadcasted_iota(jnp.int32, back.shape, 1)
    up = jnp.concatenate(
        [jnp.where(lane < 64, back, turned), jnp.where(lane < 64, turned, back)], axis=1
    ).reshape(height, g, 2 * LANES)
    total = 0.0
    for d in range(pre.shape[0]):
        for h in range(height):
            value = (up[h][None] * pre[d, 2 * h : 2 * h + 2]).astype(BF16)
            out[d, 2 * h : 2 * h + 2] = value
            total = total + jnp.sum(value.astype(F32), axis=0)
    total = jnp.sum(total, axis=0, keepdims=True)
    total = total[:, :LANES] + total[:, LANES:]
    bsum[1:2] = total + pltpu.roll(total, 64, 1)


def fourth_near(grad, w, first, last, ext):
    depth, height = grad.shape[:2]
    for d in range(depth):
        fill(ext, grad[d], d, 64, 64)
    step = height // 2

    @pl.loop(0, 2)
    def _(block):
        h0 = block * step
        for d, dz, side in ((0, 2, first), (depth - 1, 0, last)):
            left = window(ext, d - dz, h0, step, [dz])
            value = nt(left, w[:, of_steps([dz], ext.shape[3])])
            side[0, pl.ds(h0, step)] = value.astype(BF16).reshape(step, -1, LANES)


def fourth_part(w, out, ext, block):
    depth, height, g, _ = out.shape
    step = height // 2
    h0 = block * step
    for d in range(depth):
        own, _ = split_steps(d, depth)
        left = window(ext, d - 1, h0, step, own)
        value = nt(left, w[:, of_steps(own, ext.shape[3])])
        out[d, pl.ds(h0, step)] = value.reshape(step, g, LANES)


class Reduce:
    def __init__(self, net, buf, out, got_a, acc, got_b, mid, got_c):
        self.net = net
        self.buf, self.out = buf, out
        self.got_a, self.acc, self.got_b, self.mid, self.got_c = got_a, acc, got_b, mid, got_c

    def pair(self):
        n = self.net
        self.copy = n.move(self.buf.at[1 - n.core], self.got_a, n.other)

    def samples(self):
        n = self.net
        self.copy.wait()
        self.acc[...] = (self.buf[n.core].astype(F32) + self.got_a[...].astype(F32)).astype(BF16)
        self.sem = n.ticket()
        for j, to in enumerate(n.peers):
            n.move(self.acc.at[to[0]], self.got_b.at[j], to, self.sem)

    def chips(self):
        n = self.net
        n.settle(self.got_b, self.sem)
        total = self.acc[n.s].astype(F32)
        for j in range(len(n.peers)):
            total = total + self.got_b[j].astype(F32)
        self.mid[...] = total.astype(BF16)
        self.sem = n.ticket()
        for j, (chip, to) in enumerate(n.line):
            n.move(self.mid.at[chip], self.got_c.at[j], to, self.sem)

    def back_chips(self):
        n = self.net
        n.settle(self.got_c, self.sem)
        total = self.mid[n.chip].astype(F32)
        for j in range(len(n.line)):
            total = total + self.got_c[j].astype(F32)
        here = self.out.at[n.core, n.s, n.chip]
        here[...] = total.astype(BF16)
        self.sem = n.ticket()
        for _, to in n.line:
            n.move(here, here, to, self.sem)
        self.wide = [n.ticket() for _ in n.peers]
        for k, to in enumerate(n.peers):
            n.move(here, here, to, self.wide[k])

    def back_samples(self):
        n = self.net
        chips = len(n.line) + 1
        n.settle(self.got_c, self.sem)
        for j in range(chips - 1):
            here = self.out.at[n.core, n.s, lax.rem(n.chip + chips - 1 - j, chips)]
            for k, to in enumerate(n.peers):
                n.move(here, here, to, self.wide[k])

    def back_pair(self):
        n = self.net
        samples = len(n.peers) + 1
        self.sem = n.ticket()
        here = self.out.at[n.core, n.s]
        n.move(here, here, n.other, self.sem)
        for k, sem in enumerate(self.wide):
            here = self.out.at[n.core, lax.rem(n.s + samples - 1 - k, samples)]
            n.settle(here, sem)
            n.move(here, here, n.other, self.sem)

    def end(self):
        self.net.settle(self.out.at[1 - self.net.core], self.sem)


class Gather:
    def __init__(self, net, buf, out, got_a, field):
        self.net = net
        self.buf, self.out, self.got_a, self.field = buf, out, got_a, field

    def scatter(self):
        n = self.net
        self.sem = n.ticket()
        for j, (core, s, to) in enumerate(n.plane):
            n.move(self.buf.at[core, s], self.got_a.at[j], to, self.sem)

    def along(self):
        n = self.net
        n.settle(self.got_a, self.sem)
        total = self.buf[n.core, n.s].astype(F32)
        for j in range(len(n.plane)):
            total = total + self.got_a[j].astype(F32)
        here = self.field.at[n.chip]
        here[...] = total.astype(BF16)
        self.sem = n.ticket()
        for _, to in n.line:
            n.move(here, here, to, self.sem)

    def back(self):
        n = self.net
        n.settle(self.field.at[1:], self.sem)
        here = self.out.at[n.core, n.s]
        here[...] = jnp.sum(self.field[...].astype(F32), axis=0).astype(BF16)
        self.sem = n.ticket()
        for _, _, to in n.plane:
            n.move(here, here, to, self.sem)

    def end(self):
        self.net.settle(self.got_a, self.sem)


class Net:
    def __init__(self, samples, space, send, recv):
        self.count = 0
        self.send, self.recv = send, recv
        self.space = space
        self.s = lax.axis_index("sample")
        self.p = lax.axis_index("space")
        self.core = lax.rem(self.p, 2)
        self.chip = lax.div(self.p, 2)
        self.other = (self.s, self.chip * 2 + 1 - self.core)
        self.peers = [(lax.rem(self.s + j, samples), self.p) for j in range(1, samples)]
        self.plane = []
        for j in range(samples - 1, -1, -1):
            for k in (1, 0):
                if j or k:
                    s, core = lax.rem(self.s + j, samples), lax.rem(self.core + k, 2)
                    self.plane.append((core, s, (s, self.chip * 2 + core)))
        self.line = []
        for j in range(1, space // 2):
            to = lax.rem(self.chip + j, space // 2)
            self.line.append((to, (self.s, to * 2 + self.core)))
        self.has_low = self.p > 0
        self.has_high = self.p < space - 1
        self.above = (self.s, lax.rem(self.p + 1, space))
        self.below = (self.s, lax.rem(self.p + space - 1, space))

    def greet(self):
        barrier = pltpu.get_barrier_semaphore()

        def signal(to):
            pl.semaphore_signal(barrier, inc=1, device_id=to, device_id_type=MESH)

        for to in [self.above, self.below]:
            signal(to)
        for _, _, to in self.plane:
            signal(to)
        for _, to in self.line:
            signal(to)

    def met(self):
        barrier = pltpu.get_barrier_semaphore()
        pl.semaphore_wait(barrier, 2 + len(self.plane) + len(self.line))

    def ticket(self):
        self.count += 1
        return self.count - 1

    def make(self, src, dst, to, sem=None):
        sem = self.ticket() if sem is None else sem
        return pltpu.make_async_remote_copy(
            src_ref=src,
            dst_ref=dst,
            send_sem=self.send.at[sem],
            recv_sem=self.recv.at[sem],
            device_id=to,
            device_id_type=MESH,
        )

    def move(self, src, dst, to, sem=None):
        copy = self.make(src, dst, to, sem)
        copy.start()
        return copy

    def settle(self, ref, sem):
        for of in (self.send, self.recv):
            pltpu.make_async_copy(ref, ref, of.at[sem]).wait()

    def halo(self, first, last, low, high):
        up = self.make(last, low, self.above)
        down = self.make(first, high, self.below)

        @pl.when(self.has_high)
        def _():
            up.start()

        @pl.when(self.has_low)
        def _():
            down.start()

        @pl.when(self.p == 0)
        def _():
            low[...] = jnp.zeros(low.shape, low.dtype)

        @pl.when(self.p == self.space - 1)
        def _():
            high[...] = jnp.zeros(high.shape, high.dtype)

        def finish():
            @pl.when(self.has_high)
            def _():
                up.wait_send()
                down.wait_recv()

            @pl.when(self.has_low)
            def _():
                down.wait_send()
                up.wait_recv()

        return finish


def copies_of(samples):
    return 4 * 2 + 1 + 2 * (5 + samples - 1) + 3 + 2


def share(net, rows, gots):
    def group(src, got, mine, targets):
        sem = net.ticket()
        for to in targets:
            net.move(src, got.at[mine], to, sem)
        got[mine] = src[...]
        return sem

    samples = gots[0].shape[0] // 2
    mine = net.core * samples + net.s
    sem = group(rows.at[0], gots[0], mine, [to for _, _, to in net.plane])
    yield
    net.settle(gots[0].at[1:], sem)
    rows[1] = jnp.sum(gots[0][...], axis=0)
    sem = group(rows.at[1], gots[1], net.chip, [to for _, to in net.line])
    yield
    net.settle(gots[1].at[1:], sem)
    rows[2] = jnp.sum(gots[1][...], axis=0)
    yield


def mono_kernel(samples, space, *refs):
    vol_hbm, tile_hbm, w3_hbm, w4_hbm, b3_hbm, b4_hbm = refs[:6]
    out, *outs4, out3, bsum = refs[6:11]
    refs = list(refs[11:])
    w3, w4, fwd3, fwd4, back3, back4 = refs[:6]
    pre, pooled, ext3, grad4, ext4, grad3, wide4, wide3 = refs[6:14]
    halos = refs[14:22]
    near = refs[-4:]
    other_tile, rows = refs[22:24]
    gots = refs[24:26]
    parts4 = refs[26:32], refs[32:38]
    part3 = refs[38:41]
    cells, low_cells, high_cells, plane, bias3, bias4 = refs[41:47]
    send, recv, vol, tile, b3, b4, part, part_fwd, here = refs[47:-4]
    loads = [
        pltpu.make_async_copy(w3_hbm, w3, here.at[0]),
        pltpu.make_async_copy(vol_hbm, vol, here.at[2]),
        pltpu.make_async_copy(b3_hbm, b3, here.at[4]),
        pltpu.make_async_copy(b4_hbm, b4, here.at[5]),
        pltpu.make_async_copy(w4_hbm, w4, here.at[1]),
        pltpu.make_async_copy(tile_hbm, tile, here.at[3]),
    ]
    for load in loads:
        load.start()
    net = Net(samples, space, send, recv)
    net.greet()
    depth = vol.shape[0]
    fours = [Reduce(net, p[0], o, *p[1:]) for p, o in zip(parts4, outs4)]
    three = Gather(net, part3[0], out3, *part3[1:])
    net.met()
    done = net.halo(vol_hbm.at[0], vol_hbm.at[depth - 1], halos[0], halos[1])
    tile_copy = net.move(tile_hbm, other_tile, net.other)
    loads[0].wait()
    place_forward(w3, fwd3, 96)
    loads[2].wait()
    loads[3].wait()
    for bias, narrow in ((bias3, b3), (bias4, b4)):
        width = narrow.shape[1]
        for c in range(bias.shape[1] // width):
            bias[:, c * width : (c + 1) * width] = narrow[...]
    loads[1].wait()
    for d in range(depth):
        spread(vol.at[d], cells.at[d])
    first_own(cells, fwd3, pre, ext3)
    done()
    spread(halos[0], low_cells.at[0])
    spread(halos[1], high_cells.at[0])
    first_kernel(low_cells, high_cells, fwd3, bias3, pre, pooled, ext3)
    done = net.halo(pooled, pooled, halos[2], halos[3])
    fill(ext4, pooled[...], 1, 64, 64)
    loads[4].wait()
    place_forward(w4, fwd4, 64)
    second_own(fwd4, bias4, part_fwd, ext4)
    place_back(w4, back4, 128, (1, 2, 0))
    loads[5].wait()
    tile_copy.wait()
    odd = net.core == 1
    mine, theirs = tile[...].astype(F32), other_tile[...].astype(F32)
    spread(jnp.where(odd, theirs, mine), plane.at[: tile.shape[0]])
    spread(jnp.where(odd, mine, theirs), plane.at[tile.shape[0] :])
    rows[...] = jnp.zeros(rows.shape, F32)
    for each in (*fours, three):
        each.buf[...] = jnp.zeros(each.buf.shape, BF16)
    slopes(pre)
    done()
    second_kernel(halos[2], halos[3], fwd4, part_fwd, plane, grad4, rows.at[0], ext4)
    third_near(grad4, back4, near[0], near[1], wide4)
    done = net.halo(near[0], near[1], halos[4], halos[5])
    for four, taps in zip(fours, HALVES):
        wgrad_four(ext4, grad4, four.buf, taps)
        four.pair()
    part[...] = nt(third_window(wide4), back4[2 * LANES :])
    fours[0].samples()
    place_back(w3, back3, 64)
    fours[1].samples()
    done()
    third_kernel(halos[4], halos[5], part, pre, grad3, rows.at[0])
    bias_steps = share(net, rows, gots)
    next(bias_steps)
    wgrad_three(ext3, grad3, three.buf, range(9))
    three.scatter()
    fours[0].chips()
    fourth_near(grad3, back3, near[2], near[3], wide3)
    fours[1].chips()
    done = net.halo(near[2], near[3], halos[6], halos[7])
    next(bias_steps)
    fourth_part(back3, cells, wide3, 0)
    fourth_part(back3, cells, wide3, 1)
    fours[0].back_chips()
    three.along()
    done()
    fours[1].back_chips()
    for d, side in ((0, halos[6]), (depth - 1, halos[7])):
        cells[d] = cells[d] + side[0].astype(F32)
    for d in range(depth):
        for g in range(cells.shape[2]):
            out[d, :, g * LANES : (g + 1) * LANES] = cells[d, :, g, :].astype(BF16)
    fours[0].back_samples()
    fours[1].back_samples()
    three.back()
    next(bias_steps)
    bsum[...] = rows[2]
    fours[0].back_pair()
    fours[1].back_pair()
    for each in (*fours, three):
        each.end()


def finish_kernel(grad, out4a, out4b, out3, bsum, *refs):
    volume, to3, to4, bsum3, bsum4, wsum3, wsum4, sems = refs
    copies = []

    def send(src, dst):
        copies.append(pltpu.make_async_copy(src, dst, sems.at[len(copies)]))
        copies[-1].start()

    send(grad, volume)
    for out4, taps in zip((out4a, out4b), HALVES):
        for place, tap in enumerate(taps):
            for dx in range(3):
                for k in range(4):
                    rows = kept(out4, (place * 3 + dx) * 4 + k)
                    wsum4[tap * 3 + dx, k * 16 : k * 16 + 16] = rows.astype(F32)
        span = pl.ds(taps[0] * 3, len(taps) * 3)
        send(wsum4.at[span], to4.at[span])
    for t in range(27):
        value = kept(out3, t).astype(F32)
        wsum3[t, :16] = value[:, :64]
        wsum3[t, 16:] = pltpu.roll(value, 64, 1)[:, :64]
    send(wsum3, to3)
    bsum4[...] = bsum[0:1]
    bsum3[...] = bsum[1:2, : bsum3.shape[1]]
    for copy in copies:
        copy.wait()


def per_of(samples, chips, rows):
    per = 16
    while per * 2 * samples * chips < rows:
        per *= 2
    return per


def parts(samples, chips, rows):
    per = per_of(samples, chips, rows)
    return [
        pltpu.VMEM((2, samples, chips, per, LANES), BF16),
        pltpu.VMEM((samples, chips, per, LANES), BF16),
        pltpu.VMEM((samples, chips, per, LANES), BF16),
        pltpu.VMEM((max(samples - 1, 1), chips, per, LANES), BF16),
        pltpu.VMEM((chips, per, LANES), BF16),
        pltpu.VMEM((max(chips - 1, 1), per, LANES), BF16),
    ]


def pieces(samples, chips, rows):
    per = per_of(samples, 1, rows)
    return [
        pltpu.VMEM((2, samples, 1, per, LANES), BF16),
        pltpu.VMEM((2 * samples - 1, 1, per, LANES), BF16),
        pltpu.VMEM((chips, 1, per, LANES), BF16),
    ]


def local(volume, weight_three, bias_three, weight_four, bias_four, cotangent):
    cin, mid = weight_three.shape[3:]
    cout = weight_four.shape[4]
    depth, height = volume.shape[1:3]
    groups = volume.shape[3] // LANES
    samples, space = lax.axis_size("sample"), lax.axis_size("space")
    tile = cotangent[0]
    w3 = weight_three.reshape(27, cin, mid)
    w4 = weight_four.reshape(27, mid, cout)
    wide = 2 * LANES
    half = height // 2
    shape = jax.ShapeDtypeStruct
    vm = pltpu.VMEM
    copies = copies_of(samples)
    vmem = pl.BlockSpec(memory_space=pltpu.VMEM)
    far = pl.BlockSpec(memory_space=pltpu.HBM)
    counts = [3 * len(taps) * mid for taps in HALVES]
    packed = [
        shape((2, samples, chips, per_of(samples, chips, n), LANES), BF16)
        for chips, n in (*[(space // 2, n) for n in counts], (1, 27 * cin // 2))
    ]
    raw = shape(volume.shape[1:], BF16)
    results = pl.pallas_call(
        functools.partial(mono_kernel, samples, space),
        out_shape=[raw, *packed, shape((8, LANES), F32)],
        in_specs=[far] * 6,
        out_specs=[vmem] * 5,
        scratch_shapes=[
            vm(w3.shape, BF16),
            vm(w4.shape, BF16),
            vm((9 * wide, wide), BF16),
            vm((9 * wide, wide), BF16),
            vm((LANES, 9 * 3 * LANES), BF16),
            vm((3 * LANES, 3 * 4 * LANES), BF16),
            vm((depth, height, groups, wide), F32),
            vm((half, groups, LANES), BF16),
            vm((depth + 2, height + 2, groups, wide), BF16),
            vm((half, groups, wide), BF16),
            vm((3, half + 2, groups, wide), BF16),
            vm((depth, height, groups, wide), BF16),
            vm((1, half + 2, groups, 4 * LANES), BF16),
            vm((depth, height + 2, groups, 3 * LANES), BF16),
            *[vm(volume.shape[2:], BF16)] * 2,
            *[vm((half, groups, LANES), BF16)] * 2,
            *[vm((half, groups, LANES), BF16)] * 2,
            *[vm((1, height, groups, LANES), BF16)] * 2,
            vm(tile.shape, BF16),
            vm((3, 8, LANES), F32),
            vm((2 * samples, 8, LANES), F32),
            vm((space // 2, 8, LANES), F32),
            *parts(samples, space // 2, counts[0]),
            *parts(samples, space // 2, counts[1]),
            *pieces(samples, space // 2, 27 * cin // 2),
            vm((depth, height, groups, LANES), F32),
            *[vm((1, height, groups, LANES), F32)] * 2,
            vm((2 * tile.shape[0], groups, LANES), F32),
            vm((1, wide), F32),
            vm((1, wide), F32),
            pltpu.SemaphoreType.DMA((copies,)),
            pltpu.SemaphoreType.DMA((copies,)),
            vm(volume.shape[1:], BF16),
            vm(tile.shape, BF16),
            vm((1, mid), F32),
            vm((1, cout), F32),
            vm((half * groups, LANES), F32),
            vm((half * groups, wide), F32),
            pltpu.SemaphoreType.DMA((6,)),
            *[vm((half, groups, LANES), BF16)] * 2,
            *[vm((1, height, groups, LANES), BF16)] * 2,
        ],
        compiler_params=pltpu.CompilerParams(
            collective_id=0, has_side_effects=True, vmem_limit_bytes=36 * 2**20
        ),
    )(
        *[
            pltpu.with_memory_space_constraint(a, pltpu.HBM)
            for a in (volume[0], tile, w3, w4, bias_three[None], bias_four[None])
        ]
    )
    grad_field, wsum_three, wsum_four, bsum_three, bsum_four = pl.pallas_call(
        finish_kernel,
        out_shape=[
            raw,
            shape((27, cin, mid), F32),
            shape((27, mid, cout), F32),
            shape((1, mid), F32),
            shape((1, cout), F32),
        ],
        in_specs=[vmem] * 5,
        out_specs=[far] * 3 + [vmem] * 2,
        scratch_shapes=[
            vm((27, cin, mid), F32),
            vm((27, mid, cout), F32),
            pltpu.SemaphoreType.DMA((4,)),
        ],
        compiler_params=pltpu.CompilerParams(vmem_limit_bytes=16 * 2**20),
    )(*results)
    return (
        grad_field.reshape(volume.shape),
        wsum_three.reshape(weight_three.shape),
        bsum_three[0],
        wsum_four.reshape(weight_four.shape),
        bsum_four[0],
    )


def solution(mesh):
    placed = (P("sample", "space", None, None), P(), P(), P(), P(), P("sample", "space", None))
    return jax.shard_map(
        local,
        mesh=mesh,
        in_specs=placed,
        out_specs=(P("sample", "space", None, None), P(), P(), P(), P()),
        check_vma=False,
    )
```

```python
import functools

import jax
import jax.numpy as jnp
from jax import lax
from jax.experimental import pallas as pl
from jax.experimental.pallas import tpu as pltpu
from jax.sharding import PartitionSpec as P

F32 = jnp.float32
BF16 = jnp.bfloat16
MESH = pl.DeviceIdType.MESH
LANES = 128
HALVES = (range(0, 5), range(5, 9))


def slot_of(cell, cells, chans, main, low_side):
    if cell < 0:
        return main + low_side
    if cell == cells:
        return main
    return cell * chans


def place_forward(wide, fwd, low_in):
    cin, cout = wide.shape[1], wide.shape[2]
    fwd[...] = jnp.zeros(fwd.shape, fwd.dtype)
    for tap in range(9):
        for dx in range(3):
            for c in range(LANES // cin):
                row = tap * 2 * LANES + slot_of(c + dx - 1, LANES // cin, cin, LANES, low_in)
                fwd[row : row + cin, c * cout : (c + 1) * cout] = wide[tap * 3 + dx]


def place_back(wide, back, low_out, blocks=(0, 0, 0)):
    cin, cout = wide.shape[1], wide.shape[2]
    per = 3 if max(blocks) else 9
    unit = back.shape[1] // per
    back[...] = jnp.zeros(back.shape, back.dtype)
    for tap in range(9):
        for dx in range(3):
            for c in range(LANES // cin):
                row = blocks[tap // 3] * LANES + c * cin
                col = tap % per * unit
                col += slot_of(c - dx + 1, LANES // cin, cout, 2 * LANES, low_out)
                back[row : row + cin, col : col + cout] = wide[(8 - tap) * 3 + dx]


def spread(raw, dst):
    for g in range(dst.shape[1]):
        dst[:, g, :] = raw[:, g * LANES : (g + 1) * LANES].astype(F32)


def neighbours(low, high, groups):
    rows = low.shape[0]
    place = lax.broadcasted_iota(jnp.int32, low.shape, 0) % groups
    right = jnp.where(place == groups - 1, 0.0, pltpu.roll(low, rows - 1, 0))
    left = jnp.where(place == 0, 0.0, pltpu.roll(high, 1, 0))
    return right, left


def widen(plane, first, last):
    h, g, lanes = plane.shape
    flat = plane.astype(F32).reshape(h * g, lanes)
    right, left = neighbours(flat[:, :LANES], flat[:, lanes - LANES :], g)
    if first == LANES:
        side = jnp.concatenate([right, left], axis=1)
    else:
        lane = lax.broadcasted_iota(jnp.int32, right.shape, 1)
        side = jnp.where(lane < first, right, jnp.where(lane >= last, left, 0.0))
    return jnp.concatenate([plane.astype(BF16), side.astype(BF16).reshape(h, g, -1)], axis=2)


def fill(ext, plane, e, first, last):
    height = ext.shape[1] - 2
    edge = jnp.zeros(ext.shape[2:], ext.dtype)
    ext[e, 0] = edge
    ext[e, height + 1] = edge
    ext[e, 1 : height + 1] = widen(plane, first, last)


def window(ext, d, h0, rows, steps=(0, 1, 2)):
    parts = [
        ext[d + dz, pl.ds(h0 + dy, rows)].reshape(-1, ext.shape[3])
        for dz in steps
        for dy in range(3)
    ]
    return jnp.concatenate(parts, axis=1)


def of_steps(steps, unit):
    return pl.ds(steps[0] * 3 * unit, len(steps) * 3 * unit)


def split_steps(d, depth):
    own = [dz for dz in range(3) if 1 <= d + dz <= depth]
    return own, [dz for dz in range(3) if dz not in own]


def nt(a, b):
    return lax.dot_general(a, b, (((1,), (1,)), ((), ())), preferred_element_type=F32)


def slope(v):
    s = jax.nn.sigmoid(v)
    return s * (1.0 + v * (1.0 - s))


def first_own(vol, w, pre, ext):
    depth, height, g, _ = vol.shape
    for d in range(depth):
        fill(ext, vol[d], d + 1, 32, 96)
    step = 8

    @pl.loop(0, height // step)
    def _(block):
        h0 = block * step
        for d in range(depth):
            own, _ = split_steps(d, depth)
            left = window(ext, d, h0, step, own)
            value = jnp.dot(left, w[of_steps(own, ext.shape[3])], preferred_element_type=F32)
            pre[d, pl.ds(h0, step)] = value.reshape(step, g, -1)


def first_kernel(low, high, w, bias, pre, pooled, ext):
    depth, height, g, _ = pre.shape
    fill(ext, low[0], 0, 32, 96)
    fill(ext, high[0], depth + 1, 32, 96)
    step = 8

    @pl.loop(0, height // step)
    def _(block):
        h0 = block * step
        total = 0.0
        for d in range(depth):
            value = pre[d, pl.ds(h0, step)].reshape(step * g, -1) + bias[...]
            _, rest = split_steps(d, depth)
            for dz in rest:
                left = window(ext, d, h0, step, [dz])
                value = value + jnp.dot(
                    left, w[of_steps([dz], ext.shape[3])], preferred_element_type=F32
                )
            pre[d, pl.ds(h0, step)] = value.reshape(step, g, -1)
            total = total + value * jax.nn.sigmoid(value)
        total = jnp.sum(total.reshape(step // 2, 2, g, -1), axis=1).reshape(step // 2 * g, -1)
        a, b = total[:, :LANES], total[:, LANES:]
        lane = lax.broadcasted_iota(jnp.int32, a.shape, 1)
        half = LANES // 2
        mean = jnp.where(lane < half, a + pltpu.roll(a, half, 1), b + pltpu.roll(b, half, 1))
        pooled[pl.ds(block * (step // 2), step // 2)] = (
            (mean * 0.125).astype(BF16).reshape(step // 2, g, LANES)
        )


def slopes(pre):
    @pl.loop(0, pre.shape[1] // 2)
    def _(block):
        for d in range(pre.shape[0]):
            here = pl.ds(block * 2, 2)
            pre[d, here] = slope(pre[d, here])


def second_own(w, bias, part, ext):
    height = ext.shape[1] - 2
    own = w[of_steps([1], ext.shape[3])]
    part[...] = jnp.dot(window(ext, 0, 0, height, [1]), own, preferred_element_type=F32) + bias[...]


def second_kernel(low, high, w, part, cot, grad, bsum, ext):
    height, g, _ = low.shape
    fill(ext, low[...], 0, 64, 64)
    fill(ext, high[...], 2, 64, 64)
    pre = part[...]
    for dz in (0, 2):
        rest = w[of_steps([dz], ext.shape[3])]
        pre = pre + jnp.dot(window(ext, 0, 0, height, [dz]), rest, preferred_element_type=F32)
    up = cot[...]
    up = jnp.broadcast_to(up[:, None], (height // 2, 2, g, LANES)).reshape(height * g, LANES)
    up = jnp.concatenate([up, up], axis=1) * 0.125
    value = (up * slope(pre)).astype(BF16)
    grad[...] = value.reshape(grad.shape)
    total = jnp.sum(value.astype(F32), axis=0, keepdims=True)
    bsum[0:1] = total[:, :LANES] + total[:, LANES:]


def tn(a, b):
    return lax.dot_general(a, b, (((0,), (0,)), ((), ())), preferred_element_type=F32)


def keep(buf, piece, rows):
    _, samples, chips, per, _ = buf.shape
    for k in range(rows.shape[0] // 16):
        first = (piece + k) * 16
        chunk, row = first // per, first % per
        core, rest = divmod(chunk, samples * chips)
        buf[core, rest // chips, rest % chips, row : row + 16] = rows[k * 16 : k * 16 + 16]


def kept(buf, piece):
    _, samples, chips, per, _ = buf.shape
    chunk, row = piece * 16 // per, piece * 16 % per
    core, rest = divmod(chunk, samples * chips)
    return buf[core, rest // chips, rest % chips, row : row + 16]


def wgrad_four(ext, grad, buf, taps):
    height = grad.shape[0]
    up = grad[...].reshape(-1, 2 * LANES)
    for place, tap in enumerate(taps):
        part = tn(ext[tap // 3, tap % 3 : tap % 3 + height].reshape(-1, 2 * LANES), up)
        for dx in range(3):
            total = 0.0
            for c in range(2):
                row = slot_of(c + dx - 1, 2, 64, LANES, 64)
                total = total + part[row : row + 64, c * LANES : (c + 1) * LANES]
            keep(buf, (place * 3 + dx) * 4, total.astype(BF16))


def wgrad_three(ext, grad, buf, taps):
    depth, height = grad.shape[:2]
    for tap in taps:
        part = 0.0
        for d in range(depth):
            part = part + tn(
                ext[tap // 3 + d, tap % 3 : tap % 3 + height].reshape(-1, 2 * LANES),
                grad[d].reshape(-1, 2 * LANES),
            )
        for dx in range(3):
            even, odd = 0.0, 0.0
            for c in range(4):
                row = slot_of(c + dx - 1, 4, 32, LANES, 96)
                piece = part[row : row + 32, c // 2 * LANES : (c // 2 + 1) * LANES]
                if c % 2:
                    odd = odd + piece
                else:
                    even = even + piece
            total = even + pltpu.roll(odd, 64, 1)
            lane = lax.broadcasted_iota(jnp.int32, (16, LANES), 1)
            packed = jnp.where(lane < 64, total[:16], pltpu.roll(total[16:], 64, 1))
            keep(buf, tap * 3 + dx, packed.astype(BF16))


def third_near(grad, w, first, last, ext):
    fill(ext, grad[...], 0, LANES, LANES)
    value = nt(third_window(ext), w[: 2 * LANES]).astype(BF16)
    first[...] = value[:, :LANES].reshape(first.shape)
    last[...] = value[:, LANES:].reshape(last.shape)


def third_window(ext):
    return window(ext, 0, 0, ext.shape[1] - 2, [0])


def third_kernel(low, high, part, pre, out, bsum):
    height, g, _ = low.shape
    back = part[...]
    for side in (low, high):
        back = back + side[...].astype(F32).reshape(back.shape)
    back = back * 0.125
    turned = pltpu.roll(back, 64, 1)
    lane = lax.broadcasted_iota(jnp.int32, back.shape, 1)
    up = jnp.concatenate(
        [jnp.where(lane < 64, back, turned), jnp.where(lane < 64, turned, back)], axis=1
    ).reshape(height, g, 2 * LANES)
    total = 0.0
    for d in range(pre.shape[0]):
        for h in range(height):
            value = (up[h][None] * pre[d, 2 * h : 2 * h + 2]).astype(BF16)
            out[d, 2 * h : 2 * h + 2] = value
            total = total + jnp.sum(value.astype(F32), axis=0)
    total = jnp.sum(total, axis=0, keepdims=True)
    total = total[:, :LANES] + total[:, LANES:]
    bsum[1:2] = total + pltpu.roll(total, 64, 1)


def fourth_near(grad, w, first, last, ext):
    depth, height = grad.shape[:2]
    for d in range(depth):
        fill(ext, grad[d], d, 64, 64)
    step = height // 2

    @pl.loop(0, 2)
    def _(block):
        h0 = block * step
        for d, dz, side in ((0, 2, first), (depth - 1, 0, last)):
            left = window(ext, d - dz, h0, step, [dz])
            value = nt(left, w[:, of_steps([dz], ext.shape[3])])
            side[0, pl.ds(h0, step)] = value.astype(BF16).reshape(step, -1, LANES)


def fourth_part(w, out, ext, block):
    depth, height, g, _ = out.shape
    step = height // 2
    h0 = block * step
    for d in range(depth):
        own, _ = split_steps(d, depth)
        left = window(ext, d - 1, h0, step, own)
        value = nt(left, w[:, of_steps(own, ext.shape[3])])
        out[d, pl.ds(h0, step)] = value.reshape(step, g, LANES)


class Reduce:
    def __init__(self, net, buf, out, got_a, acc, got_b, mid, got_c):
        self.net = net
        self.buf, self.out = buf, out
        self.got_a, self.acc, self.got_b, self.mid, self.got_c = got_a, acc, got_b, mid, got_c

    def pair(self):
        n = self.net
        self.copy = n.move(self.buf.at[1 - n.core], self.got_a, n.other)

    def samples(self):
        n = self.net
        self.copy.wait()
        self.acc[...] = (self.buf[n.core].astype(F32) + self.got_a[...].astype(F32)).astype(BF16)
        self.sem = n.ticket()
        for j, to in enumerate(n.peers):
            n.move(self.acc.at[to[0]], self.got_b.at[j], to, self.sem)

    def chips(self):
        n = self.net
        n.settle(self.got_b, self.sem)
        total = self.acc[n.s].astype(F32)
        for j in range(len(n.peers)):
            total = total + self.got_b[j].astype(F32)
        self.mid[...] = total.astype(BF16)
        self.sem = n.ticket()
        for j, (chip, to) in enumerate(n.line):
            n.move(self.mid.at[chip], self.got_c.at[j], to, self.sem)

    def back_chips(self):
        n = self.net
        n.settle(self.got_c, self.sem)
        total = self.mid[n.chip].astype(F32)
        for j in range(len(n.line)):
            total = total + self.got_c[j].astype(F32)
        here = self.out.at[n.core, n.s, n.chip]
        here[...] = total.astype(BF16)
        self.sem = n.ticket()
        for _, to in n.line:
            n.move(here, here, to, self.sem)
        self.wide = [n.ticket() for _ in n.peers]
        for k, to in enumerate(n.peers):
            n.move(here, here, to, self.wide[k])

    def back_samples(self):
        n = self.net
        chips = len(n.line) + 1
        n.settle(self.got_c, self.sem)
        for j in range(chips - 1):
            here = self.out.at[n.core, n.s, lax.rem(n.chip + chips - 1 - j, chips)]
            for k, to in enumerate(n.peers):
                n.move(here, here, to, self.wide[k])

    def back_pair(self):
        n = self.net
        samples = len(n.peers) + 1
        self.sem = n.ticket()
        here = self.out.at[n.core, n.s]
        n.move(here, here, n.other, self.sem)
        for k, sem in enumerate(self.wide):
            here = self.out.at[n.core, lax.rem(n.s + samples - 1 - k, samples)]
            n.settle(here, sem)
            n.move(here, here, n.other, self.sem)

    def end(self):
        self.net.settle(self.out.at[1 - self.net.core], self.sem)


class Gather:
    def __init__(self, net, buf, out, got_a, field):
        self.net = net
        self.buf, self.out, self.got_a, self.field = buf, out, got_a, field

    def scatter(self):
        n = self.net
        self.sem = n.ticket()
        for j, (core, s, to) in enumerate(n.plane):
            n.move(self.buf.at[core, s], self.got_a.at[j], to, self.sem)

    def along(self):
        n = self.net
        n.settle(self.got_a, self.sem)
        total = self.buf[n.core, n.s].astype(F32)
        for j in range(len(n.plane)):
            total = total + self.got_a[j].astype(F32)
        here = self.field.at[n.chip]
        here[...] = total.astype(BF16)
        self.sem = n.ticket()
        for _, to in n.line:
            n.move(here, here, to, self.sem)

    def back(self):
        n = self.net
        n.settle(self.field.at[1:], self.sem)
        here = self.out.at[n.core, n.s]
        here[...] = jnp.sum(self.field[...].astype(F32), axis=0).astype(BF16)
        self.sem = n.ticket()
        for _, _, to in n.plane:
            n.move(here, here, to, self.sem)

    def end(self):
        self.net.settle(self.got_a, self.sem)


class Net:
    def __init__(self, samples, space, send, recv):
        self.count = 0
        self.send, self.recv = send, recv
        self.space = space
        self.s = lax.axis_index("sample")
        self.p = lax.axis_index("space")
        self.core = lax.rem(self.p, 2)
        self.chip = lax.div(self.p, 2)
        self.other = (self.s, self.chip * 2 + 1 - self.core)
        self.peers = [(lax.rem(self.s + j, samples), self.p) for j in range(1, samples)]
        self.plane = []
        for j in range(samples - 1, -1, -1):
            for k in (1, 0):
                if j or k:
                    s, core = lax.rem(self.s + j, samples), lax.rem(self.core + k, 2)
                    self.plane.append((core, s, (s, self.chip * 2 + core)))
        self.line = []
        for j in range(1, space // 2):
            to = lax.rem(self.chip + j, space // 2)
            self.line.append((to, (self.s, to * 2 + self.core)))
        self.has_low = self.p > 0
        self.has_high = self.p < space - 1
        self.above = (self.s, lax.rem(self.p + 1, space))
        self.below = (self.s, lax.rem(self.p + space - 1, space))

    def greet(self):
        barrier = pltpu.get_barrier_semaphore()

        def signal(to):
            pl.semaphore_signal(barrier, inc=1, device_id=to, device_id_type=MESH)

        for to in [self.above, self.below]:
            signal(to)
        for _, _, to in self.plane:
            signal(to)
        for _, to in self.line:
            signal(to)

    def met(self):
        barrier = pltpu.get_barrier_semaphore()
        pl.semaphore_wait(barrier, 2 + len(self.plane) + len(self.line))

    def ticket(self):
        self.count += 1
        return self.count - 1

    def make(self, src, dst, to, sem=None):
        sem = self.ticket() if sem is None else sem
        return pltpu.make_async_remote_copy(
            src_ref=src,
            dst_ref=dst,
            send_sem=self.send.at[sem],
            recv_sem=self.recv.at[sem],
            device_id=to,
            device_id_type=MESH,
        )

    def move(self, src, dst, to, sem=None):
        copy = self.make(src, dst, to, sem)
        copy.start()
        return copy

    def settle(self, ref, sem):
        for of in (self.send, self.recv):
            pltpu.make_async_copy(ref, ref, of.at[sem]).wait()

    def halo(self, first, last, low, high):
        up = self.make(last, low, self.above)
        down = self.make(first, high, self.below)

        @pl.when(self.has_high)
        def _():
            up.start()

        @pl.when(self.has_low)
        def _():
            down.start()

        @pl.when(self.p == 0)
        def _():
            low[...] = jnp.zeros(low.shape, low.dtype)

        @pl.when(self.p == self.space - 1)
        def _():
            high[...] = jnp.zeros(high.shape, high.dtype)

        def finish():
            @pl.when(self.has_high)
            def _():
                up.wait_send()
                down.wait_recv()

            @pl.when(self.has_low)
            def _():
                down.wait_send()
                up.wait_recv()

        return finish


def copies_of(samples):
    return 4 * 2 + 1 + 2 * (5 + samples - 1) + 3 + 2


def share(net, rows, gots):
    def group(src, got, mine, targets):
        sem = net.ticket()
        for to in targets:
            net.move(src, got.at[mine], to, sem)
        got[mine] = src[...]
        return sem

    samples = gots[0].shape[0] // 2
    mine = net.core * samples + net.s
    sem = group(rows.at[0], gots[0], mine, [to for _, _, to in net.plane])
    yield
    net.settle(gots[0].at[1:], sem)
    rows[1] = jnp.sum(gots[0][...], axis=0)
    sem = group(rows.at[1], gots[1], net.chip, [to for _, to in net.line])
    yield
    net.settle(gots[1].at[1:], sem)
    rows[2] = jnp.sum(gots[1][...], axis=0)
    yield


def mono_kernel(samples, space, *refs):
    vol_hbm, tile_hbm, w3_hbm, w4_hbm, b3_hbm, b4_hbm = refs[:6]
    out, *outs4, out3, bsum = refs[6:11]
    refs = list(refs[11:])
    w3, w4, fwd3, fwd4, back3, back4 = refs[:6]
    pre, pooled, ext3, grad4, ext4, grad3, wide4, wide3 = refs[6:14]
    halos = refs[14:22]
    near = refs[-4:]
    other_tile, rows = refs[22:24]
    gots = refs[24:26]
    parts4 = refs[26:32], refs[32:38]
    part3 = refs[38:41]
    cells, low_cells, high_cells, plane, bias3, bias4 = refs[41:47]
    send, recv, vol, tile, b3, b4, part, part_fwd, here = refs[47:-4]
    loads = [
        pltpu.make_async_copy(w3_hbm, w3, here.at[0]),
        pltpu.make_async_copy(vol_hbm, vol, here.at[2]),
        pltpu.make_async_copy(b3_hbm, b3, here.at[4]),
        pltpu.make_async_copy(b4_hbm, b4, here.at[5]),
        pltpu.make_async_copy(w4_hbm, w4, here.at[1]),
        pltpu.make_async_copy(tile_hbm, tile, here.at[3]),
    ]
    for load in loads:
        load.start()
    net = Net(samples, space, send, recv)
    net.greet()
    depth = vol.shape[0]
    fours = [Reduce(net, p[0], o, *p[1:]) for p, o in zip(parts4, outs4)]
    three = Gather(net, part3[0], out3, *part3[1:])
    net.met()
    done = net.halo(vol_hbm.at[0], vol_hbm.at[depth - 1], halos[0], halos[1])
    tile_copy = net.move(tile_hbm, other_tile, net.other)
    loads[0].wait()
    place_forward(w3, fwd3, 96)
    loads[2].wait()
    loads[3].wait()
    for bias, narrow in ((bias3, b3), (bias4, b4)):
        width = narrow.shape[1]
        for c in range(bias.shape[1] // width):
            bias[:, c * width : (c + 1) * width] = narrow[...]
    loads[1].wait()
    for d in range(depth):
        spread(vol.at[d], cells.at[d])
    first_own(cells, fwd3, pre, ext3)
    done()
    spread(halos[0], low_cells.at[0])
    spread(halos[1], high_cells.at[0])
    first_kernel(low_cells, high_cells, fwd3, bias3, pre, pooled, ext3)
    done = net.halo(pooled, pooled, halos[2], halos[3])
    fill(ext4, pooled[...], 1, 64, 64)
    loads[4].wait()
    place_forward(w4, fwd4, 64)
    second_own(fwd4, bias4, part_fwd, ext4)
    place_back(w4, back4, 128, (1, 2, 0))
    loads[5].wait()
    tile_copy.wait()
    odd = net.core == 1
    mine, theirs = tile[...].astype(F32), other_tile[...].astype(F32)
    spread(jnp.where(odd, theirs, mine), plane.at[: tile.shape[0]])
    spread(jnp.where(odd, mine, theirs), plane.at[tile.shape[0] :])
    rows[...] = jnp.zeros(rows.shape, F32)
    for each in (*fours, three):
        each.buf[...] = jnp.zeros(each.buf.shape, BF16)
    slopes(pre)
    done()
    second_kernel(halos[2], halos[3], fwd4, part_fwd, plane, grad4, rows.at[0], ext4)
    third_near(grad4, back4, near[0], near[1], wide4)
    done = net.halo(near[0], near[1], halos[4], halos[5])
    for four, taps in zip(fours, HALVES):
        wgrad_four(ext4, grad4, four.buf, taps)
        four.pair()
    part[...] = nt(third_window(wide4), back4[2 * LANES :])
    fours[0].samples()
    place_back(w3, back3, 64)
    fours[1].samples()
    done()
    third_kernel(halos[4], halos[5], part, pre, grad3, rows.at[0])
    bias_steps = share(net, rows, gots)
    next(bias_steps)
    for dz in range(3):

        @pl.when(net.p >= 0)
        def _(taps=range(dz * 3, dz * 3 + 3)):
            wgrad_three(ext3, grad3, three.buf, taps)

    three.scatter()
    fours[0].chips()
    fours[1].chips()
    next(bias_steps)
    fourth_near(grad3, back3, near[2], near[3], wide3)
    fourth_part(back3, cells, wide3, 0)
    fourth_part(back3, cells, wide3, 1)
    fours[0].back_chips()
    three.along()
    fours[1].back_chips()
    done = net.halo(near[2], near[3], halos[6], halos[7])
    fours[0].back_samples()
    fours[1].back_samples()
    three.back()
    next(bias_steps)
    bsum[...] = rows[2]
    done()
    for d, side in ((0, halos[6]), (depth - 1, halos[7])):
        cells[d] = cells[d] + side[0].astype(F32)
    for d in range(depth):
        for g in range(cells.shape[2]):
            out[d, :, g * LANES : (g + 1) * LANES] = cells[d, :, g, :].astype(BF16)
    fours[0].back_pair()
    fours[1].back_pair()
    for each in (*fours, three):
        each.end()


def finish_kernel(grad, out4a, out4b, out3, bsum, volume, wsum3, wsum4, bsum3, bsum4):
    volume[...] = grad[...]
    for out4, taps in zip((out4a, out4b), HALVES):
        for place, tap in enumerate(taps):
            for dx in range(3):
                for k in range(4):
                    rows = kept(out4, (place * 3 + dx) * 4 + k)
                    wsum4[tap * 3 + dx, k * 16 : k * 16 + 16] = rows.astype(F32)
    for t in range(27):
        value = kept(out3, t).astype(F32)
        wsum3[t, :16] = value[:, :64]
        wsum3[t, 16:] = pltpu.roll(value, 64, 1)[:, :64]
    bsum4[...] = bsum[0:1]
    bsum3[...] = bsum[1:2, : bsum3.shape[1]]


def per_of(samples, chips, rows):
    per = 16
    while per * 2 * samples * chips < rows:
        per *= 2
    return per


def parts(samples, chips, rows):
    per = per_of(samples, chips, rows)
    return [
        pltpu.VMEM((2, samples, chips, per, LANES), BF16),
        pltpu.VMEM((samples, chips, per, LANES), BF16),
        pltpu.VMEM((samples, chips, per, LANES), BF16),
        pltpu.VMEM((max(samples - 1, 1), chips, per, LANES), BF16),
        pltpu.VMEM((chips, per, LANES), BF16),
        pltpu.VMEM((max(chips - 1, 1), per, LANES), BF16),
    ]


def pieces(samples, chips, rows):
    per = per_of(samples, 1, rows)
    return [
        pltpu.VMEM((2, samples, 1, per, LANES), BF16),
        pltpu.VMEM((2 * samples - 1, 1, per, LANES), BF16),
        pltpu.VMEM((chips, 1, per, LANES), BF16),
    ]


def local(volume, weight_three, bias_three, weight_four, bias_four, cotangent):
    cin, mid = weight_three.shape[3:]
    cout = weight_four.shape[4]
    depth, height = volume.shape[1:3]
    groups = volume.shape[3] // LANES
    samples, space = lax.axis_size("sample"), lax.axis_size("space")
    tile = cotangent[0]
    w3 = weight_three.reshape(27, cin, mid)
    w4 = weight_four.reshape(27, mid, cout)
    wide = 2 * LANES
    half = height // 2
    shape = jax.ShapeDtypeStruct
    vm = pltpu.VMEM
    copies = copies_of(samples)
    vmem = pl.BlockSpec(memory_space=pltpu.VMEM)
    far = pl.BlockSpec(memory_space=pltpu.HBM)
    counts = [3 * len(taps) * mid for taps in HALVES]
    packed = [
        shape((2, samples, chips, per_of(samples, chips, n), LANES), BF16)
        for chips, n in (*[(space // 2, n) for n in counts], (1, 27 * cin // 2))
    ]
    raw = shape(volume.shape[1:], BF16)
    results = pl.pallas_call(
        functools.partial(mono_kernel, samples, space),
        out_shape=[raw, *packed, shape((8, LANES), F32)],
        in_specs=[far] * 6,
        out_specs=[vmem] * 5,
        scratch_shapes=[
            vm(w3.shape, BF16),
            vm(w4.shape, BF16),
            vm((9 * wide, wide), BF16),
            vm((9 * wide, wide), BF16),
            vm((LANES, 9 * 3 * LANES), BF16),
            vm((3 * LANES, 3 * 4 * LANES), BF16),
            vm((depth, height, groups, wide), F32),
            vm((half, groups, LANES), BF16),
            vm((depth + 2, height + 2, groups, wide), BF16),
            vm((half, groups, wide), BF16),
            vm((3, half + 2, groups, wide), BF16),
            vm((depth, height, groups, wide), BF16),
            vm((1, half + 2, groups, 4 * LANES), BF16),
            vm((depth, height + 2, groups, 3 * LANES), BF16),
            *[vm(volume.shape[2:], BF16)] * 2,
            *[vm((half, groups, LANES), BF16)] * 2,
            *[vm((half, groups, LANES), BF16)] * 2,
            *[vm((1, height, groups, LANES), BF16)] * 2,
            vm(tile.shape, BF16),
            vm((3, 8, LANES), F32),
            vm((2 * samples, 8, LANES), F32),
            vm((space // 2, 8, LANES), F32),
            *parts(samples, space // 2, counts[0]),
            *parts(samples, space // 2, counts[1]),
            *pieces(samples, space // 2, 27 * cin // 2),
            vm((depth, height, groups, LANES), F32),
            *[vm((1, height, groups, LANES), F32)] * 2,
            vm((2 * tile.shape[0], groups, LANES), F32),
            vm((1, wide), F32),
            vm((1, wide), F32),
            pltpu.SemaphoreType.DMA((copies,)),
            pltpu.SemaphoreType.DMA((copies,)),
            vm(volume.shape[1:], BF16),
            vm(tile.shape, BF16),
            vm((1, mid), F32),
            vm((1, cout), F32),
            vm((half * groups, LANES), F32),
            vm((half * groups, wide), F32),
            pltpu.SemaphoreType.DMA((6,)),
            *[vm((half, groups, LANES), BF16)] * 2,
            *[vm((1, height, groups, LANES), BF16)] * 2,
        ],
        compiler_params=pltpu.CompilerParams(
            collective_id=0, has_side_effects=True, vmem_limit_bytes=36 * 2**20
        ),
    )(
        *[
            pltpu.with_memory_space_constraint(a, pltpu.HBM)
            for a in (volume[0], tile, w3, w4, bias_three[None], bias_four[None])
        ]
    )
    grad_field, wsum_three, wsum_four, bsum_three, bsum_four = pl.pallas_call(
        finish_kernel,
        out_shape=[
            raw,
            shape((27, cin, mid), F32),
            shape((27, mid, cout), F32),
            shape((1, mid), F32),
            shape((1, cout), F32),
        ],
        in_specs=[vmem] * 5,
        out_specs=[vmem] * 5,
        compiler_params=pltpu.CompilerParams(vmem_limit_bytes=16 * 2**20),
    )(*results)
    return (
        grad_field.reshape(volume.shape),
        wsum_three.reshape(weight_three.shape),
        bsum_three[0],
        wsum_four.reshape(weight_four.shape),
        bsum_four[0],
    )


def solution(mesh):
    placed = (P("sample", "space", None, None), P(), P(), P(), P(), P("sample", "space", None))
    return jax.shard_map(
        local,
        mesh=mesh,
        in_specs=placed,
        out_specs=(P("sample", "space", None, None), P(), P(), P(), P()),
        check_vma=False,
    )
```

```python
import functools

import jax
import jax.numpy as jnp
from jax import lax
from jax.experimental import pallas as pl
from jax.experimental.pallas import tpu as pltpu
from jax.sharding import PartitionSpec as P

F32 = jnp.float32
BF16 = jnp.bfloat16
MESH = pl.DeviceIdType.MESH
LANES = 128
HALVES = (range(0, 5), range(5, 9))


def slot_of(cell, cells, chans, main, low_side):
    if cell < 0:
        return main + low_side
    if cell == cells:
        return main
    return cell * chans


def place_forward(wide, fwd, low_in):
    cin, cout = wide.shape[1], wide.shape[2]
    fwd[...] = jnp.zeros(fwd.shape, fwd.dtype)
    for tap in range(9):
        for dx in range(3):
            for c in range(LANES // cin):
                row = tap * 2 * LANES + slot_of(c + dx - 1, LANES // cin, cin, LANES, low_in)
                fwd[row : row + cin, c * cout : (c + 1) * cout] = wide[tap * 3 + dx]


def place_back(wide, back, low_out, blocks=(0, 0, 0)):
    cin, cout = wide.shape[1], wide.shape[2]
    per = 3 if max(blocks) else 9
    unit = back.shape[1] // per
    back[...] = jnp.zeros(back.shape, back.dtype)
    for tap in range(9):
        for dx in range(3):
            for c in range(LANES // cin):
                row = blocks[tap // 3] * LANES + c * cin
                col = tap % per * unit
                col += slot_of(c - dx + 1, LANES // cin, cout, 2 * LANES, low_out)
                back[row : row + cin, col : col + cout] = wide[(8 - tap) * 3 + dx]


def spread(raw, dst):
    for g in range(dst.shape[1]):
        dst[:, g, :] = raw[:, g * LANES : (g + 1) * LANES].astype(F32)


def neighbours(low, high, groups):
    rows = low.shape[0]
    place = lax.broadcasted_iota(jnp.int32, low.shape, 0) % groups
    right = jnp.where(place == groups - 1, 0.0, pltpu.roll(low, rows - 1, 0))
    left = jnp.where(place == 0, 0.0, pltpu.roll(high, 1, 0))
    return right, left


def widen(plane, first, last):
    h, g, lanes = plane.shape
    flat = plane.astype(F32).reshape(h * g, lanes)
    right, left = neighbours(flat[:, :LANES], flat[:, lanes - LANES :], g)
    if first == LANES:
        side = jnp.concatenate([right, left], axis=1)
    else:
        lane = lax.broadcasted_iota(jnp.int32, right.shape, 1)
        side = jnp.where(lane < first, right, jnp.where(lane >= last, left, 0.0))
    return jnp.concatenate([plane.astype(BF16), side.astype(BF16).reshape(h, g, -1)], axis=2)


def fill(ext, plane, e, first, last):
    height = ext.shape[1] - 2
    edge = jnp.zeros(ext.shape[2:], ext.dtype)
    ext[e, 0] = edge
    ext[e, height + 1] = edge
    ext[e, 1 : height + 1] = widen(plane, first, last)


def window(ext, d, h0, rows, steps=(0, 1, 2)):
    parts = [
        ext[d + dz, pl.ds(h0 + dy, rows)].reshape(-1, ext.shape[3])
        for dz in steps
        for dy in range(3)
    ]
    return jnp.concatenate(parts, axis=1)


def of_steps(steps, unit):
    return pl.ds(steps[0] * 3 * unit, len(steps) * 3 * unit)


def split_steps(d, depth):
    own = [dz for dz in range(3) if 1 <= d + dz <= depth]
    return own, [dz for dz in range(3) if dz not in own]


def nt(a, b):
    return lax.dot_general(a, b, (((1,), (1,)), ((), ())), preferred_element_type=F32)


def slope(v):
    s = jax.nn.sigmoid(v)
    return s * (1.0 + v * (1.0 - s))


def first_own(vol, w, pre, ext):
    depth, height, g, _ = vol.shape
    for d in range(depth):
        fill(ext, vol[d], d + 1, 32, 96)
    step = 8

    @pl.loop(0, height // step)
    def _(block):
        h0 = block * step
        for d in range(depth):
            own, _ = split_steps(d, depth)
            left = window(ext, d, h0, step, own)
            value = jnp.dot(left, w[of_steps(own, ext.shape[3])], preferred_element_type=F32)
            pre[d, pl.ds(h0, step)] = value.reshape(step, g, -1)


def first_kernel(low, high, w, bias, pre, pooled, ext):
    depth, height, g, _ = pre.shape
    fill(ext, low[0], 0, 32, 96)
    fill(ext, high[0], depth + 1, 32, 96)
    step = 8

    @pl.loop(0, height // step)
    def _(block):
        h0 = block * step
        total = 0.0
        for d in range(depth):
            value = pre[d, pl.ds(h0, step)].reshape(step * g, -1) + bias[...]
            _, rest = split_steps(d, depth)
            for dz in rest:
                left = window(ext, d, h0, step, [dz])
                value = value + jnp.dot(
                    left, w[of_steps([dz], ext.shape[3])], preferred_element_type=F32
                )
            pre[d, pl.ds(h0, step)] = value.reshape(step, g, -1)
            total = total + value * jax.nn.sigmoid(value)
        total = jnp.sum(total.reshape(step // 2, 2, g, -1), axis=1).reshape(step // 2 * g, -1)
        a, b = total[:, :LANES], total[:, LANES:]
        lane = lax.broadcasted_iota(jnp.int32, a.shape, 1)
        half = LANES // 2
        mean = jnp.where(lane < half, a + pltpu.roll(a, half, 1), b + pltpu.roll(b, half, 1))
        pooled[pl.ds(block * (step // 2), step // 2)] = (
            (mean * 0.125).astype(BF16).reshape(step // 2, g, LANES)
        )


def slopes(pre):
    @pl.loop(0, pre.shape[1] // 2)
    def _(block):
        for d in range(pre.shape[0]):
            here = pl.ds(block * 2, 2)
            pre[d, here] = slope(pre[d, here])


def second_own(w, bias, part, ext):
    height = ext.shape[1] - 2
    own = w[of_steps([1], ext.shape[3])]
    part[...] = jnp.dot(window(ext, 0, 0, height, [1]), own, preferred_element_type=F32) + bias[...]


def second_kernel(low, high, w, part, cot, grad, bsum, ext):
    height, g, _ = low.shape
    fill(ext, low[...], 0, 64, 64)
    fill(ext, high[...], 2, 64, 64)
    pre = part[...]
    for dz in (0, 2):
        rest = w[of_steps([dz], ext.shape[3])]
        pre = pre + jnp.dot(window(ext, 0, 0, height, [dz]), rest, preferred_element_type=F32)
    up = cot[...]
    up = jnp.broadcast_to(up[:, None], (height // 2, 2, g, LANES)).reshape(height * g, LANES)
    up = jnp.concatenate([up, up], axis=1) * 0.125
    value = (up * slope(pre)).astype(BF16)
    grad[...] = value.reshape(grad.shape)
    total = jnp.sum(value.astype(F32), axis=0, keepdims=True)
    bsum[0:1] = total[:, :LANES] + total[:, LANES:]


def tn(a, b):
    return lax.dot_general(a, b, (((0,), (0,)), ((), ())), preferred_element_type=F32)


def keep(buf, piece, rows):
    _, samples, chips, per, _ = buf.shape
    for k in range(rows.shape[0] // 16):
        first = (piece + k) * 16
        chunk, row = first // per, first % per
        core, rest = divmod(chunk, samples * chips)
        buf[core, rest // chips, rest % chips, row : row + 16] = rows[k * 16 : k * 16 + 16]


def kept(buf, piece):
    _, samples, chips, per, _ = buf.shape
    chunk, row = piece * 16 // per, piece * 16 % per
    core, rest = divmod(chunk, samples * chips)
    return buf[core, rest // chips, rest % chips, row : row + 16]


def wgrad_four(ext, grad, buf, taps):
    height = grad.shape[0]
    up = grad[...].reshape(-1, 2 * LANES)
    for place, tap in enumerate(taps):
        part = tn(ext[tap // 3, tap % 3 : tap % 3 + height].reshape(-1, 2 * LANES), up)
        for dx in range(3):
            total = 0.0
            for c in range(2):
                row = slot_of(c + dx - 1, 2, 64, LANES, 64)
                total = total + part[row : row + 64, c * LANES : (c + 1) * LANES]
            keep(buf, (place * 3 + dx) * 4, total.astype(BF16))


def wgrad_three(ext, grad, buf, taps):
    depth, height = grad.shape[:2]
    for tap in taps:
        part = 0.0
        for d in range(depth):
            part = part + tn(
                ext[tap // 3 + d, tap % 3 : tap % 3 + height].reshape(-1, 2 * LANES),
                grad[d].reshape(-1, 2 * LANES),
            )
        for dx in range(3):
            even, odd = 0.0, 0.0
            for c in range(4):
                row = slot_of(c + dx - 1, 4, 32, LANES, 96)
                piece = part[row : row + 32, c // 2 * LANES : (c // 2 + 1) * LANES]
                if c % 2:
                    odd = odd + piece
                else:
                    even = even + piece
            total = even + pltpu.roll(odd, 64, 1)
            lane = lax.broadcasted_iota(jnp.int32, (16, LANES), 1)
            packed = jnp.where(lane < 64, total[:16], pltpu.roll(total[16:], 64, 1))
            keep(buf, tap * 3 + dx, packed.astype(BF16))


def third_near(grad, w, first, last, ext):
    fill(ext, grad[...], 0, LANES, LANES)
    value = nt(third_window(ext), w[: 2 * LANES]).astype(BF16)
    first[...] = value[:, :LANES].reshape(first.shape)
    last[...] = value[:, LANES:].reshape(last.shape)


def third_window(ext):
    return window(ext, 0, 0, ext.shape[1] - 2, [0])


def third_kernel(low, high, part, pre, out, bsum):
    height, g, _ = low.shape
    back = part[...]
    for side in (low, high):
        back = back + side[...].astype(F32).reshape(back.shape)
    back = back * 0.125
    turned = pltpu.roll(back, 64, 1)
    lane = lax.broadcasted_iota(jnp.int32, back.shape, 1)
    up = jnp.concatenate(
        [jnp.where(lane < 64, back, turned), jnp.where(lane < 64, turned, back)], axis=1
    ).reshape(height, g, 2 * LANES)
    total = 0.0
    for d in range(pre.shape[0]):
        for h in range(height):
            value = (up[h][None] * pre[d, 2 * h : 2 * h + 2]).astype(BF16)
            out[d, 2 * h : 2 * h + 2] = value
            total = total + jnp.sum(value.astype(F32), axis=0)
    total = jnp.sum(total, axis=0, keepdims=True)
    total = total[:, :LANES] + total[:, LANES:]
    bsum[1:2] = total + pltpu.roll(total, 64, 1)


def fourth_near(grad, w, first, last, ext):
    depth, height = grad.shape[:2]
    for d in range(depth):
        fill(ext, grad[d], d, 64, 64)
    step = height // 2

    @pl.loop(0, 2)
    def _(block):
        h0 = block * step
        for d, dz, side in ((0, 2, first), (depth - 1, 0, last)):
            left = window(ext, d - dz, h0, step, [dz])
            value = nt(left, w[:, of_steps([dz], ext.shape[3])])
            side[0, pl.ds(h0, step)] = value.astype(BF16).reshape(step, -1, LANES)


def fourth_part(w, out, ext, block):
    depth, height, g, _ = out.shape
    step = height // 2
    h0 = block * step
    for d in range(depth):
        own, _ = split_steps(d, depth)
        left = window(ext, d - 1, h0, step, own)
        value = nt(left, w[:, of_steps(own, ext.shape[3])])
        out[d, pl.ds(h0, step)] = value.reshape(step, g, LANES)


class Reduce:
    def __init__(self, net, buf, out, got_a, acc, got_b, mid, got_c):
        self.net = net
        self.buf, self.out = buf, out
        self.got_a, self.acc, self.got_b, self.mid, self.got_c = got_a, acc, got_b, mid, got_c

    def pair(self):
        n = self.net
        self.copy = n.move(self.buf.at[1 - n.core], self.got_a, n.other)

    def samples(self):
        n = self.net
        self.copy.wait()
        self.acc[...] = (self.buf[n.core].astype(F32) + self.got_a[...].astype(F32)).astype(BF16)
        self.sem = n.ticket()
        for j, to in enumerate(n.peers):
            n.move(self.acc.at[to[0]], self.got_b.at[j], to, self.sem)

    def chips(self):
        n = self.net
        n.settle(self.got_b, self.sem)
        total = self.acc[n.s].astype(F32)
        for j in range(len(n.peers)):
            total = total + self.got_b[j].astype(F32)
        self.mid[...] = total.astype(BF16)
        self.sem = n.ticket()
        for j, (chip, to) in enumerate(n.line):
            n.move(self.mid.at[chip], self.got_c.at[j], to, self.sem)

    def back_chips(self):
        n = self.net
        n.settle(self.got_c, self.sem)
        total = self.mid[n.chip].astype(F32)
        for j in range(len(n.line)):
            total = total + self.got_c[j].astype(F32)
        here = self.out.at[n.core, n.s, n.chip]
        here[...] = total.astype(BF16)
        self.sem = n.ticket()
        for _, to in n.line:
            n.move(here, here, to, self.sem)
        self.wide = [n.ticket() for _ in n.peers]
        for k, to in enumerate(n.peers):
            n.move(here, here, to, self.wide[k])

    def back_samples(self):
        n = self.net
        chips = len(n.line) + 1
        n.settle(self.got_c, self.sem)
        for j in range(chips - 1):
            here = self.out.at[n.core, n.s, lax.rem(n.chip + chips - 1 - j, chips)]
            for k, to in enumerate(n.peers):
                n.move(here, here, to, self.wide[k])

    def back_pair(self):
        n = self.net
        samples = len(n.peers) + 1
        self.sem = n.ticket()
        here = self.out.at[n.core, n.s]
        n.move(here, here, n.other, self.sem)
        for k, sem in enumerate(self.wide):
            here = self.out.at[n.core, lax.rem(n.s + samples - 1 - k, samples)]
            n.settle(here, sem)
            n.move(here, here, n.other, self.sem)

    def end(self):
        self.net.settle(self.out.at[1 - self.net.core], self.sem)


class Gather:
    def __init__(self, net, buf, out, got_a, field):
        self.net = net
        self.buf, self.out, self.got_a, self.field = buf, out, got_a, field

    def scatter(self):
        n = self.net
        self.sem = n.ticket()
        for j, (core, s, to) in enumerate(n.plane):
            n.move(self.buf.at[core, s], self.got_a.at[j], to, self.sem)

    def along(self):
        n = self.net
        n.settle(self.got_a, self.sem)
        total = self.buf[n.core, n.s].astype(F32)
        for j in range(len(n.plane)):
            total = total + self.got_a[j].astype(F32)
        here = self.field.at[n.chip]
        here[...] = total.astype(BF16)
        self.sem = n.ticket()
        for _, to in n.line:
            n.move(here, here, to, self.sem)

    def back(self):
        n = self.net
        n.settle(self.field.at[1:], self.sem)
        here = self.out.at[n.core, n.s]
        here[...] = jnp.sum(self.field[...].astype(F32), axis=0).astype(BF16)
        self.sem = n.ticket()
        for _, _, to in n.plane:
            n.move(here, here, to, self.sem)

    def end(self):
        self.net.settle(self.got_a, self.sem)


class Net:
    def __init__(self, samples, space, send, recv):
        self.count = 0
        self.send, self.recv = send, recv
        self.space = space
        self.s = lax.axis_index("sample")
        self.p = lax.axis_index("space")
        self.core = lax.rem(self.p, 2)
        self.chip = lax.div(self.p, 2)
        self.other = (self.s, self.chip * 2 + 1 - self.core)
        self.peers = [(lax.rem(self.s + j, samples), self.p) for j in range(1, samples)]
        self.plane = []
        for j in range(samples - 1, -1, -1):
            for k in (1, 0):
                if j or k:
                    s, core = lax.rem(self.s + j, samples), lax.rem(self.core + k, 2)
                    self.plane.append((core, s, (s, self.chip * 2 + core)))
        self.line = []
        for j in range(1, space // 2):
            to = lax.rem(self.chip + j, space // 2)
            self.line.append((to, (self.s, to * 2 + self.core)))
        self.has_low = self.p > 0
        self.has_high = self.p < space - 1
        self.above = (self.s, lax.rem(self.p + 1, space))
        self.below = (self.s, lax.rem(self.p + space - 1, space))

    def greet(self):
        barrier = pltpu.get_barrier_semaphore()

        def signal(to):
            pl.semaphore_signal(barrier, inc=1, device_id=to, device_id_type=MESH)

        for to in [self.above, self.below]:
            signal(to)
        for _, _, to in self.plane:
            signal(to)
        for _, to in self.line:
            signal(to)

    def met(self):
        barrier = pltpu.get_barrier_semaphore()
        pl.semaphore_wait(barrier, 2 + len(self.plane) + len(self.line))

    def ticket(self):
        self.count += 1
        return self.count - 1

    def make(self, src, dst, to, sem=None):
        sem = self.ticket() if sem is None else sem
        return pltpu.make_async_remote_copy(
            src_ref=src,
            dst_ref=dst,
            send_sem=self.send.at[sem],
            recv_sem=self.recv.at[sem],
            device_id=to,
            device_id_type=MESH,
        )

    def move(self, src, dst, to, sem=None):
        copy = self.make(src, dst, to, sem)
        copy.start()
        return copy

    def settle(self, ref, sem):
        for of in (self.send, self.recv):
            pltpu.make_async_copy(ref, ref, of.at[sem]).wait()

    def halo(self, first, last, low, high):
        up = self.make(last, low, self.above)
        down = self.make(first, high, self.below)

        @pl.when(self.has_high)
        def _():
            up.start()

        @pl.when(self.has_low)
        def _():
            down.start()

        @pl.when(self.p == 0)
        def _():
            low[...] = jnp.zeros(low.shape, low.dtype)

        @pl.when(self.p == self.space - 1)
        def _():
            high[...] = jnp.zeros(high.shape, high.dtype)

        def finish():
            @pl.when(self.has_high)
            def _():
                up.wait_send()
                down.wait_recv()

            @pl.when(self.has_low)
            def _():
                down.wait_send()
                up.wait_recv()

        return finish


def copies_of(samples):
    return 4 * 2 + 1 + 2 * (5 + samples - 1) + 3 + 2


def share(net, rows, gots):
    def group(src, got, mine, targets):
        sem = net.ticket()
        for to in targets:
            net.move(src, got.at[mine], to, sem)
        got[mine] = src[...]
        return sem

    samples = gots[0].shape[0] // 2
    mine = net.core * samples + net.s
    sem = group(rows.at[0], gots[0], mine, [to for _, _, to in net.plane])
    yield
    net.settle(gots[0].at[1:], sem)
    rows[1] = jnp.sum(gots[0][...], axis=0)
    sem = group(rows.at[1], gots[1], net.chip, [to for _, to in net.line])
    yield
    net.settle(gots[1].at[1:], sem)
    rows[2] = jnp.sum(gots[1][...], axis=0)
    yield


def mono_kernel(samples, space, *refs):
    vol_hbm, tile_hbm, w3_hbm, w4_hbm, b3_hbm, b4_hbm = refs[:6]
    out, *outs4, out3, bsum = refs[6:11]
    refs = list(refs[11:])
    w3, w4, fwd3, fwd4, back3, back4 = refs[:6]
    pre, pooled, ext3, grad4, ext4, grad3, wide4, wide3 = refs[6:14]
    halos = refs[14:22]
    near = refs[-4:]
    other_tile, rows = refs[22:24]
    gots = refs[24:26]
    parts4 = refs[26:32], refs[32:38]
    part3 = refs[38:41]
    cells, low_cells, high_cells, plane, bias3, bias4 = refs[41:47]
    send, recv, vol, tile, b3, b4, part, part_fwd, here = refs[47:-4]
    loads = [
        pltpu.make_async_copy(w3_hbm, w3, here.at[0]),
        pltpu.make_async_copy(vol_hbm, vol, here.at[2]),
        pltpu.make_async_copy(b3_hbm, b3, here.at[4]),
        pltpu.make_async_copy(b4_hbm, b4, here.at[5]),
        pltpu.make_async_copy(w4_hbm, w4, here.at[1]),
        pltpu.make_async_copy(tile_hbm, tile, here.at[3]),
    ]
    for load in loads:
        load.start()
    net = Net(samples, space, send, recv)
    net.greet()
    depth = vol.shape[0]
    fours = [Reduce(net, p[0], o, *p[1:]) for p, o in zip(parts4, outs4)]
    three = Gather(net, part3[0], out3, *part3[1:])
    net.met()
    done = net.halo(vol_hbm.at[0], vol_hbm.at[depth - 1], halos[0], halos[1])
    tile_copy = net.move(tile_hbm, other_tile, net.other)
    loads[0].wait()
    place_forward(w3, fwd3, 96)
    loads[2].wait()
    loads[3].wait()
    for bias, narrow in ((bias3, b3), (bias4, b4)):
        width = narrow.shape[1]
        for c in range(bias.shape[1] // width):
            bias[:, c * width : (c + 1) * width] = narrow[...]
    loads[1].wait()
    for d in range(depth):
        spread(vol.at[d], cells.at[d])
    first_own(cells, fwd3, pre, ext3)
    done()
    spread(halos[0], low_cells.at[0])
    spread(halos[1], high_cells.at[0])
    first_kernel(low_cells, high_cells, fwd3, bias3, pre, pooled, ext3)
    done = net.halo(pooled, pooled, halos[2], halos[3])
    fill(ext4, pooled[...], 1, 64, 64)
    loads[4].wait()
    place_forward(w4, fwd4, 64)
    second_own(fwd4, bias4, part_fwd, ext4)
    place_back(w4, back4, 128, (1, 2, 0))
    loads[5].wait()
    tile_copy.wait()
    odd = net.core == 1
    mine, theirs = tile[...].astype(F32), other_tile[...].astype(F32)
    spread(jnp.where(odd, theirs, mine), plane.at[: tile.shape[0]])
    spread(jnp.where(odd, mine, theirs), plane.at[tile.shape[0] :])
    rows[...] = jnp.zeros(rows.shape, F32)
    for each in (*fours, three):
        each.buf[...] = jnp.zeros(each.buf.shape, BF16)
    slopes(pre)
    done()
    second_kernel(halos[2], halos[3], fwd4, part_fwd, plane, grad4, rows.at[0], ext4)
    third_near(grad4, back4, near[0], near[1], wide4)
    done = net.halo(near[0], near[1], halos[4], halos[5])
    for four, taps in zip(fours, HALVES):
        wgrad_four(ext4, grad4, four.buf, taps)
        four.pair()
    part[...] = nt(third_window(wide4), back4[2 * LANES :])
    fours[0].samples()
    fours[1].samples()
    place_back(w3, back3, 64)
    done()
    third_kernel(halos[4], halos[5], part, pre, grad3, rows.at[0])
    bias_steps = share(net, rows, gots)
    next(bias_steps)
    wgrad_three(ext3, grad3, three.buf, range(0, 7))
    fours[0].chips()
    wgrad_three(ext3, grad3, three.buf, range(7, 9))
    three.scatter()
    fours[1].chips()
    fourth_near(grad3, back3, near[2], near[3], wide3)
    next(bias_steps)
    fourth_part(back3, cells, wide3, 0)
    fourth_part(back3, cells, wide3, 1)
    fours[0].back_chips()
    three.along()
    fours[1].back_chips()
    done = net.halo(near[2], near[3], halos[6], halos[7])
    fours[0].back_samples()
    fours[1].back_samples()
    three.back()
    next(bias_steps)
    bsum[...] = rows[2]
    fours[0].back_pair()
    fours[1].back_pair()
    done()
    for d, side in ((0, halos[6]), (depth - 1, halos[7])):
        cells[d] = cells[d] + side[0].astype(F32)
    for d in range(depth):
        for g in range(cells.shape[2]):
            out[d, :, g * LANES : (g + 1) * LANES] = cells[d, :, g, :].astype(BF16)
    for each in (*fours, three):
        each.end()


def finish_kernel(grad, out4a, out4b, out3, bsum, volume, wsum3, wsum4, bsum3, bsum4):
    volume[...] = grad[...]
    for out4, taps in zip((out4a, out4b), HALVES):
        for place, tap in enumerate(taps):
            for dx in range(3):
                for k in range(4):
                    rows = kept(out4, (place * 3 + dx) * 4 + k)
                    wsum4[tap * 3 + dx, k * 16 : k * 16 + 16] = rows.astype(F32)
    for t in range(27):
        value = kept(out3, t).astype(F32)
        wsum3[t, :16] = value[:, :64]
        wsum3[t, 16:] = pltpu.roll(value, 64, 1)[:, :64]
    bsum4[...] = bsum[0:1]
    bsum3[...] = bsum[1:2, : bsum3.shape[1]]


def per_of(samples, chips, rows):
    per = 16
    while per * 2 * samples * chips < rows:
        per *= 2
    return per


def parts(samples, chips, rows):
    per = per_of(samples, chips, rows)
    return [
        pltpu.VMEM((2, samples, chips, per, LANES), BF16),
        pltpu.VMEM((samples, chips, per, LANES), BF16),
        pltpu.VMEM((samples, chips, per, LANES), BF16),
        pltpu.VMEM((max(samples - 1, 1), chips, per, LANES), BF16),
        pltpu.VMEM((chips, per, LANES), BF16),
        pltpu.VMEM((max(chips - 1, 1), per, LANES), BF16),
    ]


def pieces(samples, chips, rows):
    per = per_of(samples, 1, rows)
    return [
        pltpu.VMEM((2, samples, 1, per, LANES), BF16),
        pltpu.VMEM((2 * samples - 1, 1, per, LANES), BF16),
        pltpu.VMEM((chips, 1, per, LANES), BF16),
    ]


def local(volume, weight_three, bias_three, weight_four, bias_four, cotangent):
    cin, mid = weight_three.shape[3:]
    cout = weight_four.shape[4]
    depth, height = volume.shape[1:3]
    groups = volume.shape[3] // LANES
    samples, space = lax.axis_size("sample"), lax.axis_size("space")
    tile = cotangent[0]
    w3 = weight_three.reshape(27, cin, mid)
    w4 = weight_four.reshape(27, mid, cout)
    wide = 2 * LANES
    half = height // 2
    shape = jax.ShapeDtypeStruct
    vm = pltpu.VMEM
    copies = copies_of(samples)
    vmem = pl.BlockSpec(memory_space=pltpu.VMEM)
    far = pl.BlockSpec(memory_space=pltpu.HBM)
    counts = [3 * len(taps) * mid for taps in HALVES]
    packed = [
        shape((2, samples, chips, per_of(samples, chips, n), LANES), BF16)
        for chips, n in (*[(space // 2, n) for n in counts], (1, 27 * cin // 2))
    ]
    raw = shape(volume.shape[1:], BF16)
    results = pl.pallas_call(
        functools.partial(mono_kernel, samples, space),
        out_shape=[raw, *packed, shape((8, LANES), F32)],
        in_specs=[far] * 6,
        out_specs=[vmem] * 5,
        scratch_shapes=[
            vm(w3.shape, BF16),
            vm(w4.shape, BF16),
            vm((9 * wide, wide), BF16),
            vm((9 * wide, wide), BF16),
            vm((LANES, 9 * 3 * LANES), BF16),
            vm((3 * LANES, 3 * 4 * LANES), BF16),
            vm((depth, height, groups, wide), F32),
            vm((half, groups, LANES), BF16),
            vm((depth + 2, height + 2, groups, wide), BF16),
            vm((half, groups, wide), BF16),
            vm((3, half + 2, groups, wide), BF16),
            vm((depth, height, groups, wide), BF16),
            vm((1, half + 2, groups, 4 * LANES), BF16),
            vm((depth, height + 2, groups, 3 * LANES), BF16),
            *[vm(volume.shape[2:], BF16)] * 2,
            *[vm((half, groups, LANES), BF16)] * 2,
            *[vm((half, groups, LANES), BF16)] * 2,
            *[vm((1, height, groups, LANES), BF16)] * 2,
            vm(tile.shape, BF16),
            vm((3, 8, LANES), F32),
            vm((2 * samples, 8, LANES), F32),
            vm((space // 2, 8, LANES), F32),
            *parts(samples, space // 2, counts[0]),
            *parts(samples, space // 2, counts[1]),
            *pieces(samples, space // 2, 27 * cin // 2),
            vm((depth, height, groups, LANES), F32),
            *[vm((1, height, groups, LANES), F32)] * 2,
            vm((2 * tile.shape[0], groups, LANES), F32),
            vm((1, wide), F32),
            vm((1, wide), F32),
            pltpu.SemaphoreType.DMA((copies,)),
            pltpu.SemaphoreType.DMA((copies,)),
            vm(volume.shape[1:], BF16),
            vm(tile.shape, BF16),
            vm((1, mid), F32),
            vm((1, cout), F32),
            vm((half * groups, LANES), F32),
            vm((half * groups, wide), F32),
            pltpu.SemaphoreType.DMA((6,)),
            *[vm((half, groups, LANES), BF16)] * 2,
            *[vm((1, height, groups, LANES), BF16)] * 2,
        ],
        compiler_params=pltpu.CompilerParams(
            collective_id=0, has_side_effects=True, vmem_limit_bytes=36 * 2**20
        ),
    )(
        *[
            pltpu.with_memory_space_constraint(a, pltpu.HBM)
            for a in (volume[0], tile, w3, w4, bias_three[None], bias_four[None])
        ]
    )
    grad_field, wsum_three, wsum_four, bsum_three, bsum_four = pl.pallas_call(
        finish_kernel,
        out_shape=[
            raw,
            shape((27, cin, mid), F32),
            shape((27, mid, cout), F32),
            shape((1, mid), F32),
            shape((1, cout), F32),
        ],
        in_specs=[vmem] * 5,
        out_specs=[vmem] * 5,
        compiler_params=pltpu.CompilerParams(vmem_limit_bytes=16 * 2**20),
    )(*results)
    return (
        grad_field.reshape(volume.shape),
        wsum_three.reshape(weight_three.shape),
        bsum_three[0],
        wsum_four.reshape(weight_four.shape),
        bsum_four[0],
    )


def solution(mesh):
    placed = (P("sample", "space", None, None), P(), P(), P(), P(), P("sample", "space", None))
    return jax.shard_map(
        local,
        mesh=mesh,
        in_specs=placed,
        out_specs=(P("sample", "space", None, None), P(), P(), P(), P()),
        check_vma=False,
    )
```

```python
import functools

import jax
import jax.numpy as jnp
from jax import lax
from jax.experimental import pallas as pl
from jax.experimental.pallas import tpu as pltpu
from jax.sharding import PartitionSpec as P

F32 = jnp.float32
BF16 = jnp.bfloat16
MESH = pl.DeviceIdType.MESH
LANES = 128
HALVES = (range(0, 5), range(5, 9))


def slot_of(cell, cells, chans, main, low_side):
    if cell < 0:
        return main + low_side
    if cell == cells:
        return main
    return cell * chans


def place_forward(wide, fwd, low_in):
    cin, cout = wide.shape[1], wide.shape[2]
    fwd[...] = jnp.zeros(fwd.shape, fwd.dtype)
    for tap in range(9):
        for dx in range(3):
            for c in range(LANES // cin):
                row = tap * 2 * LANES + slot_of(c + dx - 1, LANES // cin, cin, LANES, low_in)
                fwd[row : row + cin, c * cout : (c + 1) * cout] = wide[tap * 3 + dx]


def place_back(wide, back, low_out, blocks=(0, 0, 0)):
    cin, cout = wide.shape[1], wide.shape[2]
    per = 3 if max(blocks) else 9
    unit = back.shape[1] // per
    back[...] = jnp.zeros(back.shape, back.dtype)
    for tap in range(9):
        for dx in range(3):
            for c in range(LANES // cin):
                row = blocks[tap // 3] * LANES + c * cin
                col = tap % per * unit
                col += slot_of(c - dx + 1, LANES // cin, cout, 2 * LANES, low_out)
                back[row : row + cin, col : col + cout] = wide[(8 - tap) * 3 + dx]


def spread(raw, dst):
    for g in range(dst.shape[1]):
        dst[:, g, :] = raw[:, g * LANES : (g + 1) * LANES].astype(F32)


def neighbours(low, high, groups):
    rows = low.shape[0]
    place = lax.broadcasted_iota(jnp.int32, low.shape, 0) % groups
    right = jnp.where(place == groups - 1, 0.0, pltpu.roll(low, rows - 1, 0))
    left = jnp.where(place == 0, 0.0, pltpu.roll(high, 1, 0))
    return right, left


def widen(plane, first, last):
    h, g, lanes = plane.shape
    flat = plane.astype(F32).reshape(h * g, lanes)
    right, left = neighbours(flat[:, :LANES], flat[:, lanes - LANES :], g)
    if first == LANES:
        side = jnp.concatenate([right, left], axis=1)
    else:
        lane = lax.broadcasted_iota(jnp.int32, right.shape, 1)
        side = jnp.where(lane < first, right, jnp.where(lane >= last, left, 0.0))
    return jnp.concatenate([plane.astype(BF16), side.astype(BF16).reshape(h, g, -1)], axis=2)


def fill(ext, plane, e, first, last):
    height = ext.shape[1] - 2
    edge = jnp.zeros(ext.shape[2:], ext.dtype)
    ext[e, 0] = edge
    ext[e, height + 1] = edge
    ext[e, 1 : height + 1] = widen(plane, first, last)


def window(ext, d, h0, rows, steps=(0, 1, 2)):
    parts = [
        ext[d + dz, pl.ds(h0 + dy, rows)].reshape(-1, ext.shape[3])
        for dz in steps
        for dy in range(3)
    ]
    return jnp.concatenate(parts, axis=1)


def of_steps(steps, unit):
    return pl.ds(steps[0] * 3 * unit, len(steps) * 3 * unit)


def split_steps(d, depth):
    own = [dz for dz in range(3) if 1 <= d + dz <= depth]
    return own, [dz for dz in range(3) if dz not in own]


def nt(a, b):
    return lax.dot_general(a, b, (((1,), (1,)), ((), ())), preferred_element_type=F32)


def slope(v):
    s = jax.nn.sigmoid(v)
    return s * (1.0 + v * (1.0 - s))


def first_own(vol, w, pre, ext):
    depth, height, g, _ = vol.shape
    for d in range(depth):
        fill(ext, vol[d], d + 1, 32, 96)
    step = 8

    @pl.loop(0, height // step)
    def _(block):
        h0 = block * step
        for d in range(depth):
            own, _ = split_steps(d, depth)
            left = window(ext, d, h0, step, own)
            value = jnp.dot(left, w[of_steps(own, ext.shape[3])], preferred_element_type=F32)
            pre[d, pl.ds(h0, step)] = value.reshape(step, g, -1)


def first_kernel(low, high, w, bias, pre, pooled, ext):
    depth, height, g, _ = pre.shape
    fill(ext, low[0], 0, 32, 96)
    fill(ext, high[0], depth + 1, 32, 96)
    step = 8

    @pl.loop(0, height // step)
    def _(block):
        h0 = block * step
        total = 0.0
        for d in range(depth):
            value = pre[d, pl.ds(h0, step)].reshape(step * g, -1) + bias[...]
            _, rest = split_steps(d, depth)
            for dz in rest:
                left = window(ext, d, h0, step, [dz])
                value = value + jnp.dot(
                    left, w[of_steps([dz], ext.shape[3])], preferred_element_type=F32
                )
            pre[d, pl.ds(h0, step)] = value.reshape(step, g, -1)
            total = total + value * jax.nn.sigmoid(value)
        total = jnp.sum(total.reshape(step // 2, 2, g, -1), axis=1).reshape(step // 2 * g, -1)
        a, b = total[:, :LANES], total[:, LANES:]
        lane = lax.broadcasted_iota(jnp.int32, a.shape, 1)
        half = LANES // 2
        mean = jnp.where(lane < half, a + pltpu.roll(a, half, 1), b + pltpu.roll(b, half, 1))
        pooled[pl.ds(block * (step // 2), step // 2)] = (
            (mean * 0.125).astype(BF16).reshape(step // 2, g, LANES)
        )


def slopes(pre):
    @pl.loop(0, pre.shape[1] // 2)
    def _(block):
        for d in range(pre.shape[0]):
            here = pl.ds(block * 2, 2)
            pre[d, here] = slope(pre[d, here])


def second_own(w, bias, part, ext):
    height = ext.shape[1] - 2
    own = w[of_steps([1], ext.shape[3])]
    part[...] = jnp.dot(window(ext, 0, 0, height, [1]), own, preferred_element_type=F32) + bias[...]


def second_kernel(low, high, w, part, cot, grad, bsum, ext):
    height, g, _ = low.shape
    fill(ext, low[...], 0, 64, 64)
    fill(ext, high[...], 2, 64, 64)
    pre = part[...]
    for dz in (0, 2):
        rest = w[of_steps([dz], ext.shape[3])]
        pre = pre + jnp.dot(window(ext, 0, 0, height, [dz]), rest, preferred_element_type=F32)
    up = cot[...]
    up = jnp.broadcast_to(up[:, None], (height // 2, 2, g, LANES)).reshape(height * g, LANES)
    up = jnp.concatenate([up, up], axis=1) * 0.125
    value = (up * slope(pre)).astype(BF16)
    grad[...] = value.reshape(grad.shape)
    total = jnp.sum(value.astype(F32), axis=0, keepdims=True)
    bsum[0:1] = total[:, :LANES] + total[:, LANES:]


def tn(a, b):
    return lax.dot_general(a, b, (((0,), (0,)), ((), ())), preferred_element_type=F32)


def keep(buf, piece, rows):
    _, samples, chips, per, _ = buf.shape
    for k in range(rows.shape[0] // 16):
        first = (piece + k) * 16
        chunk, row = first // per, first % per
        core, rest = divmod(chunk, samples * chips)
        buf[core, rest // chips, rest % chips, row : row + 16] = rows[k * 16 : k * 16 + 16]


def kept(buf, piece):
    _, samples, chips, per, _ = buf.shape
    chunk, row = piece * 16 // per, piece * 16 % per
    core, rest = divmod(chunk, samples * chips)
    return buf[core, rest // chips, rest % chips, row : row + 16]


def wgrad_four(ext, grad, buf, taps):
    height = grad.shape[0]
    up = grad[...].reshape(-1, 2 * LANES)
    for place, tap in enumerate(taps):
        part = tn(ext[tap // 3, tap % 3 : tap % 3 + height].reshape(-1, 2 * LANES), up)
        for dx in range(3):
            total = 0.0
            for c in range(2):
                row = slot_of(c + dx - 1, 2, 64, LANES, 64)
                total = total + part[row : row + 64, c * LANES : (c + 1) * LANES]
            keep(buf, (place * 3 + dx) * 4, total.astype(BF16))


def wgrad_three(ext, grad, buf, taps):
    depth, height = grad.shape[:2]
    for tap in taps:
        part = 0.0
        for d in range(depth):
            part = part + tn(
                ext[tap // 3 + d, tap % 3 : tap % 3 + height].reshape(-1, 2 * LANES),
                grad[d].reshape(-1, 2 * LANES),
            )
        for dx in range(3):
            even, odd = 0.0, 0.0
            for c in range(4):
                row = slot_of(c + dx - 1, 4, 32, LANES, 96)
                piece = part[row : row + 32, c // 2 * LANES : (c // 2 + 1) * LANES]
                if c % 2:
                    odd = odd + piece
                else:
                    even = even + piece
            total = even + pltpu.roll(odd, 64, 1)
            lane = lax.broadcasted_iota(jnp.int32, (16, LANES), 1)
            packed = jnp.where(lane < 64, total[:16], pltpu.roll(total[16:], 64, 1))
            keep(buf, tap * 3 + dx, packed.astype(BF16))


def third_near(grad, w, first, last, ext):
    fill(ext, grad[...], 0, LANES, LANES)
    value = nt(third_window(ext), w[: 2 * LANES]).astype(BF16)
    first[...] = value[:, :LANES].reshape(first.shape)
    last[...] = value[:, LANES:].reshape(last.shape)


def third_window(ext):
    return window(ext, 0, 0, ext.shape[1] - 2, [0])


def third_kernel(low, high, part, pre, out, bsum):
    height, g, _ = low.shape
    back = part[...]
    for side in (low, high):
        back = back + side[...].astype(F32).reshape(back.shape)
    back = back * 0.125
    turned = pltpu.roll(back, 64, 1)
    lane = lax.broadcasted_iota(jnp.int32, back.shape, 1)
    up = jnp.concatenate(
        [jnp.where(lane < 64, back, turned), jnp.where(lane < 64, turned, back)], axis=1
    ).reshape(height, g, 2 * LANES)
    total = 0.0
    for d in range(pre.shape[0]):
        for h in range(height):
            value = (up[h][None] * pre[d, 2 * h : 2 * h + 2]).astype(BF16)
            out[d, 2 * h : 2 * h + 2] = value
            total = total + jnp.sum(value.astype(F32), axis=0)
    total = jnp.sum(total, axis=0, keepdims=True)
    total = total[:, :LANES] + total[:, LANES:]
    bsum[1:2] = total + pltpu.roll(total, 64, 1)


def fourth_near(grad, w, first, last, ext):
    depth, height = grad.shape[:2]
    for d in range(depth):
        fill(ext, grad[d], d, 64, 64)
    step = height // 2

    @pl.loop(0, 2)
    def _(block):
        h0 = block * step
        for d, dz, side in ((0, 2, first), (depth - 1, 0, last)):
            left = window(ext, d - dz, h0, step, [dz])
            value = nt(left, w[:, of_steps([dz], ext.shape[3])])
            side[0, pl.ds(h0, step)] = value.astype(BF16).reshape(step, -1, LANES)


def fourth_part(w, out, ext, block):
    depth, height, g, _ = out.shape
    step = height // 2
    h0 = block * step
    for d in range(depth):
        own, _ = split_steps(d, depth)
        left = window(ext, d - 1, h0, step, own)
        value = nt(left, w[:, of_steps(own, ext.shape[3])])
        out[d, pl.ds(h0, step)] = value.reshape(step, g, LANES)


class Reduce:
    def __init__(self, net, buf, out, got_a, acc, got_b, mid, got_c):
        self.net = net
        self.buf, self.out = buf, out
        self.got_a, self.acc, self.got_b, self.mid, self.got_c = got_a, acc, got_b, mid, got_c

    def pair(self):
        n = self.net
        self.copy = n.move(self.buf.at[1 - n.core], self.got_a, n.other)

    def samples(self):
        n = self.net
        self.copy.wait()
        self.acc[...] = (self.buf[n.core].astype(F32) + self.got_a[...].astype(F32)).astype(BF16)
        self.sem = n.ticket()
        for j, to in enumerate(n.peers):
            n.move(self.acc.at[to[0]], self.got_b.at[j], to, self.sem)

    def chips(self):
        n = self.net
        n.settle(self.got_b, self.sem)
        total = self.acc[n.s].astype(F32)
        for j in range(len(n.peers)):
            total = total + self.got_b[j].astype(F32)
        self.mid[...] = total.astype(BF16)
        self.sem = n.ticket()
        for j, (chip, to) in enumerate(n.line):
            n.move(self.mid.at[chip], self.got_c.at[j], to, self.sem)

    def back_chips(self):
        n = self.net
        n.settle(self.got_c, self.sem)
        total = self.mid[n.chip].astype(F32)
        for j in range(len(n.line)):
            total = total + self.got_c[j].astype(F32)
        here = self.out.at[n.core, n.s, n.chip]
        here[...] = total.astype(BF16)
        self.sem = n.ticket()
        for _, to in n.line:
            n.move(here, here, to, self.sem)
        self.wide = [n.ticket() for _ in n.peers]
        for k, to in enumerate(n.peers):
            n.move(here, here, to, self.wide[k])

    def back_samples(self):
        n = self.net
        chips = len(n.line) + 1
        n.settle(self.got_c, self.sem)
        for j in range(chips - 1):
            here = self.out.at[n.core, n.s, lax.rem(n.chip + chips - 1 - j, chips)]
            for k, to in enumerate(n.peers):
                n.move(here, here, to, self.wide[k])

    def back_pair(self):
        n = self.net
        samples = len(n.peers) + 1
        self.sem = n.ticket()
        here = self.out.at[n.core, n.s]
        n.move(here, here, n.other, self.sem)
        for k, sem in enumerate(self.wide):
            here = self.out.at[n.core, lax.rem(n.s + samples - 1 - k, samples)]
            n.settle(here, sem)
            n.move(here, here, n.other, self.sem)

    def end(self):
        self.net.settle(self.out.at[1 - self.net.core], self.sem)


class Gather:
    def __init__(self, net, buf, out, got_a, field):
        self.net = net
        self.buf, self.out, self.got_a, self.field = buf, out, got_a, field

    def scatter(self):
        n = self.net
        self.sem = n.ticket()
        for j, (core, s, to) in enumerate(n.plane):
            n.move(self.buf.at[core, s], self.got_a.at[j], to, self.sem)

    def along(self):
        n = self.net
        n.settle(self.got_a, self.sem)
        total = self.buf[n.core, n.s].astype(F32)
        for j in range(len(n.plane)):
            total = total + self.got_a[j].astype(F32)
        here = self.field.at[n.chip]
        here[...] = total.astype(BF16)
        self.sem = n.ticket()
        for _, to in n.line:
            n.move(here, here, to, self.sem)

    def back(self):
        n = self.net
        n.settle(self.field.at[1:], self.sem)
        here = self.out.at[n.core, n.s]
        here[...] = jnp.sum(self.field[...].astype(F32), axis=0).astype(BF16)
        self.sem = n.ticket()
        for _, _, to in n.plane:
            n.move(here, here, to, self.sem)

    def end(self):
        self.net.settle(self.got_a, self.sem)


class Net:
    def __init__(self, samples, space, send, recv):
        self.count = 0
        self.send, self.recv = send, recv
        self.space = space
        self.s = lax.axis_index("sample")
        self.p = lax.axis_index("space")
        self.core = lax.rem(self.p, 2)
        self.chip = lax.div(self.p, 2)
        self.other = (self.s, self.chip * 2 + 1 - self.core)
        self.peers = [(lax.rem(self.s + j, samples), self.p) for j in range(1, samples)]
        self.plane = []
        for j in range(samples - 1, -1, -1):
            for k in (1, 0):
                if j or k:
                    s, core = lax.rem(self.s + j, samples), lax.rem(self.core + k, 2)
                    self.plane.append((core, s, (s, self.chip * 2 + core)))
        self.line = []
        for j in range(1, space // 2):
            to = lax.rem(self.chip + j, space // 2)
            self.line.append((to, (self.s, to * 2 + self.core)))
        self.has_low = self.p > 0
        self.has_high = self.p < space - 1
        self.above = (self.s, lax.rem(self.p + 1, space))
        self.below = (self.s, lax.rem(self.p + space - 1, space))

    def greet(self):
        barrier = pltpu.get_barrier_semaphore()

        def signal(to):
            pl.semaphore_signal(barrier, inc=1, device_id=to, device_id_type=MESH)

        for to in [self.above, self.below]:
            signal(to)
        for _, _, to in self.plane:
            signal(to)
        for _, to in self.line:
            signal(to)

    def met(self):
        barrier = pltpu.get_barrier_semaphore()
        pl.semaphore_wait(barrier, 2 + len(self.plane) + len(self.line))

    def ticket(self):
        self.count += 1
        return self.count - 1

    def make(self, src, dst, to, sem=None):
        sem = self.ticket() if sem is None else sem
        return pltpu.make_async_remote_copy(
            src_ref=src,
            dst_ref=dst,
            send_sem=self.send.at[sem],
            recv_sem=self.recv.at[sem],
            device_id=to,
            device_id_type=MESH,
        )

    def move(self, src, dst, to, sem=None):
        copy = self.make(src, dst, to, sem)
        copy.start()
        return copy

    def settle(self, ref, sem):
        for of in (self.send, self.recv):
            pltpu.make_async_copy(ref, ref, of.at[sem]).wait()

    def halo(self, first, last, low, high):
        up = self.make(last, low, self.above)
        down = self.make(first, high, self.below)

        @pl.when(self.has_high)
        def _():
            up.start()

        @pl.when(self.has_low)
        def _():
            down.start()

        @pl.when(self.p == 0)
        def _():
            low[...] = jnp.zeros(low.shape, low.dtype)

        @pl.when(self.p == self.space - 1)
        def _():
            high[...] = jnp.zeros(high.shape, high.dtype)

        def finish():
            @pl.when(self.has_high)
            def _():
                up.wait_send()
                down.wait_recv()

            @pl.when(self.has_low)
            def _():
                down.wait_send()
                up.wait_recv()

        return finish


def copies_of(samples):
    return 4 * 2 + 1 + 2 * (5 + samples - 1) + 3 + 2


def share(net, rows, gots):
    def group(src, got, mine, targets):
        sem = net.ticket()
        for to in targets:
            net.move(src, got.at[mine], to, sem)
        got[mine] = src[...]
        return sem

    samples = gots[0].shape[0] // 2
    mine = net.core * samples + net.s
    sem = group(rows.at[0], gots[0], mine, [to for _, _, to in net.plane])
    yield
    net.settle(gots[0].at[1:], sem)
    rows[1] = jnp.sum(gots[0][...], axis=0)
    sem = group(rows.at[1], gots[1], net.chip, [to for _, to in net.line])
    yield
    net.settle(gots[1].at[1:], sem)
    rows[2] = jnp.sum(gots[1][...], axis=0)
    yield


def mono_kernel(samples, space, *refs):
    vol_hbm, tile_hbm, w3_hbm, w4_hbm, b3_hbm, b4_hbm = refs[:6]
    out, *outs4, out3, bsum = refs[6:11]
    refs = list(refs[11:])
    w3, w4, fwd3, fwd4, back3, back4 = refs[:6]
    pre, pooled, ext3, grad4, ext4, grad3, wide4, wide3 = refs[6:14]
    halos = refs[14:22]
    near = refs[-4:]
    other_tile, rows = refs[22:24]
    gots = refs[24:26]
    parts4 = refs[26:32], refs[32:38]
    part3 = refs[38:41]
    cells, low_cells, high_cells, plane, bias3, bias4 = refs[41:47]
    send, recv, vol, tile, b3, b4, part, part_fwd, here = refs[47:-4]
    loads = [
        pltpu.make_async_copy(w3_hbm, w3, here.at[0]),
        pltpu.make_async_copy(vol_hbm, vol, here.at[2]),
        pltpu.make_async_copy(b3_hbm, b3, here.at[4]),
        pltpu.make_async_copy(b4_hbm, b4, here.at[5]),
        pltpu.make_async_copy(w4_hbm, w4, here.at[1]),
        pltpu.make_async_copy(tile_hbm, tile, here.at[3]),
    ]
    for load in loads:
        load.start()
    net = Net(samples, space, send, recv)
    net.greet()
    depth = vol.shape[0]
    fours = [Reduce(net, p[0], o, *p[1:]) for p, o in zip(parts4, outs4)]
    three = Gather(net, part3[0], out3, *part3[1:])
    net.met()
    done = net.halo(vol_hbm.at[0], vol_hbm.at[depth - 1], halos[0], halos[1])
    tile_copy = net.move(tile_hbm, other_tile, net.other)
    loads[0].wait()
    place_forward(w3, fwd3, 96)
    loads[2].wait()
    loads[3].wait()
    for bias, narrow in ((bias3, b3), (bias4, b4)):
        width = narrow.shape[1]
        for c in range(bias.shape[1] // width):
            bias[:, c * width : (c + 1) * width] = narrow[...]
    loads[1].wait()
    for d in range(depth):
        spread(vol.at[d], cells.at[d])
    first_own(cells, fwd3, pre, ext3)
    done()
    spread(halos[0], low_cells.at[0])
    spread(halos[1], high_cells.at[0])
    first_kernel(low_cells, high_cells, fwd3, bias3, pre, pooled, ext3)
    done = net.halo(pooled, pooled, halos[2], halos[3])
    fill(ext4, pooled[...], 1, 64, 64)
    loads[4].wait()
    place_forward(w4, fwd4, 64)
    second_own(fwd4, bias4, part_fwd, ext4)
    place_back(w4, back4, 128, (1, 2, 0))
    loads[5].wait()
    tile_copy.wait()
    odd = net.core == 1
    mine, theirs = tile[...].astype(F32), other_tile[...].astype(F32)
    spread(jnp.where(odd, theirs, mine), plane.at[: tile.shape[0]])
    spread(jnp.where(odd, mine, theirs), plane.at[tile.shape[0] :])
    rows[...] = jnp.zeros(rows.shape, F32)
    for each in (*fours, three):
        each.buf[...] = jnp.zeros(each.buf.shape, BF16)
    slopes(pre)
    place_back(w3, back3, 64)
    done()
    second_kernel(halos[2], halos[3], fwd4, part_fwd, plane, grad4, rows.at[0], ext4)
    third_near(grad4, back4, near[0], near[1], wide4)
    done = net.halo(near[0], near[1], halos[4], halos[5])
    for four, taps in zip(fours, HALVES):
        wgrad_four(ext4, grad4, four.buf, taps)
        four.pair()
    fours[0].samples()
    fours[1].samples()
    part[...] = nt(third_window(wide4), back4[2 * LANES :])
    done()
    third_kernel(halos[4], halos[5], part, pre, grad3, rows.at[0])
    bias_steps = share(net, rows, gots)
    next(bias_steps)
    wgrad_three(ext3, grad3, three.buf, range(0, 7))
    fours[0].chips()
    wgrad_three(ext3, grad3, three.buf, range(7, 9))
    three.scatter()
    fours[1].chips()
    fourth_near(grad3, back3, near[2], near[3], wide3)
    next(bias_steps)
    fourth_part(back3, cells, wide3, 0)
    fourth_part(back3, cells, wide3, 1)
    fours[0].back_chips()
    three.along()
    fours[1].back_chips()
    done = net.halo(near[2], near[3], halos[6], halos[7])
    fours[0].back_samples()
    fours[1].back_samples()
    three.back()
    next(bias_steps)
    bsum[...] = rows[2]
    fours[0].back_pair()
    fours[1].back_pair()
    done()
    for d, side in ((0, halos[6]), (depth - 1, halos[7])):
        cells[d] = cells[d] + side[0].astype(F32)
    for d in range(depth):
        for g in range(cells.shape[2]):
            out[d, :, g * LANES : (g + 1) * LANES] = cells[d, :, g, :].astype(BF16)
    for each in (*fours, three):
        each.end()


def finish_kernel(grad, out4a, out4b, out3, bsum, volume, wsum3, wsum4, bsum3, bsum4):
    volume[...] = grad[...]
    for out4, taps in zip((out4a, out4b), HALVES):
        for place, tap in enumerate(taps):
            for dx in range(3):
                for k in range(4):
                    rows = kept(out4, (place * 3 + dx) * 4 + k)
                    wsum4[tap * 3 + dx, k * 16 : k * 16 + 16] = rows.astype(F32)
    for t in range(27):
        value = kept(out3, t).astype(F32)
        wsum3[t, :16] = value[:, :64]
        wsum3[t, 16:] = pltpu.roll(value, 64, 1)[:, :64]
    bsum4[...] = bsum[0:1]
    bsum3[...] = bsum[1:2, : bsum3.shape[1]]


def per_of(samples, chips, rows):
    per = 16
    while per * 2 * samples * chips < rows:
        per *= 2
    return per


def parts(samples, chips, rows):
    per = per_of(samples, chips, rows)
    return [
        pltpu.VMEM((2, samples, chips, per, LANES), BF16),
        pltpu.VMEM((samples, chips, per, LANES), BF16),
        pltpu.VMEM((samples, chips, per, LANES), BF16),
        pltpu.VMEM((max(samples - 1, 1), chips, per, LANES), BF16),
        pltpu.VMEM((chips, per, LANES), BF16),
        pltpu.VMEM((max(chips - 1, 1), per, LANES), BF16),
    ]


def pieces(samples, chips, rows):
    per = per_of(samples, 1, rows)
    return [
        pltpu.VMEM((2, samples, 1, per, LANES), BF16),
        pltpu.VMEM((2 * samples - 1, 1, per, LANES), BF16),
        pltpu.VMEM((chips, 1, per, LANES), BF16),
    ]


def local(volume, weight_three, bias_three, weight_four, bias_four, cotangent):
    cin, mid = weight_three.shape[3:]
    cout = weight_four.shape[4]
    depth, height = volume.shape[1:3]
    groups = volume.shape[3] // LANES
    samples, space = lax.axis_size("sample"), lax.axis_size("space")
    tile = cotangent[0]
    w3 = weight_three.reshape(27, cin, mid)
    w4 = weight_four.reshape(27, mid, cout)
    wide = 2 * LANES
    half = height // 2
    shape = jax.ShapeDtypeStruct
    vm = pltpu.VMEM
    copies = copies_of(samples)
    vmem = pl.BlockSpec(memory_space=pltpu.VMEM)
    far = pl.BlockSpec(memory_space=pltpu.HBM)
    counts = [3 * len(taps) * mid for taps in HALVES]
    packed = [
        shape((2, samples, chips, per_of(samples, chips, n), LANES), BF16)
        for chips, n in (*[(space // 2, n) for n in counts], (1, 27 * cin // 2))
    ]
    raw = shape(volume.shape[1:], BF16)
    results = pl.pallas_call(
        functools.partial(mono_kernel, samples, space),
        out_shape=[raw, *packed, shape((8, LANES), F32)],
        in_specs=[far] * 6,
        out_specs=[vmem] * 5,
        scratch_shapes=[
            vm(w3.shape, BF16),
            vm(w4.shape, BF16),
            vm((9 * wide, wide), BF16),
            vm((9 * wide, wide), BF16),
            vm((LANES, 9 * 3 * LANES), BF16),
            vm((3 * LANES, 3 * 4 * LANES), BF16),
            vm((depth, height, groups, wide), F32),
            vm((half, groups, LANES), BF16),
            vm((depth + 2, height + 2, groups, wide), BF16),
            vm((half, groups, wide), BF16),
            vm((3, half + 2, groups, wide), BF16),
            vm((depth, height, groups, wide), BF16),
            vm((1, half + 2, groups, 4 * LANES), BF16),
            vm((depth, height + 2, groups, 3 * LANES), BF16),
            *[vm(volume.shape[2:], BF16)] * 2,
            *[vm((half, groups, LANES), BF16)] * 2,
            *[vm((half, groups, LANES), BF16)] * 2,
            *[vm((1, height, groups, LANES), BF16)] * 2,
            vm(tile.shape, BF16),
            vm((3, 8, LANES), F32),
            vm((2 * samples, 8, LANES), F32),
            vm((space // 2, 8, LANES), F32),
            *parts(samples, space // 2, counts[0]),
            *parts(samples, space // 2, counts[1]),
            *pieces(samples, space // 2, 27 * cin // 2),
            vm((depth, height, groups, LANES), F32),
            *[vm((1, height, groups, LANES), F32)] * 2,
            vm((2 * tile.shape[0], groups, LANES), F32),
            vm((1, wide), F32),
            vm((1, wide), F32),
            pltpu.SemaphoreType.DMA((copies,)),
            pltpu.SemaphoreType.DMA((copies,)),
            vm(volume.shape[1:], BF16),
            vm(tile.shape, BF16),
            vm((1, mid), F32),
            vm((1, cout), F32),
            vm((half * groups, LANES), F32),
            vm((half * groups, wide), F32),
            pltpu.SemaphoreType.DMA((6,)),
            *[vm((half, groups, LANES), BF16)] * 2,
            *[vm((1, height, groups, LANES), BF16)] * 2,
        ],
        compiler_params=pltpu.CompilerParams(
            collective_id=0, has_side_effects=True, vmem_limit_bytes=36 * 2**20
        ),
    )(
        *[
            pltpu.with_memory_space_constraint(a, pltpu.HBM)
            for a in (volume[0], tile, w3, w4, bias_three[None], bias_four[None])
        ]
    )
    grad_field, wsum_three, wsum_four, bsum_three, bsum_four = pl.pallas_call(
        finish_kernel,
        out_shape=[
            raw,
            shape((27, cin, mid), F32),
            shape((27, mid, cout), F32),
            shape((1, mid), F32),
            shape((1, cout), F32),
        ],
        in_specs=[vmem] * 5,
        out_specs=[vmem] * 5,
        compiler_params=pltpu.CompilerParams(vmem_limit_bytes=16 * 2**20),
    )(*results)
    return (
        grad_field.reshape(volume.shape),
        wsum_three.reshape(weight_three.shape),
        bsum_three[0],
        wsum_four.reshape(weight_four.shape),
        bsum_four[0],
    )


def solution(mesh):
    placed = (P("sample", "space", None, None), P(), P(), P(), P(), P("sample", "space", None))
    return jax.shard_map(
        local,
        mesh=mesh,
        in_specs=placed,
        out_specs=(P("sample", "space", None, None), P(), P(), P(), P()),
        check_vma=False,
    )
```
